32 devices in a mesh: fsdp: 8 (over z, x), tp: 4 (over y, core).
Axes of the slice: x: 2, y: 2, z: 4, core: 2. Of those that a mesh axis runs over, the one named last changes fastest.
Arguments:
- tokens: bfloat16 [4096, 2048], P(('fsdp', 'tp')), may hold values from -6 to 6
- seg_ids: int32 [8, 512], P('fsdp'), may hold values from 0 to 5, never falling along the last dimension, each value on 1 to 384 neighbouring positions
- pad_mask: int32 [8, 512], P('fsdp'), may hold values from 0 to 1, as said below
- expert_ids: int32 [4096, 8], P('fsdp'), may hold values from 0 to 15, all different within a row; in each aligned block of 512 rows (0 to 511, 512 to 1023, ...) at most 264 rows name the same one
- w_qkv: bfloat16 [3, 2048, 2048], P(None, 'fsdp', 'tp'), may hold values from -0.125 to 0.125
- w_out: bfloat16 [2048, 2048], P('tp', 'fsdp'), may hold values from -1 to 1
- w_router: bfloat16 [2048, 16], P(('fsdp', 'tp')), may hold values from -0.0625 to 0.0625
- norm_gains: bfloat16 [4, 2048], P(None, ('fsdp', 'tp')), may hold values from 0.25 to 1.75
- w_gate: bfloat16 [16, 2048, 1024], P('fsdp', None, 'tp'), may hold values from -0.125 to 0.125
- w_up: bfloat16 [16, 2048, 1024], P('fsdp', None, 'tp'), may hold values from -0.125 to 0.125
- w_down: bfloat16 [16, 1024, 2048], P('fsdp', 'tp'), may hold values from -4 to 4
- cotangent: bfloat16 [4096, 2048], P(('fsdp', 'tp')), may hold values from -6 to 6
Outputs:
- layer_out: bfloat16 [4096, 2048], P(('fsdp', 'tp'))
- input_grad: float32 [4096, 2048], P(('fsdp', 'tp'))
- grad_qkv: float32 [3, 2048, 2048], P(None, 'fsdp', 'tp')
- grad_out: float32 [2048, 2048], P('tp', 'fsdp')
- grad_router: float32 [2048, 16], P(('fsdp', 'tp'))
- grad_gains: float32 [4, 2048], P(None, ('fsdp', 'tp'))
- grad_gate: float32 [16, 2048, 1024], P('fsdp', None, 'tp')
- grad_up: float32 [16, 2048, 1024], P('fsdp', None, 'tp')
- grad_down: float32 [16, 1024, 2048], P('fsdp', 'tp')
The draws below stay inside these ranges and needn't reach their ends.
Inputs may be any that keep to these rules, and one draw needn't show every extreme that they name: `expert_ids`: in the 512 rows of each sequence every row names 8 different experts, no expert is named by more than 264 rows, a bound that some block reaches. `seg_ids`: within a sequence the document numbers never fall. `pad_mask`: in each sequence the real tokens come first and padding tokens follow.
All inputs are finite; a program needn't handle non-finite values.
Results may differ from the reference program's by a relative error of at most 0.025.
Values may be sent and summed in bfloat16 or wider, within the bound.
No kernel may reach another device: no remote copies, remote signals or barrier semaphores. Data moves between devices by JAX's collectives and lax.ppermute only.
A program may use at most 384 MiB of HBM per device.

```python
import math
import jax
import jax.numpy as jnp
import numpy as np
from jax import lax

D = 2048
HEADS = 16
HD = 128
FF = 1024
TOPK = 8
SEQ = 512
E = 16
NSEQ = 8
TOKENS = 4096
CAP = 264
N_TP = 4


def draw_pad_mask(key, part):
    pad_count = jax.random.randint(key, (NSEQ, 1), 0, SEQ // 8 + 1)
    positions = jnp.arange(SEQ, dtype=jnp.int32)[None, :]
    return (positions < SEQ - pad_count).astype(jnp.int32)


def levels(rng, shape, split, smallest, top_value):
    level = 1.0
    for axis_at, blocks in split:
        heights = jax.random.uniform(jax.random.fold_in(jax.random.fold_in(rng, 6), axis_at), (blocks,), jnp.float32, smallest / len(split), top_value / len(split))
        level = level * jnp.repeat(jnp.exp(heights), shape[axis_at] // blocks).reshape((-1,) + (1,) * (len(shape) - 1 - axis_at))
    return level


def split_up(count, total, limit, lean):
    loads = [(1 << 20) // math.isqrt(rank ** lean) + 1 for rank in range(2, count + 1)]
    rest, holding = total - limit - (count - 1), [1] * (count - 1)
    while rest > 0:
        candidates = [i for i in range(count - 1) if holding[i] < limit]
        pool, budget = sum([loads[i] for i in candidates]), rest
        for i in candidates:
            extra = min(limit - holding[i], max(1, budget * loads[i] // pool), rest)
            holding[i] = holding[i] + extra
            rest = rest - extra
    return np.array([limit] + holding)


def ragged_sizes(key, amount, total, most, skew):
    if amount == 2:
        one = jax.random.randint(key, (), max(1, total - most), min(most, total - 1) + 1)
        return jnp.stack([one, total - one])
    sizes = jnp.asarray(split_up(amount, total, most, skew), jnp.int32)
    couples = (amount - 1) // 2
    donor, sink = sizes[1:1 + 2 * couples:2], sizes[2:2 + 2 * couples:2]
    slack = jnp.minimum(donor - 1, most - sink)
    passed = jax.random.randint(jax.random.fold_in(key, 1), (couples,), 0, 1 << 20) % (slack + 1)
    sizes = sizes.at[1:1 + 2 * couples:2].set(donor - passed).at[2:2 + 2 * couples:2].set(sink + passed)
    return sizes[jax.random.permutation(jax.random.fold_in(key, 2), amount)]


def assign_block(rng, own, number, rows, number_of, top, reach, lean):
    ranking = jax.random.permutation(rng, number_of)
    packed, usual = load_shares(number_of, rows * top, reach, lean, True), load_shares(number_of, rows * top, reach, lean, False)
    places = jnp.arange(number_of)

    def named(sizes, rotation):
        used = int((sizes > 0).sum())
        fixed = max(1, used // 4)
        moved = fixed + (places - fixed + rotation * (used - fixed)) % max(1, number_of - fixed)
        return jnp.zeros((number_of,), jnp.int32).at[ranking[jnp.where(places < fixed, places, moved)]].set(jnp.asarray(sizes, jnp.int32))

    sizes = jnp.where(number % 4 == 0, named(packed, number // 4), named(usual, number - number // 4 - 1))
    mixed = jax.random.permutation(jax.random.fold_in(own, 3), number_of)
    giver, receiver = mixed[0:number_of // 2 * 2:2], mixed[1:number_of // 2 * 2:2]
    slack = jnp.minimum(sizes[giver] - 1, reach - sizes[receiver]) // 2
    slack = jnp.where((giver == ranking[0]) | (receiver == ranking[0]) | (sizes[receiver] == 0), 0, jnp.maximum(slack, 0))
    moved = jax.random.randint(jax.random.fold_in(own, 4), (number_of // 2,), 0, 1 << 20) % (slack + 1)
    sizes = sizes.at[giver].add(-moved).at[receiver].add(moved)
    items = jnp.searchsorted(jnp.cumsum(sizes), jnp.arange(rows * top), side="right").astype(jnp.int32)
    table = items.reshape(top, rows).T
    table = table[jax.random.permutation(jax.random.fold_in(own, 1), rows)]
    rotation = jax.random.randint(jax.random.fold_in(own, 2), (rows, 1), 0, top)
    return jnp.take_along_axis(table, (jnp.arange(top)[None, :] + rotation) % top, axis=1)


def load_shares(amount, total, reach, slope, full):
    weights = [(1 << 20) // math.isqrt(rank ** slope) + 1 for rank in range(1, amount + 1)]
    largest = reach if full else min(reach, max(-(-total // amount), total * weights[0] // sum(weights)))
    least = 1 if total - largest >= amount - 1 else 0
    holding, surplus = [largest] + [least] * (amount - 1), total - largest - least * (amount - 1)
    while surplus > 0:
        free = [i for i in range(1, amount) if holding[i] < largest] or [i for i in range(1, amount) if holding[i] < reach]
        pool, budget = sum([weights[i] for i in free]), surplus
        for i in free:
            more = min(reach - holding[i], max(1, budget * weights[i] // pool), surplus)
            holding[i] = holding[i] + more
            surplus = surplus - more
    return np.array(holding)


def noise(rng, extent, width, bound, cuts=(), kind=jnp.bfloat16):
    result = jax.random.normal(rng, extent, jnp.float32) * width
    if len(cuts) > 0:
        result = levels(rng, extent, cuts, -0.22, 0.18) * result
    return jnp.clip(result, min=-bound, max=bound).astype(kind)


def setup_inputs(seed: int = 0) -> dict:
    arg_keys = jax.random.split(jax.random.key(seed), 13)
    tokens = noise(arg_keys[0], (TOKENS, D), 1.0, 6.0, ((0, 32),))
    seg_ids = jax.vmap(lambda own: jnp.searchsorted(jnp.cumsum(ragged_sizes(own, SEQ // 128 + 2, SEQ, min(800, SEQ * 3 // 4), 2)), jnp.arange(SEQ), side="right"))(jax.random.split(arg_keys[1], NSEQ)).reshape((NSEQ, SEQ)).astype(jnp.int32)
    pad_mask = draw_pad_mask(jax.random.fold_in(arg_keys[12], 71), 0)
    expert_ids_keys = jax.random.split(jax.random.fold_in(arg_keys[3], 1), TOKENS // SEQ)
    expert_ids_turns = jax.random.permutation(jax.random.fold_in(arg_keys[3], 3), TOKENS // SEQ)
    expert_ids = jax.vmap(lambda own, number: assign_block(jax.random.fold_in(arg_keys[3], 2), own, number, SEQ, E, TOPK, CAP, 1))(expert_ids_keys, expert_ids_turns).reshape((TOKENS, TOPK))
    w_qkv = noise(arg_keys[4], (3, D, D), D ** -0.5, 0.125, ((1, 8), (2, 4)))
    w_out = noise(arg_keys[5], (D, D), (D // 64) ** -0.5, 1.0, ((0, 4), (1, 8)))
    w_router = noise(arg_keys[6], (D, E), (4 * D) ** -0.5, 0.0625, ((0, 32),))
    norm_gains = jnp.clip(1.0 + 0.15 * jax.random.normal(arg_keys[7], (4, D), jnp.float32), 0.25, 1.75).astype(jnp.bfloat16)
    w_gate = noise(arg_keys[8], (E, D, FF), D ** -0.5, 0.125, ((0, 8), (2, 4)))
    w_up = noise(arg_keys[9], (E, D, FF), D ** -0.5, 0.125, ((0, 8), (2, 4)))
    w_down = noise(arg_keys[10], (E, FF, D), (max(1, FF // 512)) ** -0.5, 4.0, ((0, 8), (1, 4)))
    cotangent = noise(arg_keys[11], (TOKENS, D), 1.0, 6.0, ((0, 32),))
    return dict(tokens=tokens, seg_ids=seg_ids, pad_mask=pad_mask, expert_ids=expert_ids, w_qkv=w_qkv, w_out=w_out, w_router=w_router, norm_gains=norm_gains, w_gate=w_gate, w_up=w_up, w_down=w_down, cotangent=cotangent)


EPSILON = 1e-05
NEG_FILL = -1e+30
HIGH = lax.Precision.HIGHEST

@jax.custom_vjp
def low(v):
    return lax.optimization_barrier(v.astype(jnp.bfloat16)).astype(jnp.float32)

@jax.custom_vjp
def low_back(v):
    return v

def low_keep(v):
    return (low(v), None)

def low_pass(kept, grad):
    return (grad,)

def back_keep(v):
    return (v, None)

def back_low(kept, grad):
    return (low(grad),)
low.defvjp(low_keep, low_pass)
low_back.defvjp(back_keep, back_low)

def rms_norm(values, gain):
    return values * lax.rsqrt(lax.optimization_barrier(jnp.mean(values * values, axis=-1, keepdims=True)) + EPSILON) * gain

def route_slots(expert_ids, n_experts, capacity):
    seq_len, top_count = expert_ids.shape
    experts = jnp.arange(n_experts, dtype=jnp.int32)
    counts = lax.optimization_barrier(jnp.sum((expert_ids[:, :, None] == experts[None, None, :]).astype(jnp.int32), axis=1))
    earlier = jnp.cumsum(counts, axis=0) - counts
    slot_rank = jnp.take_along_axis(earlier, expert_ids, axis=1)
    flat_index = (expert_ids * capacity + slot_rank).astype(jnp.int32)
    token_index = jnp.broadcast_to(jnp.arange(seq_len, dtype=jnp.int32)[:, None], (seq_len, top_count))
    source = jnp.full((n_experts * capacity,), seq_len, jnp.int32)
    source = source.at[flat_index.reshape(-1)].set(token_index.reshape(-1))
    return (flat_index, source)

def rope_tables(seq_len, head_size):
    half_size = head_size // 2
    inverse = 10000.0 ** (-2.0 * jnp.arange(half_size, dtype=jnp.float32) / head_size)
    angles = jnp.arange(seq_len, dtype=jnp.float32)[:, None] * inverse[None, :]
    return (jnp.cos(angles)[:, None, :], jnp.sin(angles)[:, None, :])

def rotate(values, cosine, sine):
    half_size = values.shape[-1] // 2
    first = values[..., :half_size]
    second = values[..., half_size:]
    return jnp.concatenate([first * cosine - second * sine, second * cosine + first * sine], axis=-1)

def allowed_mask(segment, padding, row_start, row_count):
    row_index = row_start + jnp.arange(row_count, dtype=jnp.int32)
    col_index = jnp.arange(segment.shape[0], dtype=jnp.int32)
    row_doc = lax.dynamic_slice_in_dim(segment, row_start, row_count)
    same_doc = row_doc[:, None] == segment[None, :]
    causal = col_index[None, :] <= row_index[:, None]
    usable = (padding[None, :] == 1) | (col_index[None, :] == row_index[:, None])
    return same_doc & causal & usable

def sequence_forward(x_seq, segment, padding, route_ids, weights):
    w_qkv, w_out, w_router, gains, w_gate, w_up, w_down = weights
    cosine, sine = rope_tables(SEQ, HD)
    normed1 = low(rms_norm(x_seq, gains[0]))
    projected = jnp.einsum('sd,cdh->csh', normed1, w_qkv, precision=HIGH)
    query_raw = low_back(projected[0])
    key_raw = low_back(projected[1])
    values = low(low_back(projected[2])).reshape(SEQ, HEADS, HD)
    queries = low(rotate(rms_norm(query_raw, gains[2]).reshape(SEQ, HEADS, HD), cosine, sine))
    keys = low(rotate(rms_norm(key_raw, gains[3]).reshape(SEQ, HEADS, HD), cosine, sine))
    scores = low_back(jnp.einsum('qhd,khd->hqk', queries, keys, precision=HIGH) * HD ** (-0.5))
    allowed = allowed_mask(segment, padding, 0, SEQ)
    scores = jnp.where(allowed[None], scores, NEG_FILL)
    probs = low(jax.nn.softmax(scores, axis=-1))
    mixed = low(low_back(jnp.einsum('hqk,khd->qhd', probs, values, precision=HIGH).reshape(SEQ, D)))
    hidden = x_seq + low_back(jnp.dot(mixed, w_out, precision=HIGH))
    normed2 = low(rms_norm(hidden, gains[1]))
    logits = low_back(jnp.dot(normed2, w_router, precision=HIGH))
    router_probs = jax.nn.softmax(logits, axis=-1)
    gates = jnp.take_along_axis(router_probs, route_ids, axis=1)
    flat_index, source = route_slots(route_ids, E, CAP)
    padded = jnp.concatenate([normed2, jnp.zeros((1, D), normed2.dtype)], axis=0)
    buffer = padded[source].reshape(E, CAP, D)
    group_width = FF // N_TP
    gate_groups = w_gate.reshape(E, D, N_TP, group_width).transpose(2, 0, 1, 3)
    up_groups = w_up.reshape(E, D, N_TP, group_width).transpose(2, 0, 1, 3)
    down_groups = w_down.reshape(E, N_TP, group_width, D).transpose(1, 0, 2, 3)

    def group_part(group):
        gate_weight, up_weight, down_weight = group
        inputs = low_back(buffer)
        gate_pre = low_back(jnp.einsum('ecd,edf->ecf', inputs, gate_weight, precision=HIGH))
        up_pre = low_back(jnp.einsum('ecd,edf->ecf', inputs, up_weight, precision=HIGH))
        active = low(jax.nn.silu(gate_pre) * up_pre)
        return low(low_back(jnp.einsum('ecf,efd->ecd', active, down_weight, precision=HIGH)))
    parts = lax.map(group_part, (gate_groups, up_groups, down_groups))
    summed = lax.optimization_barrier(jnp.sum(parts, axis=0)).reshape(E * CAP, D)
    expert_out = jnp.einsum('skd,sk->sd', summed[flat_index], gates, precision=HIGH)
    return hidden + expert_out

def reference(tokens, seg_ids, pad_mask, expert_ids, w_qkv, w_out, w_router, norm_gains, w_gate, w_up, w_down, cotangent):
    weights = tuple((member.astype(jnp.float32) for member in (w_qkv, w_out, w_router, norm_gains, w_gate, w_up, w_down)))
    x_all = tokens.astype(jnp.float32)
    route_all = expert_ids.reshape(NSEQ, SEQ, TOPK)
    checked = jax.checkpoint(sequence_forward)

    def forward(x_values, *weight_values):

        def scan_step(carried, pieces):
            x_seq, segment, padding, route_ids = pieces
            return (carried, checked(x_seq, segment, padding, route_ids, weight_values))
        unused, outputs = lax.scan(scan_step, jnp.zeros((), jnp.float32), (x_values.reshape(NSEQ, SEQ, D), seg_ids, pad_mask, route_all))
        return outputs.reshape(TOKENS, D)
    layer_out, pullback = jax.vjp(forward, x_all, *weights)
    grads = pullback(cotangent.astype(jnp.float32))
    return (layer_out.astype(jnp.bfloat16), grads[0], grads[1], grads[2], grads[3], grads[4], grads[5], grads[6], grads[7])
```

```python
import jax
import jax.numpy as jnp
from jax import lax
from jax.sharding import PartitionSpec as P

HD = 128


EPSILON = 1e-05
NEG_FILL = -1e30


def route_slots(expert_ids, n_experts, capacity):
    seq_len, top_count = expert_ids.shape
    experts = jnp.arange(n_experts, dtype=jnp.int32)
    counts = jnp.sum((expert_ids[:, :, None] == experts[None, None, :]).astype(jnp.int32), axis=1)
    earlier = jnp.cumsum(counts, axis=0) - counts
    slot_rank = jnp.take_along_axis(earlier, expert_ids, axis=1)
    flat_index = expert_ids * capacity + slot_rank
    token_index = jnp.broadcast_to(
        jnp.arange(seq_len, dtype=jnp.int32)[:, None], (seq_len, top_count)
    )
    source = jnp.full((n_experts * capacity,), seq_len, jnp.int32)
    source = source.at[flat_index.reshape(-1)].set(token_index.reshape(-1))
    return (flat_index, source)


def rope_tables(seq_len, head_size):
    half_size = head_size // 2
    inverse = 10000.0 ** (-2.0 * jnp.arange(half_size, dtype=jnp.float32) / head_size)
    angles = jnp.arange(seq_len, dtype=jnp.float32)[:, None] * inverse[None, :]
    return (jnp.cos(angles)[:, None, :], jnp.sin(angles)[:, None, :])


def rotate(values, cosine, sine):
    half_size = values.shape[-1] // 2
    first = values[..., :half_size]
    second = values[..., half_size:]
    return jnp.concatenate(
        [first * cosine - second * sine, second * cosine + first * sine], axis=-1
    )


def rotate_back(grads, cosine, sine):
    half_size = grads.shape[-1] // 2
    first = grads[..., :half_size]
    second = grads[..., half_size:]
    return jnp.concatenate(
        [first * cosine + second * sine, second * cosine - first * sine], axis=-1
    )


def allowed_mask(segment, padding, row_start, row_count):
    row_index = row_start + jnp.arange(row_count, dtype=jnp.int32)
    col_index = jnp.arange(segment.shape[0], dtype=jnp.int32)
    same_doc = segment[:, None] == segment[None, :]
    causal = col_index[None, :] <= row_index[:, None]
    usable = (padding[None, :] == 1) | (col_index[None, :] == row_index[:, None])
    return same_doc & causal & usable


def norm_forward(values, gain):
    scale = lax.rsqrt(jnp.mean(values * values, axis=-1, keepdims=True) + EPSILON)
    return (values * scale * gain, scale)


def norm_backward(values, scale, gain, grads):
    unit = values * scale
    gain_grad = jnp.sum(grads * unit, axis=0)
    scaled = grads * gain
    return (scale * (scaled - unit * jnp.mean(scaled * unit, axis=-1, keepdims=True)), gain_grad)


def gather_rows(values):
    return lax.all_gather(values, "tp", axis=0, tiled=True)


def scatter_rows(values):
    return lax.psum_scatter(
        values.astype(jnp.bfloat16), "tp", scatter_dimension=0, tiled=True
    ).astype(jnp.float32)


def tp_totals(first, second):
    return lax.psum((first, second), "tp")


def shards(
    tokens,
    seg_ids,
    pad_mask,
    expert_ids,
    w_qkv,
    w_out,
    w_router,
    norm_gains,
    w_gate,
    w_up,
    w_down,
    cotangent,
):
    tp_rank = lax.axis_index("tp")
    fsdp_count = lax.axis_size("fsdp")
    local_rows, width = tokens.shape
    seq_len = seg_ids.shape[1]
    exp_local = w_gate.shape[0]
    ff_local = w_gate.shape[2]
    n_experts = exp_local * fsdp_count
    top_count = expert_ids.shape[1]
    capacity = (seq_len * top_count * 33 + 32 * n_experts - 1) // (32 * n_experts)
    head_cols = w_qkv.shape[2]
    heads_local = head_cols // HD
    block_rows = min(512, seq_len)
    n_blocks = seq_len // block_rows
    score_scale = HD ** (-0.5)

    def send_experts(buffer):
        return lax.all_to_all(buffer, "fsdp", split_axis=0, concat_axis=1, tiled=True)

    def return_experts(buffer):
        back = lax.all_to_all(buffer, "fsdp", split_axis=1, concat_axis=0, tiled=True)
        return back.reshape(n_experts * capacity, back.shape[2])

    qkv_full, out_full = (
        lax.all_gather(w_qkv, "fsdp", axis=1, tiled=True),
        lax.all_gather(w_out, "fsdp", axis=1, tiled=True),
    )
    router_full, gains_full = (
        lax.all_gather(w_router, ("fsdp", "tp"), axis=0, tiled=True),
        lax.all_gather(norm_gains, ("fsdp", "tp"), axis=1, tiled=True),
    )
    gains_wide = gains_full.astype(jnp.float32)
    col_start = tp_rank * head_cols
    gain_query = lax.dynamic_slice_in_dim(gains_wide[2], col_start, head_cols)
    gain_key = lax.dynamic_slice_in_dim(gains_wide[3], col_start, head_cols)
    segment = seg_ids[0]
    padding = pad_mask[0]
    cosine, sine = rope_tables(seq_len, HD)
    x_own = tokens.astype(jnp.float32)
    normed1, scale1 = norm_forward(x_own, gains_wide[0])
    rows1 = gather_rows(normed1.astype(jnp.bfloat16))
    projected = jnp.einsum("sd,cdh->csh", rows1, qkv_full, preferred_element_type=jnp.float32)
    query_raw = projected[0]
    key_raw = projected[1]
    square_q, square_k = tp_totals(
        jnp.sum(query_raw * query_raw, axis=-1), jnp.sum(key_raw * key_raw, axis=-1)
    )
    scale_q = lax.rsqrt(square_q / width + EPSILON)[:, None]
    scale_k = lax.rsqrt(square_k / width + EPSILON)[:, None]
    unit_q = query_raw * scale_q
    unit_k = key_raw * scale_k
    queries = rotate((unit_q * gain_query).reshape(seq_len, heads_local, HD), cosine, sine).astype(
        jnp.bfloat16
    )
    keys = rotate((unit_k * gain_key).reshape(seq_len, heads_local, HD), cosine, sine).astype(
        jnp.bfloat16
    )
    values = projected[2].astype(jnp.bfloat16).reshape(seq_len, heads_local, HD)
    block_starts = jnp.arange(n_blocks, dtype=jnp.int32) * block_rows

    def block_scores(start):
        raw_scores = (
            jnp.einsum("qhd,khd->hqk", queries, keys, preferred_element_type=jnp.float32)
            * score_scale
        )
        allowed = allowed_mask(segment, padding, start, block_rows)
        return (queries, jnp.where(allowed[None], raw_scores, NEG_FILL), allowed)

    def attend(start):
        query_block, scores, allowed = block_scores(start)
        peak = jnp.max(scores, axis=-1, keepdims=True)
        powered = jnp.exp(scores - peak)
        total = jnp.sum(powered, axis=-1, keepdims=True)
        probs_low = (powered / total).astype(jnp.bfloat16)
        mixed_block = jnp.einsum(
            "hqk,khd->qhd", probs_low, values, preferred_element_type=jnp.float32
        )
        return (
            mixed_block.reshape(block_rows, head_cols).astype(jnp.bfloat16),
            (peak + jnp.log(total))[..., 0],
        )

    mixed_blocks, log_sums = lax.map(attend, block_starts)
    mixed = mixed_blocks.reshape(seq_len, head_cols)
    hidden = x_own + scatter_rows(jnp.dot(mixed, out_full, preferred_element_type=jnp.float32))
    normed2, scale2 = norm_forward(hidden, gains_wide[1])
    own_normed2 = normed2.astype(jnp.bfloat16)
    rows2 = gather_rows(own_normed2)
    logits = jnp.dot(rows2, router_full, preferred_element_type=jnp.float32)
    router_probs = jax.nn.softmax(logits, axis=-1)
    gates = jnp.take_along_axis(router_probs, expert_ids, axis=1)
    flat_index, source = route_slots(expert_ids, n_experts, capacity)
    padded_rows = jnp.concatenate([rows2, jnp.zeros((1, width), jnp.bfloat16)], axis=0)
    received = send_experts(padded_rows[source].reshape(n_experts, capacity, width))
    w_pair = jnp.concatenate([w_gate, w_up], axis=2)
    pair_pre = jnp.einsum("erd,edf->erf", received, w_pair, preferred_element_type=jnp.float32)
    gate_pre = pair_pre[..., :ff_local]
    up_pre = pair_pre[..., ff_local:]
    sigmoid_gate = jax.nn.sigmoid(gate_pre)
    silu_gate = gate_pre * sigmoid_gate
    active = (silu_gate * up_pre).astype(jnp.bfloat16)
    expert_part = jnp.einsum(
        "erf,efd->erd", active, w_down, preferred_element_type=jnp.float32
    ).astype(jnp.bfloat16)
    returned = return_experts(expert_part)
    combined = jnp.zeros((seq_len, returned.shape[1]), jnp.float32)
    for pick_rank in range(top_count):
        combined = combined + gates[:, pick_rank : pick_rank + 1] * returned[
            flat_index[:, pick_rank]
        ].astype(jnp.float32)
    layer_out = (hidden + scatter_rows(combined)).astype(jnp.bfloat16)
    grad_rows = gather_rows(cotangent)
    grad_cols = grad_rows.astype(jnp.float32)
    partial_dots = jnp.stack(
        [
            jnp.sum(returned[flat_index[:, pick_rank]].astype(jnp.float32) * grad_cols, axis=-1)
            for pick_rank in range(top_count)
        ],
        axis=1,
    )
    gate_dots = lax.psum(partial_dots, "tp")
    expert_range = jnp.arange(n_experts, dtype=jnp.int32)
    chosen = jnp.sum(
        gate_dots[:, :, None]
        * (expert_ids[:, :, None] == expert_range[None, None, :]).astype(jnp.float32),
        axis=1,
    )
    weighted = jnp.sum(gates * gate_dots, axis=-1, keepdims=True)
    logit_grad = (router_probs * (chosen - weighted)).astype(jnp.bfloat16)
    own_logit_grad = lax.dynamic_slice_in_dim(logit_grad, tp_rank * local_rows, local_rows, 0)
    slot_gates = (
        jnp.zeros((n_experts * capacity,), jnp.float32)
        .at[flat_index.reshape(-1)]
        .set(gates.reshape(-1))
    )
    padded_grads = jnp.concatenate([grad_rows, jnp.zeros((1, width), jnp.bfloat16)], axis=0)
    slot_grads = (padded_grads[source].astype(jnp.float32) * slot_gates[:, None]).astype(
        jnp.bfloat16
    )
    grad_received = send_experts(slot_grads.reshape(n_experts, capacity, width))
    active_grad = jnp.einsum(
        "erd,efd->erf", grad_received, w_down, preferred_element_type=jnp.float32
    )
    gate_grad = (
        active_grad * up_pre * sigmoid_gate * (1.0 + gate_pre * (1.0 - sigmoid_gate))
    ).astype(jnp.bfloat16)
    up_grad = (active_grad * silu_gate).astype(jnp.bfloat16)
    pair_grad = jnp.concatenate([gate_grad, up_grad], axis=2)
    grad_down = jnp.einsum(
        "erf,erd->efd", active, grad_received, preferred_element_type=jnp.float32
    )
    grad_pair = jnp.einsum("erd,erf->edf", received, pair_grad, preferred_element_type=jnp.float32)
    grad_gate = grad_pair[..., :ff_local]
    grad_up = grad_pair[..., ff_local:]
    input_part = jnp.einsum(
        "erf,edf->erd", pair_grad, w_pair, preferred_element_type=jnp.float32
    ).astype(jnp.bfloat16)
    sent_back = return_experts(input_part)
    token_grad = jnp.zeros((seq_len, sent_back.shape[1]), jnp.float32)
    for pick_rank in range(top_count):
        token_grad = token_grad + sent_back[flat_index[:, pick_rank]].astype(jnp.float32)
    normed2_grad = scatter_rows(token_grad) + jnp.dot(
        own_logit_grad, router_full.T, preferred_element_type=jnp.float32
    )
    hidden_norm_grad, gain2_grad = norm_backward(hidden, scale2, gains_wide[1], normed2_grad)
    hidden_grad = cotangent.astype(jnp.float32) + hidden_norm_grad
    router_grad = jnp.dot(own_normed2.T, own_logit_grad, preferred_element_type=jnp.float32)
    hidden_rows = gather_rows(hidden_grad.astype(jnp.bfloat16))
    grad_out_full = jnp.dot(mixed.T, hidden_rows, preferred_element_type=jnp.float32)
    mixed_grad = (
        jnp.dot(hidden_rows, out_full.T, preferred_element_type=jnp.float32)
        .astype(jnp.bfloat16)
        .reshape(seq_len, heads_local, HD)
    )

    def attend_back(carried, pieces):
        key_acc, value_acc = carried
        start, log_sum = pieces
        query_block, scores, allowed = block_scores(start)
        probs = jnp.where(allowed[None], jnp.exp(scores - log_sum[:, :, None]), 0.0)
        prob_grad = jnp.einsum(
            "qhd,khd->hqk", mixed_grad, values, preferred_element_type=jnp.float32
        )
        delta = jnp.sum(probs * prob_grad, axis=-1, keepdims=True)
        score_grad = (probs * (prob_grad - delta)).astype(jnp.bfloat16)
        query_block_grad = (
            jnp.einsum("hqk,khd->qhd", score_grad, keys, preferred_element_type=jnp.float32)
            * score_scale
        )
        key_acc = (
            key_acc
            + jnp.einsum(
                "hqk,qhd->khd", score_grad, query_block, preferred_element_type=jnp.float32
            )
            * score_scale
        )
        value_acc = value_acc + jnp.einsum(
            "hqk,qhd->khd",
            probs.astype(jnp.bfloat16),
            mixed_grad,
            preferred_element_type=jnp.float32,
        )
        return ((key_acc, value_acc), query_block_grad)

    zero_heads = jnp.zeros((seq_len, heads_local, HD), jnp.float32)
    (key_grad, value_grad), query_blocks = lax.scan(
        attend_back, (zero_heads, zero_heads), (block_starts, log_sums)
    )
    query_grad = query_blocks.reshape(seq_len, heads_local, HD)
    query_norm_grad = rotate_back(query_grad, cosine, sine).reshape(seq_len, head_cols)
    key_norm_grad = rotate_back(key_grad, cosine, sine).reshape(seq_len, head_cols)
    gain_query_grad = jnp.sum(query_norm_grad * unit_q, axis=0)
    gain_key_grad = jnp.sum(key_norm_grad * unit_k, axis=0)
    scaled_q = query_norm_grad * gain_query
    scaled_k = key_norm_grad * gain_key
    inner_q, inner_k = tp_totals(
        jnp.sum(scaled_q * unit_q, axis=-1), jnp.sum(scaled_k * unit_k, axis=-1)
    )
    query_raw_grad = scale_q * (scaled_q - unit_q * (inner_q / width)[:, None])
    key_raw_grad = scale_k * (scaled_k - unit_k * (inner_k / width)[:, None])
    qkv_grad = jnp.stack(
        [query_raw_grad, key_raw_grad, value_grad.reshape(seq_len, head_cols)]
    ).astype(jnp.bfloat16)
    grad_qkv_full = jnp.einsum("sd,csh->cdh", rows1, qkv_grad, preferred_element_type=jnp.float32)
    normed1_part = jnp.einsum("csh,cdh->sd", qkv_grad, qkv_full, preferred_element_type=jnp.float32)
    normed1_grad = scatter_rows(normed1_part)
    input_norm_grad, gain1_grad = norm_backward(x_own, scale1, gains_wide[0], normed1_grad)
    input_grad = hidden_grad + input_norm_grad
    zero_width = jnp.zeros((width,), jnp.float32)
    gains_grad = jnp.stack(
        [
            gain1_grad,
            gain2_grad,
            lax.dynamic_update_slice_in_dim(zero_width, gain_query_grad, col_start, 0),
            lax.dynamic_update_slice_in_dim(zero_width, gain_key_grad, col_start, 0),
        ]
    )
    grad_qkv, grad_out = (
        lax.psum_scatter(
            grad_qkv_full.astype(jnp.bfloat16), "fsdp", scatter_dimension=1, tiled=True
        ).astype(jnp.float32),
        lax.psum_scatter(
            grad_out_full.astype(jnp.bfloat16), "fsdp", scatter_dimension=1, tiled=True
        ).astype(jnp.float32),
    )
    grad_router, grad_gains = (
        lax.psum_scatter(router_grad, ("fsdp", "tp"), scatter_dimension=0, tiled=True),
        lax.psum_scatter(gains_grad, ("fsdp", "tp"), scatter_dimension=1, tiled=True),
    )
    return (
        layer_out,
        input_grad,
        grad_qkv,
        grad_out,
        grad_router,
        grad_gains,
        grad_gate,
        grad_up,
        grad_down,
    )


def gather_all(values, axis=0):
    return lax.all_gather(values, ("fsdp", "tp"), axis=axis, tiled=True)


def scatter_all(values):
    return lax.psum_scatter(values, ("fsdp", "tp"), scatter_dimension=0, tiled=True)


def dense_shards(
    tokens,
    seg_ids,
    pad_mask,
    expert_ids,
    w_qkv,
    w_out,
    w_router,
    norm_gains,
    w_gate,
    w_up,
    w_down,
    cotangent,
):
    fsdp_rank = lax.axis_index("fsdp")
    tp_rank = lax.axis_index("tp")
    fsdp_count = lax.axis_size("fsdp")
    tp_count = lax.axis_size("tp")
    local_rows, width = tokens.shape
    seq_len = seg_ids.shape[1]
    exp_local, _, ff_local = w_gate.shape
    n_experts = exp_local * fsdp_count
    head_cols = w_qkv.shape[2]
    heads_local = head_cols // HD
    score_scale = HD ** (-0.5)
    own_start = tp_rank * local_rows

    def own_rows(values):
        return lax.dynamic_slice_in_dim(values, own_start, local_rows, 0)

    rows_x = gather_rows(tokens).astype(jnp.float32)
    qkv_full = lax.all_gather(w_qkv, "fsdp", axis=1, tiled=True)
    out_full = lax.all_gather(w_out, "fsdp", axis=1, tiled=True)
    small_full = gather_all(jnp.concatenate([w_router, norm_gains.T], axis=1))
    router_full = small_full[:, :n_experts]
    gains_wide = small_full[:, n_experts:].T.astype(jnp.float32)
    all_y = gather_all(cotangent)
    col_start = tp_rank * head_cols
    gain_query = lax.dynamic_slice_in_dim(gains_wide[2], col_start, head_cols)
    gain_key = lax.dynamic_slice_in_dim(gains_wide[3], col_start, head_cols)
    cosine, sine = rope_tables(seq_len, HD)
    x_own = tokens.astype(jnp.float32)
    normed1, scale1 = norm_forward(rows_x, gains_wide[0])
    rows1 = normed1.astype(jnp.bfloat16)
    projected = jnp.einsum("sd,cdh->csh", rows1, qkv_full, preferred_element_type=jnp.float32)
    query_raw = projected[0]
    key_raw = projected[1]
    square_q, square_k = tp_totals(
        jnp.sum(query_raw * query_raw, axis=-1), jnp.sum(key_raw * key_raw, axis=-1)
    )
    scale_q = lax.rsqrt(square_q / width + EPSILON)[:, None]
    scale_k = lax.rsqrt(square_k / width + EPSILON)[:, None]
    unit_q = query_raw * scale_q
    unit_k = key_raw * scale_k
    queries = rotate((unit_q * gain_query).reshape(seq_len, heads_local, HD), cosine, sine).astype(
        jnp.bfloat16
    )
    keys = rotate((unit_k * gain_key).reshape(seq_len, heads_local, HD), cosine, sine).astype(
        jnp.bfloat16
    )
    values = projected[2].astype(jnp.bfloat16).reshape(seq_len, heads_local, HD)
    raw_scores = (
        jnp.einsum("qhd,khd->hqk", queries, keys, preferred_element_type=jnp.float32) * score_scale
    )
    allowed = allowed_mask(seg_ids[0], pad_mask[0], 0, seq_len)
    scores = jnp.where(allowed[None], raw_scores, NEG_FILL)
    powered = jnp.exp(scores - jnp.max(scores, axis=-1, keepdims=True))
    probs = powered / jnp.sum(powered, axis=-1, keepdims=True)
    probs_low = probs.astype(jnp.bfloat16)
    mixed = (
        jnp.einsum("hqk,khd->qhd", probs_low, values, preferred_element_type=jnp.float32)
        .reshape(seq_len, head_cols)
        .astype(jnp.bfloat16)
    )
    hidden = x_own + scatter_rows(jnp.dot(mixed, out_full, preferred_element_type=jnp.float32))
    normed2, scale2 = norm_forward(hidden, gains_wide[1])
    own_normed2 = normed2.astype(jnp.bfloat16)
    all_n2 = gather_all(own_normed2)

    logits = jnp.dot(own_normed2, router_full, preferred_element_type=jnp.float32)
    router_probs = jax.nn.softmax(logits, axis=-1)
    own_ids = own_rows(expert_ids)
    expert_range = jnp.arange(n_experts, dtype=jnp.int32)
    named = (own_ids[:, :, None] == expert_range[None, None, :]).any(axis=1)
    own_gates = jnp.where(named, router_probs, 0.0)
    all_gates = gather_all(own_gates)
    local_gates = lax.dynamic_slice_in_dim(all_gates, fsdp_rank * exp_local, exp_local, 1)

    gate_pre = jnp.einsum("td,edf->tef", all_n2, w_gate, preferred_element_type=jnp.float32)
    up_pre = jnp.einsum("td,edf->tef", all_n2, w_up, preferred_element_type=jnp.float32)
    y_down = jnp.einsum("td,efd->tef", all_y, w_down, preferred_element_type=jnp.float32)
    sigmoid_gate = jax.nn.sigmoid(gate_pre)
    silu_gate = gate_pre * sigmoid_gate
    active = silu_gate * up_pre
    part_dots = jnp.sum(active * y_down, axis=-1)
    gated_active = (active * local_gates[:, :, None]).astype(jnp.bfloat16)
    active_grad = y_down * local_gates[:, :, None]
    gate_grad = (
        active_grad * up_pre * sigmoid_gate * (1.0 + gate_pre * (1.0 - sigmoid_gate))
    ).astype(jnp.bfloat16)
    up_grad = (active_grad * silu_gate).astype(jnp.bfloat16)
    token_grad = (
        jnp.einsum("tef,edf->td", gate_grad, w_gate, preferred_element_type=jnp.float32)
        + jnp.einsum("tef,edf->td", up_grad, w_up, preferred_element_type=jnp.float32)
    ).astype(jnp.bfloat16)
    combined = jnp.einsum(
        "tef,efd->td", gated_active, w_down, preferred_element_type=jnp.float32
    ).astype(jnp.bfloat16)

    all_dots = lax.all_gather(lax.psum(part_dots.T, "tp"), "fsdp", axis=0, tiled=True)
    own_dots = lax.dynamic_slice_in_dim(
        all_dots, (fsdp_rank * tp_count + tp_rank) * local_rows, local_rows, 1
    ).T
    chosen = jnp.where(named, own_dots, 0.0)
    weighted = jnp.sum(own_gates * chosen, axis=-1, keepdims=True)
    own_logit_grad = (router_probs * (chosen - weighted)).astype(jnp.bfloat16)

    normed2_grad = scatter_all(token_grad).astype(jnp.float32) + jnp.dot(
        own_logit_grad, router_full.T, preferred_element_type=jnp.float32
    )
    hidden_norm_grad, gain2_grad = norm_backward(hidden, scale2, gains_wide[1], normed2_grad)
    hidden_grad = cotangent.astype(jnp.float32) + hidden_norm_grad
    hidden_rows = gather_rows(hidden_grad.astype(jnp.bfloat16))

    layer_out = (hidden + scatter_all(combined).astype(jnp.float32)).astype(jnp.bfloat16)
    grad_down = jnp.einsum("tef,td->efd", gated_active, all_y, preferred_element_type=jnp.float32)
    grad_gate = jnp.einsum("td,tef->edf", all_n2, gate_grad, preferred_element_type=jnp.float32)
    grad_up = jnp.einsum("td,tef->edf", all_n2, up_grad, preferred_element_type=jnp.float32)
    all_logit_grad = gather_all(own_logit_grad)
    router_rows = w_router.shape[0]
    router_cols = lax.dynamic_slice_in_dim(
        all_n2, (fsdp_rank * tp_count + tp_rank) * router_rows, router_rows, 1
    )
    grad_router = jnp.einsum(
        "td,te->de", router_cols, all_logit_grad, preferred_element_type=jnp.float32
    )

    grad_out_full = jnp.dot(mixed.T, hidden_rows, preferred_element_type=jnp.float32)
    mixed_grad = (
        jnp.dot(hidden_rows, out_full.T, preferred_element_type=jnp.float32)
        .astype(jnp.bfloat16)
        .reshape(seq_len, heads_local, HD)
    )
    prob_grad = jnp.einsum("qhd,khd->hqk", mixed_grad, values, preferred_element_type=jnp.float32)
    delta = jnp.sum(probs * prob_grad, axis=-1, keepdims=True)
    score_grad = (probs * (prob_grad - delta)).astype(jnp.bfloat16)
    query_grad = (
        jnp.einsum("hqk,khd->qhd", score_grad, keys, preferred_element_type=jnp.float32)
        * score_scale
    )
    key_grad = (
        jnp.einsum("hqk,qhd->khd", score_grad, queries, preferred_element_type=jnp.float32)
        * score_scale
    )
    value_grad = jnp.einsum(
        "hqk,qhd->khd", probs_low, mixed_grad, preferred_element_type=jnp.float32
    )
    query_norm_grad = rotate_back(query_grad, cosine, sine).reshape(seq_len, head_cols)
    key_norm_grad = rotate_back(key_grad, cosine, sine).reshape(seq_len, head_cols)
    gain_query_grad = jnp.sum(query_norm_grad * unit_q, axis=0)
    gain_key_grad = jnp.sum(key_norm_grad * unit_k, axis=0)
    scaled_q = query_norm_grad * gain_query
    scaled_k = key_norm_grad * gain_key
    inner_q, inner_k = tp_totals(
        jnp.sum(scaled_q * unit_q, axis=-1), jnp.sum(scaled_k * unit_k, axis=-1)
    )
    query_raw_grad = scale_q * (scaled_q - unit_q * (inner_q / width)[:, None])
    key_raw_grad = scale_k * (scaled_k - unit_k * (inner_k / width)[:, None])
    qkv_grad = jnp.stack(
        [query_raw_grad, key_raw_grad, value_grad.reshape(seq_len, head_cols)]
    ).astype(jnp.bfloat16)
    grad_qkv_full = jnp.einsum("sd,csh->cdh", rows1, qkv_grad, preferred_element_type=jnp.float32)
    normed1_part = jnp.einsum("csh,cdh->sd", qkv_grad, qkv_full, preferred_element_type=jnp.float32)
    normed1_grad = scatter_rows(normed1_part)
    gain1_grad = jnp.sum(normed1_part * (rows_x * scale1), axis=0)
    input_norm_grad, _ = norm_backward(x_own, own_rows(scale1), gains_wide[0], normed1_grad)
    input_grad = hidden_grad + input_norm_grad
    zero_width = jnp.zeros((width,), jnp.float32)
    gains_grad = jnp.stack(
        [
            gain1_grad,
            gain2_grad,
            lax.dynamic_update_slice_in_dim(zero_width, gain_query_grad, col_start, 0),
            lax.dynamic_update_slice_in_dim(zero_width, gain_key_grad, col_start, 0),
        ]
    )
    grad_qkv = lax.psum_scatter(
        grad_qkv_full.astype(jnp.bfloat16), "fsdp", scatter_dimension=1, tiled=True
    ).astype(jnp.float32)
    grad_out = lax.psum_scatter(
        grad_out_full.astype(jnp.bfloat16), "fsdp", scatter_dimension=1, tiled=True
    ).astype(jnp.float32)
    gain_cols = norm_gains.shape[1]
    grad_gains = lax.dynamic_slice_in_dim(
        lax.psum(gains_grad, ("fsdp", "tp")),
        (fsdp_rank * tp_count + tp_rank) * gain_cols,
        gain_cols,
        1,
    )
    return (
        layer_out,
        input_grad,
        grad_qkv,
        grad_out,
        grad_router,
        grad_gains,
        grad_gate,
        grad_up,
        grad_down,
    )


def pick_shards(*arguments):
    n_experts = arguments[8].shape[0] * lax.axis_size("fsdp")
    top_count = arguments[3].shape[1]
    body = dense_shards if n_experts <= 2 * top_count else shards
    return body(*arguments)


def solution(mesh):
    placed = (
        P(("fsdp", "tp"), None),
        P("fsdp", None),
        P("fsdp", None),
        P("fsdp", None),
        P(None, "fsdp", "tp"),
        P("tp", "fsdp"),
        P(("fsdp", "tp"), None),
        P(None, ("fsdp", "tp")),
        P("fsdp", None, "tp"),
        P("fsdp", None, "tp"),
        P("fsdp", "tp", None),
        P(("fsdp", "tp"), None),
    )
    return jax.shard_map(
        pick_shards,
        mesh=mesh,
        in_specs=placed,
        out_specs=(
            P(("fsdp", "tp"), None),
            P(("fsdp", "tp"), None),
            P(None, "fsdp", "tp"),
            P("tp", "fsdp"),
            P(("fsdp", "tp"), None),
            P(None, ("fsdp", "tp")),
            P("fsdp", None, "tp"),
            P("fsdp", None, "tp"),
            P("fsdp", "tp", None),
        ),
        check_vma=False,
    )
```

```python
import functools
import itertools

import jax
import jax.numpy as jnp
from jax import lax
from jax.experimental import pallas as pl
from jax.experimental.pallas import tpu as pltpu
from jax.sharding import PartitionSpec as P

HD = 128


EPSILON = 1e-05
NEG_FILL = -1e30


def route_slots(expert_ids, n_experts, capacity):
    seq_len, top_count = expert_ids.shape
    experts = jnp.arange(n_experts, dtype=jnp.int32)
    counts = jnp.sum((expert_ids[:, :, None] == experts[None, None, :]).astype(jnp.int32), axis=1)
    earlier = jnp.cumsum(counts, axis=0) - counts
    slot_rank = jnp.take_along_axis(earlier, expert_ids, axis=1)
    flat_index = expert_ids * capacity + slot_rank
    token_index = jnp.broadcast_to(
        jnp.arange(seq_len, dtype=jnp.int32)[:, None], (seq_len, top_count)
    )
    source = jnp.full((n_experts * capacity,), seq_len, jnp.int32)
    source = source.at[flat_index.reshape(-1)].set(token_index.reshape(-1))
    return (flat_index, source)


def rope_tables(seq_len, head_size):
    half_size = head_size // 2
    inverse = 10000.0 ** (-2.0 * jnp.arange(half_size, dtype=jnp.float32) / head_size)
    angles = jnp.arange(seq_len, dtype=jnp.float32)[:, None] * inverse[None, :]
    return (jnp.cos(angles)[:, None, :], jnp.sin(angles)[:, None, :])


def rotate(values, cosine, sine):
    half_size = values.shape[-1] // 2
    first = values[..., :half_size]
    second = values[..., half_size:]
    return jnp.concatenate(
        [first * cosine - second * sine, second * cosine + first * sine], axis=-1
    )


def rotate_back(grads, cosine, sine):
    half_size = grads.shape[-1] // 2
    first = grads[..., :half_size]
    second = grads[..., half_size:]
    return jnp.concatenate(
        [first * cosine + second * sine, second * cosine - first * sine], axis=-1
    )


def allowed_mask(segment, padding, row_start, row_count):
    row_index = row_start + jnp.arange(row_count, dtype=jnp.int32)
    col_index = jnp.arange(segment.shape[0], dtype=jnp.int32)
    same_doc = segment[:, None] == segment[None, :]
    causal = col_index[None, :] <= row_index[:, None]
    usable = (padding[None, :] == 1) | (col_index[None, :] == row_index[:, None])
    return same_doc & causal & usable


def norm_forward(values, gain):
    scale = lax.rsqrt(jnp.mean(values * values, axis=-1, keepdims=True) + EPSILON)
    return (values * scale * gain, scale)


def norm_backward(values, scale, gain, grads):
    unit = values * scale
    gain_grad = jnp.sum(grads * unit, axis=0)
    scaled = grads * gain
    return (scale * (scaled - unit * jnp.mean(scaled * unit, axis=-1, keepdims=True)), gain_grad)


def gather_rows(values):
    return lax.all_gather(values, "tp", axis=0, tiled=True)


def scatter_rows(values):
    return lax.psum_scatter(
        values.astype(jnp.bfloat16), "tp", scatter_dimension=0, tiled=True
    ).astype(jnp.float32)


def tp_totals(first, second):
    return lax.psum((first, second), "tp")


def shards(
    tokens,
    seg_ids,
    pad_mask,
    expert_ids,
    w_qkv,
    w_out,
    w_router,
    norm_gains,
    w_gate,
    w_up,
    w_down,
    cotangent,
):
    tp_rank = lax.axis_index("tp")
    fsdp_count = lax.axis_size("fsdp")
    local_rows, width = tokens.shape
    seq_len = seg_ids.shape[1]
    exp_local = w_gate.shape[0]
    ff_local = w_gate.shape[2]
    n_experts = exp_local * fsdp_count
    top_count = expert_ids.shape[1]
    capacity = (seq_len * top_count * 33 + 32 * n_experts - 1) // (32 * n_experts)
    head_cols = w_qkv.shape[2]
    heads_local = head_cols // HD
    block_rows = min(512, seq_len)
    n_blocks = seq_len // block_rows
    score_scale = HD ** (-0.5)

    def send_experts(buffer):
        return lax.all_to_all(buffer, "fsdp", split_axis=0, concat_axis=1, tiled=True)

    def return_experts(buffer):
        back = lax.all_to_all(buffer, "fsdp", split_axis=1, concat_axis=0, tiled=True)
        return back.reshape(n_experts * capacity, back.shape[2])

    qkv_full, out_full = (
        lax.all_gather(w_qkv, "fsdp", axis=1, tiled=True),
        lax.all_gather(w_out, "fsdp", axis=1, tiled=True),
    )
    router_full, gains_full = (
        lax.all_gather(w_router, ("fsdp", "tp"), axis=0, tiled=True),
        lax.all_gather(norm_gains, ("fsdp", "tp"), axis=1, tiled=True),
    )
    gains_wide = gains_full.astype(jnp.float32)
    col_start = tp_rank * head_cols
    gain_query = lax.dynamic_slice_in_dim(gains_wide[2], col_start, head_cols)
    gain_key = lax.dynamic_slice_in_dim(gains_wide[3], col_start, head_cols)
    segment = seg_ids[0]
    padding = pad_mask[0]
    cosine, sine = rope_tables(seq_len, HD)
    x_own = tokens.astype(jnp.float32)
    normed1, scale1 = norm_forward(x_own, gains_wide[0])
    rows1 = gather_rows(normed1.astype(jnp.bfloat16))
    projected = jnp.einsum("sd,cdh->csh", rows1, qkv_full, preferred_element_type=jnp.float32)
    query_raw = projected[0]
    key_raw = projected[1]
    square_q, square_k = tp_totals(
        jnp.sum(query_raw * query_raw, axis=-1), jnp.sum(key_raw * key_raw, axis=-1)
    )
    scale_q = lax.rsqrt(square_q / width + EPSILON)[:, None]
    scale_k = lax.rsqrt(square_k / width + EPSILON)[:, None]
    unit_q = query_raw * scale_q
    unit_k = key_raw * scale_k
    queries = rotate((unit_q * gain_query).reshape(seq_len, heads_local, HD), cosine, sine).astype(
        jnp.bfloat16
    )
    keys = rotate((unit_k * gain_key).reshape(seq_len, heads_local, HD), cosine, sine).astype(
        jnp.bfloat16
    )
    values = projected[2].astype(jnp.bfloat16).reshape(seq_len, heads_local, HD)
    block_starts = jnp.arange(n_blocks, dtype=jnp.int32) * block_rows

    def block_scores(start):
        raw_scores = (
            jnp.einsum("qhd,khd->hqk", queries, keys, preferred_element_type=jnp.float32)
            * score_scale
        )
        allowed = allowed_mask(segment, padding, start, block_rows)
        return (queries, jnp.where(allowed[None], raw_scores, NEG_FILL), allowed)

    def attend(start):
        query_block, scores, allowed = block_scores(start)
        peak = jnp.max(scores, axis=-1, keepdims=True)
        powered = jnp.exp(scores - peak)
        total = jnp.sum(powered, axis=-1, keepdims=True)
        probs_low = (powered / total).astype(jnp.bfloat16)
        mixed_block = jnp.einsum(
            "hqk,khd->qhd", probs_low, values, preferred_element_type=jnp.float32
        )
        return (
            mixed_block.reshape(block_rows, head_cols).astype(jnp.bfloat16),
            (peak + jnp.log(total))[..., 0],
        )

    mixed_blocks, log_sums = lax.map(attend, block_starts)
    mixed = mixed_blocks.reshape(seq_len, head_cols)
    hidden = x_own + scatter_rows(jnp.dot(mixed, out_full, preferred_element_type=jnp.float32))
    normed2, scale2 = norm_forward(hidden, gains_wide[1])
    own_normed2 = normed2.astype(jnp.bfloat16)
    rows2 = gather_rows(own_normed2)
    logits = jnp.dot(rows2, router_full, preferred_element_type=jnp.float32)
    router_probs = jax.nn.softmax(logits, axis=-1)
    gates = jnp.take_along_axis(router_probs, expert_ids, axis=1)
    flat_index, source = route_slots(expert_ids, n_experts, capacity)
    padded_rows = jnp.concatenate([rows2, jnp.zeros((1, width), jnp.bfloat16)], axis=0)
    received = send_experts(padded_rows[source].reshape(n_experts, capacity, width))
    w_pair = jnp.concatenate([w_gate, w_up], axis=2)
    pair_pre = jnp.einsum("erd,edf->erf", received, w_pair, preferred_element_type=jnp.float32)
    gate_pre = pair_pre[..., :ff_local]
    up_pre = pair_pre[..., ff_local:]
    sigmoid_gate = jax.nn.sigmoid(gate_pre)
    silu_gate = gate_pre * sigmoid_gate
    active = (silu_gate * up_pre).astype(jnp.bfloat16)
    expert_part = jnp.einsum(
        "erf,efd->erd", active, w_down, preferred_element_type=jnp.float32
    ).astype(jnp.bfloat16)
    returned = return_experts(expert_part)
    combined = jnp.zeros((seq_len, returned.shape[1]), jnp.float32)
    for pick_rank in range(top_count):
        combined = combined + gates[:, pick_rank : pick_rank + 1] * returned[
            flat_index[:, pick_rank]
        ].astype(jnp.float32)
    layer_out = (hidden + scatter_rows(combined)).astype(jnp.bfloat16)
    grad_rows = gather_rows(cotangent)
    grad_cols = grad_rows.astype(jnp.float32)
    partial_dots = jnp.stack(
        [
            jnp.sum(returned[flat_index[:, pick_rank]].astype(jnp.float32) * grad_cols, axis=-1)
            for pick_rank in range(top_count)
        ],
        axis=1,
    )
    gate_dots = lax.psum(partial_dots, "tp")
    expert_range = jnp.arange(n_experts, dtype=jnp.int32)
    chosen = jnp.sum(
        gate_dots[:, :, None]
        * (expert_ids[:, :, None] == expert_range[None, None, :]).astype(jnp.float32),
        axis=1,
    )
    weighted = jnp.sum(gates * gate_dots, axis=-1, keepdims=True)
    logit_grad = (router_probs * (chosen - weighted)).astype(jnp.bfloat16)
    own_logit_grad = lax.dynamic_slice_in_dim(logit_grad, tp_rank * local_rows, local_rows, 0)
    slot_gates = (
        jnp.zeros((n_experts * capacity,), jnp.float32)
        .at[flat_index.reshape(-1)]
        .set(gates.reshape(-1))
    )
    padded_grads = jnp.concatenate([grad_rows, jnp.zeros((1, width), jnp.bfloat16)], axis=0)
    slot_grads = (padded_grads[source].astype(jnp.float32) * slot_gates[:, None]).astype(
        jnp.bfloat16
    )
    grad_received = send_experts(slot_grads.reshape(n_experts, capacity, width))
    active_grad = jnp.einsum(
        "erd,efd->erf", grad_received, w_down, preferred_element_type=jnp.float32
    )
    gate_grad = (
        active_grad * up_pre * sigmoid_gate * (1.0 + gate_pre * (1.0 - sigmoid_gate))
    ).astype(jnp.bfloat16)
    up_grad = (active_grad * silu_gate).astype(jnp.bfloat16)
    pair_grad = jnp.concatenate([gate_grad, up_grad], axis=2)
    grad_down = jnp.einsum(
        "erf,erd->efd", active, grad_received, preferred_element_type=jnp.float32
    )
    grad_pair = jnp.einsum("erd,erf->edf", received, pair_grad, preferred_element_type=jnp.float32)
    grad_gate = grad_pair[..., :ff_local]
    grad_up = grad_pair[..., ff_local:]
    input_part = jnp.einsum(
        "erf,edf->erd", pair_grad, w_pair, preferred_element_type=jnp.float32
    ).astype(jnp.bfloat16)
    sent_back = return_experts(input_part)
    token_grad = jnp.zeros((seq_len, sent_back.shape[1]), jnp.float32)
    for pick_rank in range(top_count):
        token_grad = token_grad + sent_back[flat_index[:, pick_rank]].astype(jnp.float32)
    normed2_grad = scatter_rows(token_grad) + jnp.dot(
        own_logit_grad, router_full.T, preferred_element_type=jnp.float32
    )
    hidden_norm_grad, gain2_grad = norm_backward(hidden, scale2, gains_wide[1], normed2_grad)
    hidden_grad = cotangent.astype(jnp.float32) + hidden_norm_grad
    router_grad = jnp.dot(own_normed2.T, own_logit_grad, preferred_element_type=jnp.float32)
    hidden_rows = gather_rows(hidden_grad.astype(jnp.bfloat16))
    grad_out_full = jnp.dot(mixed.T, hidden_rows, preferred_element_type=jnp.float32)
    mixed_grad = (
        jnp.dot(hidden_rows, out_full.T, preferred_element_type=jnp.float32)
        .astype(jnp.bfloat16)
        .reshape(seq_len, heads_local, HD)
    )

    def attend_back(carried, pieces):
        key_acc, value_acc = carried
        start, log_sum = pieces
        query_block, scores, allowed = block_scores(start)
        probs = jnp.where(allowed[None], jnp.exp(scores - log_sum[:, :, None]), 0.0)
        prob_grad = jnp.einsum(
            "qhd,khd->hqk", mixed_grad, values, preferred_element_type=jnp.float32
        )
        delta = jnp.sum(probs * prob_grad, axis=-1, keepdims=True)
        score_grad = (probs * (prob_grad - delta)).astype(jnp.bfloat16)
        query_block_grad = (
            jnp.einsum("hqk,khd->qhd", score_grad, keys, preferred_element_type=jnp.float32)
            * score_scale
        )
        key_acc = (
            key_acc
            + jnp.einsum(
                "hqk,qhd->khd", score_grad, query_block, preferred_element_type=jnp.float32
            )
            * score_scale
        )
        value_acc = value_acc + jnp.einsum(
            "hqk,qhd->khd",
            probs.astype(jnp.bfloat16),
            mixed_grad,
            preferred_element_type=jnp.float32,
        )
        return ((key_acc, value_acc), query_block_grad)

    zero_heads = jnp.zeros((seq_len, heads_local, HD), jnp.float32)
    (key_grad, value_grad), query_blocks = lax.scan(
        attend_back, (zero_heads, zero_heads), (block_starts, log_sums)
    )
    query_grad = query_blocks.reshape(seq_len, heads_local, HD)
    query_norm_grad = rotate_back(query_grad, cosine, sine).reshape(seq_len, head_cols)
    key_norm_grad = rotate_back(key_grad, cosine, sine).reshape(seq_len, head_cols)
    gain_query_grad = jnp.sum(query_norm_grad * unit_q, axis=0)
    gain_key_grad = jnp.sum(key_norm_grad * unit_k, axis=0)
    scaled_q = query_norm_grad * gain_query
    scaled_k = key_norm_grad * gain_key
    inner_q, inner_k = tp_totals(
        jnp.sum(scaled_q * unit_q, axis=-1), jnp.sum(scaled_k * unit_k, axis=-1)
    )
    query_raw_grad = scale_q * (scaled_q - unit_q * (inner_q / width)[:, None])
    key_raw_grad = scale_k * (scaled_k - unit_k * (inner_k / width)[:, None])
    qkv_grad = jnp.stack(
        [query_raw_grad, key_raw_grad, value_grad.reshape(seq_len, head_cols)]
    ).astype(jnp.bfloat16)
    grad_qkv_full = jnp.einsum("sd,csh->cdh", rows1, qkv_grad, preferred_element_type=jnp.float32)
    normed1_part = jnp.einsum("csh,cdh->sd", qkv_grad, qkv_full, preferred_element_type=jnp.float32)
    normed1_grad = scatter_rows(normed1_part)
    input_norm_grad, gain1_grad = norm_backward(x_own, scale1, gains_wide[0], normed1_grad)
    input_grad = hidden_grad + input_norm_grad
    zero_width = jnp.zeros((width,), jnp.float32)
    gains_grad = jnp.stack(
        [
            gain1_grad,
            gain2_grad,
            lax.dynamic_update_slice_in_dim(zero_width, gain_query_grad, col_start, 0),
            lax.dynamic_update_slice_in_dim(zero_width, gain_key_grad, col_start, 0),
        ]
    )
    grad_qkv, grad_out = (
        lax.psum_scatter(
            grad_qkv_full.astype(jnp.bfloat16), "fsdp", scatter_dimension=1, tiled=True
        ).astype(jnp.float32),
        lax.psum_scatter(
            grad_out_full.astype(jnp.bfloat16), "fsdp", scatter_dimension=1, tiled=True
        ).astype(jnp.float32),
    )
    grad_router, grad_gains = (
        lax.psum_scatter(router_grad, ("fsdp", "tp"), scatter_dimension=0, tiled=True),
        lax.psum_scatter(gains_grad, ("fsdp", "tp"), scatter_dimension=1, tiled=True),
    )
    return (
        layer_out,
        input_grad,
        grad_qkv,
        grad_out,
        grad_router,
        grad_gains,
        grad_gate,
        grad_up,
        grad_down,
    )


GRID = (4, 2, 2, 2)
LANES = 128
CONTRACT_LAST = (((1,), (1,)), ((), ()))


def permutation(target):
    def place(z, x, y, c):
        return ((z * GRID[1] + x) * GRID[2] + y) * GRID[3] + c

    return [
        (place(*at), place(*target(*at))) for at in itertools.product(*(range(n) for n in GRID))
    ]


SWAP_CORE = permutation(lambda z, x, y, c: (z, x, y, 1 - c))
SWAP_X = permutation(lambda z, x, y, c: (z, 1 - x, y, c))
SWAP_Y = permutation(lambda z, x, y, c: (z, x, 1 - y, c))
SWAP_FIRST = permutation(lambda z, x, y, c: (z, 1 - x, y, c) if c == 0 else (z, x, 1 - y, c))
SWAP_SECOND = permutation(lambda z, x, y, c: (z, x, 1 - y, c) if c == 0 else (z, 1 - x, y, c))
SWAP_Z = [permutation(lambda z, x, y, c, b=b: (z ^ b, x, y, c)) for b in (1, 2)]


def shift_z(steps):
    return permutation(lambda z, x, y, c: ((z + steps) % GRID[0], x, y, c))


def send(values, pairs):
    return lax.ppermute(values, ("fsdp", "tp"), pairs)


def add_low(*terms):
    return sum(term.astype(jnp.float32) for term in terms).astype(jnp.bfloat16)


def gather_rounds(own):
    rounds = []
    column = own
    for step in range(GRID[0]):
        if step:
            column = send(column, shift_z(1))
        half = jnp.concatenate([column, send(column, SWAP_FIRST)], axis=0)
        plane = jnp.concatenate([half, send(half, SWAP_SECOND)], axis=0)
        rounds.append((plane, send(plane, SWAP_CORE)))
    return rounds


def scatter_rounds(rounds):
    total = None
    for step, (plane, other) in enumerate(rounds):
        rows = plane.shape[0] // 4
        back = send(other, SWAP_CORE)
        second = send(add_low(plane[2 * rows :], back[2 * rows :]), SWAP_SECOND)
        first = send(
            add_low(plane[rows : 2 * rows], back[rows : 2 * rows], second[rows:]), SWAP_FIRST
        )
        mine = [plane[:rows], back[:rows], second[:rows], first]
        if step:
            mine = [send(add_low(*mine), shift_z(-step))]
        mine = sum(term.astype(jnp.float32) for term in mine)
        total = mine if total is None else total + mine
    return total


def scatter_small(rounds):
    plane = jnp.stack([pair[0] for pair in rounds])
    other = jnp.stack([pair[1] for pair in rounds])
    rows = plane.shape[-1] // 4
    plane = plane + send(other, SWAP_CORE)
    half = plane[..., : 2 * rows] + send(plane[..., 2 * rows :], SWAP_SECOND)
    mine = half[..., :rows] + send(half[..., rows:], SWAP_FIRST)
    return mine[0] + sum(send(mine[step], shift_z(-step)) for step in range(1, GRID[0]))


def butterfly_sum(values):
    for pairs in (SWAP_CORE, SWAP_Y, SWAP_X, *SWAP_Z):
        values = values + send(values, pairs)
    return values


def tp_gather(own):
    is_core1 = lax.axis_index("tp") % 2 == 1
    is_y1 = lax.axis_index("tp") >= 2
    far = send(own, SWAP_Y)
    mine = jnp.stack([jnp.where(is_y1, far, own), jnp.where(is_y1, own, far)])
    theirs = send(mine, SWAP_CORE)
    both = jnp.stack(
        [jnp.where(is_core1, theirs, mine), jnp.where(is_core1, mine, theirs)], axis=1
    )
    return both.reshape(4 * own.shape[0], *own.shape[1:])


def tp_scatter(values):
    core = lax.axis_index("tp") % 2
    side = lax.axis_index("tp") // 2
    rows = values.shape[0] // 4
    blocks = values.astype(jnp.bfloat16).reshape(2, 2, rows, values.shape[1])
    theirs = lax.dynamic_index_in_dim(blocks, 1 - core, 1, keepdims=False)
    mine = lax.dynamic_index_in_dim(blocks, core, 1, keepdims=False)
    back = send(theirs, SWAP_CORE)

    def at(pair, which):
        return lax.dynamic_index_in_dim(pair, which, 0, keepdims=False)

    far = send(add_low(at(mine, 1 - side), at(back, 1 - side)), SWAP_Y)
    return sum(term.astype(jnp.float32) for term in (at(mine, side), at(back, side), far))


def expert_kernel(
    rows_ref,
    grads_ref,
    router_ref,
    place_ref,
    gate_ref,
    up_ref,
    down_ref,
    route_ref,
    active_ref,
    hidden_ref,
    dots_ref,
    *,
    n_experts,
):
    exp_local, width, units = gate_ref.shape
    rows = rows_ref[...]
    grads = grads_ref[:, :width]
    named = grads_ref[:, width:].astype(jnp.float32)
    lane = lax.broadcasted_iota(jnp.int32, (1, LANES), 1)
    logits = jnp.dot(rows, router_ref[...], preferred_element_type=jnp.float32)
    logits = jnp.where(lane < n_experts, logits, NEG_FILL)
    powered = jnp.exp(logits - jnp.max(logits, axis=-1, keepdims=True))
    gates = powered / jnp.sum(powered, axis=-1, keepdims=True) * named
    route = None
    dots = jnp.zeros(logits.shape, jnp.float32)
    for expert in range(exp_local):
        place = place_ref[expert : expert + 1, :]
        gate = jnp.sum(gates * place, axis=-1, keepdims=True)
        gate_pre = jnp.dot(rows, gate_ref[expert], preferred_element_type=jnp.float32)
        up_pre = jnp.dot(rows, up_ref[expert], preferred_element_type=jnp.float32)
        y_down = lax.dot_general(
            grads, down_ref[expert], CONTRACT_LAST, preferred_element_type=jnp.float32
        )
        sigmoid = 1.0 / (1.0 + jnp.exp(-gate_pre))
        silu = gate_pre * sigmoid
        active = silu * up_pre
        dots = dots + jnp.sum(active * y_down, axis=-1, keepdims=True) * place
        active_ref[:, expert * units : (expert + 1) * units] = (active * gate).astype(jnp.bfloat16)
        active_grad = y_down * gate
        gate_grad = (active_grad * up_pre * sigmoid * (1.0 + gate_pre * (1.0 - sigmoid))).astype(
            jnp.bfloat16
        )
        up_grad = (active_grad * silu).astype(jnp.bfloat16)
        hidden_ref[:, expert * units : (expert + 1) * units] = gate_grad
        hidden_ref[:, (exp_local + expert) * units : (exp_local + expert + 1) * units] = up_grad
        part = lax.dot_general(
            gate_grad, gate_ref[expert], CONTRACT_LAST, preferred_element_type=jnp.float32
        ) + lax.dot_general(
            up_grad, up_ref[expert], CONTRACT_LAST, preferred_element_type=jnp.float32
        )
        route = part if route is None else route + part
    route_ref[...] = route.astype(jnp.bfloat16)
    dots_ref[...] = jnp.transpose(dots)[:n_experts]


def expert_rows(rows, grads, router, place, w_gate, w_up, w_down, n_experts):
    count, width = rows.shape
    exp_local, _, units = w_gate.shape
    flops = 2 * count * width * units * exp_local * 5
    moved = 2 * (3 * rows.size + 3 * w_gate.size + 3 * count * exp_local * units)
    return pl.pallas_call(
        functools.partial(expert_kernel, n_experts=n_experts),
        out_shape=[
            jax.ShapeDtypeStruct((count, width), jnp.bfloat16),
            jax.ShapeDtypeStruct((count, exp_local * units), jnp.bfloat16),
            jax.ShapeDtypeStruct((count, 2 * exp_local * units), jnp.bfloat16),
            jax.ShapeDtypeStruct((n_experts, count), jnp.float32),
        ],
        cost_estimate=pl.CostEstimate(
            flops=flops, bytes_accessed=moved, transcendentals=count * units * exp_local
        ),
        compiler_params=pltpu.CompilerParams(vmem_limit_bytes=40 * 1024 * 1024),
        name="expert_rows",
    )(rows, grads, router, place, w_gate, w_up, w_down)


def dense_shards(
    tokens,
    seg_ids,
    pad_mask,
    expert_ids,
    w_qkv,
    w_out,
    w_router,
    norm_gains,
    w_gate,
    w_up,
    w_down,
    cotangent,
):
    fsdp_rank = lax.axis_index("fsdp")
    tp_rank = lax.axis_index("tp")
    fsdp_count = lax.axis_size("fsdp")
    tp_count = lax.axis_size("tp")
    local_rows, width = tokens.shape
    seq_len = seg_ids.shape[1]
    exp_local, _, ff_local = w_gate.shape
    n_experts = exp_local * fsdp_count
    head_cols = w_qkv.shape[2]
    heads_local = head_cols // HD
    score_scale = HD ** (-0.5)
    own_start = tp_rank * local_rows
    small_cols = norm_gains.shape[1]
    small_start = (fsdp_rank * tp_count + tp_rank) * small_cols

    def own_rows(values):
        return lax.dynamic_slice_in_dim(values, own_start, local_rows, 0)

    rows_x = tp_gather(tokens).astype(jnp.float32)
    qkv_full = lax.all_gather(w_qkv, "fsdp", axis=1, tiled=True)
    out_full = lax.all_gather(w_out, "fsdp", axis=1, tiled=True)
    small_own = jnp.concatenate([w_router.T, norm_gains], axis=0)
    small_full = butterfly_sum(
        lax.dynamic_update_slice_in_dim(
            jnp.zeros((n_experts + 4, width), jnp.bfloat16), small_own, small_start, 1
        )
    )
    router_full = small_full[:n_experts].T
    gains_wide = small_full[n_experts:].astype(jnp.float32)
    own_ids = own_rows(expert_ids)
    expert_range = jnp.arange(n_experts, dtype=jnp.int32)
    named = (own_ids[:, :, None] == expert_range[None, None, :]).any(axis=1)
    named_wide = jnp.pad(named.astype(jnp.bfloat16), ((0, 0), (0, LANES - n_experts)))
    grad_rounds = gather_rounds(jnp.concatenate([cotangent, named_wide], axis=1))

    col_start = tp_rank * head_cols
    gain_query = lax.dynamic_slice_in_dim(gains_wide[2], col_start, head_cols)
    gain_key = lax.dynamic_slice_in_dim(gains_wide[3], col_start, head_cols)
    cosine, sine = rope_tables(seq_len, HD)
    x_own = tokens.astype(jnp.float32)
    normed1, scale1 = norm_forward(rows_x, gains_wide[0])
    rows1 = normed1.astype(jnp.bfloat16)
    projected = jnp.einsum("sd,cdh->csh", rows1, qkv_full, preferred_element_type=jnp.float32)
    query_raw = projected[0]
    key_raw = projected[1]
    square_q, square_k = tp_totals(
        jnp.sum(query_raw * query_raw, axis=-1), jnp.sum(key_raw * key_raw, axis=-1)
    )
    scale_q = lax.rsqrt(square_q / width + EPSILON)[:, None]
    scale_k = lax.rsqrt(square_k / width + EPSILON)[:, None]
    unit_q = query_raw * scale_q
    unit_k = key_raw * scale_k
    queries = rotate((unit_q * gain_query).reshape(seq_len, heads_local, HD), cosine, sine).astype(
        jnp.bfloat16
    )
    keys = rotate((unit_k * gain_key).reshape(seq_len, heads_local, HD), cosine, sine).astype(
        jnp.bfloat16
    )
    values = projected[2].astype(jnp.bfloat16).reshape(seq_len, heads_local, HD)
    raw_scores = (
        jnp.einsum("qhd,khd->hqk", queries, keys, preferred_element_type=jnp.float32) * score_scale
    )
    allowed = allowed_mask(seg_ids[0], pad_mask[0], 0, seq_len)
    scores = jnp.where(allowed[None], raw_scores, NEG_FILL)
    powered = jnp.exp(scores - jnp.max(scores, axis=-1, keepdims=True))
    probs = powered / jnp.sum(powered, axis=-1, keepdims=True)
    probs_low = probs.astype(jnp.bfloat16)
    mixed = (
        jnp.einsum("hqk,khd->qhd", probs_low, values, preferred_element_type=jnp.float32)
        .reshape(seq_len, head_cols)
        .astype(jnp.bfloat16)
    )
    hidden = x_own + tp_scatter(jnp.dot(mixed, out_full, preferred_element_type=jnp.float32))
    normed2, scale2 = norm_forward(hidden, gains_wide[1])
    own_normed2 = normed2.astype(jnp.bfloat16)
    row_rounds = gather_rounds(own_normed2)

    router_wide = jnp.pad(router_full, ((0, 0), (0, LANES - n_experts)))
    place = (
        jnp.arange(LANES)[None, :] == fsdp_rank * exp_local + jnp.arange(exp_local)[:, None]
    ).astype(jnp.float32)
    results = [
        [
            expert_rows(rows, grads, router_wide, place, w_gate, w_up, w_down, n_experts)
            for rows, grads in zip(row_pair, grad_pair)
        ]
        for row_pair, grad_pair in zip(row_rounds, grad_rounds)
    ]
    token_grad = scatter_rounds([(mine[0], other[0]) for mine, other in results])
    own_dots = scatter_small([(mine[3], other[3]) for mine, other in results]).T

    logits = jnp.dot(own_normed2, router_full, preferred_element_type=jnp.float32)
    router_probs = jax.nn.softmax(logits, axis=-1)
    own_gates = jnp.where(named, router_probs, 0.0)
    chosen = jnp.where(named, own_dots, 0.0)
    weighted = jnp.sum(own_gates * chosen, axis=-1, keepdims=True)
    own_logit_grad = (router_probs * (chosen - weighted)).astype(jnp.bfloat16)

    normed2_grad = token_grad + jnp.dot(
        own_logit_grad, router_full.T, preferred_element_type=jnp.float32
    )
    hidden_norm_grad, gain2_grad = norm_backward(hidden, scale2, gains_wide[1], normed2_grad)
    hidden_grad = cotangent.astype(jnp.float32) + hidden_norm_grad
    hidden_rows = tp_gather(hidden_grad.astype(jnp.bfloat16))

    actives, _ = lax.optimization_barrier(([[half[1] for half in pair] for pair in results], hidden_grad))
    down_rows = w_down.reshape(exp_local * ff_local, width)
    combined = scatter_rounds(
        [
            [
                jnp.dot(active, down_rows, preferred_element_type=jnp.float32).astype(jnp.bfloat16)
                for active in pair
            ]
            for pair in actives
        ]
    )
    layer_out = (hidden + combined).astype(jnp.bfloat16)

    all_n2 = jnp.concatenate([half for pair in row_rounds for half in pair], axis=0)
    all_y = jnp.concatenate([half[:, :width] for pair in grad_rounds for half in pair], axis=0)
    all_active = jnp.concatenate([half[1] for pair in results for half in pair], axis=0)
    all_hidden = jnp.concatenate([half[2] for pair in results for half in pair], axis=0)

    def pair_dots(left, right):
        return lax.dot_general(
            left, right, (((0,), (0,)), ((), ())), preferred_element_type=jnp.float32
        )

    def hidden_piece(index):
        return all_hidden[:, index * ff_local : (index + 1) * ff_local]

    grad_down = pair_dots(all_active, all_y).reshape(exp_local, ff_local, width)
    grad_gate = jnp.stack([pair_dots(all_n2, hidden_piece(e)) for e in range(exp_local)])
    grad_up = jnp.stack([pair_dots(all_n2, hidden_piece(exp_local + e)) for e in range(exp_local)])

    grad_out_full = jnp.dot(mixed.T, hidden_rows, preferred_element_type=jnp.float32)
    mixed_grad = (
        jnp.dot(hidden_rows, out_full.T, preferred_element_type=jnp.float32)
        .astype(jnp.bfloat16)
        .reshape(seq_len, heads_local, HD)
    )
    prob_grad = jnp.einsum("qhd,khd->hqk", mixed_grad, values, preferred_element_type=jnp.float32)
    delta = jnp.sum(probs * prob_grad, axis=-1, keepdims=True)
    score_grad = (probs * (prob_grad - delta)).astype(jnp.bfloat16)
    query_grad = (
        jnp.einsum("hqk,khd->qhd", score_grad, keys, preferred_element_type=jnp.float32)
        * score_scale
    )
    key_grad = (
        jnp.einsum("hqk,qhd->khd", score_grad, queries, preferred_element_type=jnp.float32)
        * score_scale
    )
    value_grad = jnp.einsum(
        "hqk,qhd->khd", probs_low, mixed_grad, preferred_element_type=jnp.float32
    )
    query_norm_grad = rotate_back(query_grad, cosine, sine).reshape(seq_len, head_cols)
    key_norm_grad = rotate_back(key_grad, cosine, sine).reshape(seq_len, head_cols)
    gain_query_grad = jnp.sum(query_norm_grad * unit_q, axis=0)
    gain_key_grad = jnp.sum(key_norm_grad * unit_k, axis=0)
    scaled_q = query_norm_grad * gain_query
    scaled_k = key_norm_grad * gain_key
    inner_q, inner_k = tp_totals(
        jnp.sum(scaled_q * unit_q, axis=-1), jnp.sum(scaled_k * unit_k, axis=-1)
    )
    query_raw_grad = scale_q * (scaled_q - unit_q * (inner_q / width)[:, None])
    key_raw_grad = scale_k * (scaled_k - unit_k * (inner_k / width)[:, None])
    qkv_grad = jnp.stack(
        [query_raw_grad, key_raw_grad, value_grad.reshape(seq_len, head_cols)]
    ).astype(jnp.bfloat16)
    grad_qkv_full = jnp.einsum("sd,csh->cdh", rows1, qkv_grad, preferred_element_type=jnp.float32)
    normed1_part = jnp.einsum("csh,cdh->sd", qkv_grad, qkv_full, preferred_element_type=jnp.float32)
    normed1_grad = tp_scatter(normed1_part)
    gain1_grad = jnp.sum(normed1_part * (rows_x * scale1), axis=0)
    input_norm_grad, _ = norm_backward(x_own, own_rows(scale1), gains_wide[0], normed1_grad)
    input_grad = hidden_grad + input_norm_grad
    zero_width = jnp.zeros((width,), jnp.float32)
    gains_grad = jnp.stack(
        [
            gain1_grad,
            gain2_grad,
            lax.dynamic_update_slice_in_dim(zero_width, gain_query_grad, col_start, 0),
            lax.dynamic_update_slice_in_dim(zero_width, gain_key_grad, col_start, 0),
        ]
    )
    router_part = pair_dots(own_logit_grad, own_normed2)
    small_grad = lax.dynamic_slice_in_dim(
        butterfly_sum(jnp.concatenate([router_part, gains_grad], axis=0)),
        small_start,
        small_cols,
        1,
    )
    grad_router = small_grad[:n_experts].T
    grad_gains = small_grad[n_experts:]
    grad_qkv = lax.psum_scatter(
        grad_qkv_full.astype(jnp.bfloat16), "fsdp", scatter_dimension=1, tiled=True
    ).astype(jnp.float32)
    grad_out = lax.psum_scatter(
        grad_out_full.astype(jnp.bfloat16), "fsdp", scatter_dimension=1, tiled=True
    ).astype(jnp.float32)
    return (
        layer_out,
        input_grad,
        grad_qkv,
        grad_out,
        grad_router,
        grad_gains,
        grad_gate,
        grad_up,
        grad_down,
    )


def pick_shards(*arguments):
    fsdp_count, tp_count = lax.axis_size("fsdp"), lax.axis_size("tp")
    n_experts = arguments[8].shape[0] * fsdp_count
    top_count = arguments[3].shape[1]
    fits = (fsdp_count, tp_count) == (GRID[0] * GRID[1], GRID[2] * GRID[3])
    body = dense_shards if fits and n_experts <= 2 * top_count else shards
    return body(*arguments)


def solution(mesh):
    placed = (
        P(("fsdp", "tp"), None),
        P("fsdp", None),
        P("fsdp", None),
        P("fsdp", None),
        P(None, "fsdp", "tp"),
        P("tp", "fsdp"),
        P(("fsdp", "tp"), None),
        P(None, ("fsdp", "tp")),
        P("fsdp", None, "tp"),
        P("fsdp", None, "tp"),
        P("fsdp", "tp", None),
        P(("fsdp", "tp"), None),
    )
    return jax.shard_map(
        pick_shards,
        mesh=mesh,
        in_specs=placed,
        out_specs=(
            P(("fsdp", "tp"), None),
            P(("fsdp", "tp"), None),
            P(None, "fsdp", "tp"),
            P("tp", "fsdp"),
            P(("fsdp", "tp"), None),
            P(None, ("fsdp", "tp")),
            P("fsdp", None, "tp"),
            P("fsdp", None, "tp"),
            P("fsdp", "tp", None),
        ),
        check_vma=False,
    )
```

```python
import functools
import itertools

import jax
import jax.numpy as jnp
from jax import lax
from jax.experimental import pallas as pl
from jax.experimental.pallas import tpu as pltpu
from jax.sharding import Mesh
from jax.sharding import PartitionSpec as P

HD = 128


EPSILON = 1e-05
NEG_FILL = -1e30


def route_slots(expert_ids, n_experts, capacity):
    seq_len, top_count = expert_ids.shape
    experts = jnp.arange(n_experts, dtype=jnp.int32)
    counts = jnp.sum((expert_ids[:, :, None] == experts[None, None, :]).astype(jnp.int32), axis=1)
    earlier = jnp.cumsum(counts, axis=0) - counts
    slot_rank = jnp.take_along_axis(earlier, expert_ids, axis=1)
    flat_index = expert_ids * capacity + slot_rank
    token_index = jnp.broadcast_to(
        jnp.arange(seq_len, dtype=jnp.int32)[:, None], (seq_len, top_count)
    )
    source = jnp.full((n_experts * capacity,), seq_len, jnp.int32)
    source = source.at[flat_index.reshape(-1)].set(token_index.reshape(-1))
    return (flat_index, source)


def rope_tables(seq_len, head_size):
    half_size = head_size // 2
    inverse = 10000.0 ** (-2.0 * jnp.arange(half_size, dtype=jnp.float32) / head_size)
    angles = jnp.arange(seq_len, dtype=jnp.float32)[:, None] * inverse[None, :]
    return (jnp.cos(angles)[:, None, :], jnp.sin(angles)[:, None, :])


def rotate(values, cosine, sine):
    half_size = values.shape[-1] // 2
    first = values[..., :half_size]
    second = values[..., half_size:]
    return jnp.concatenate(
        [first * cosine - second * sine, second * cosine + first * sine], axis=-1
    )


def rotate_back(grads, cosine, sine):
    half_size = grads.shape[-1] // 2
    first = grads[..., :half_size]
    second = grads[..., half_size:]
    return jnp.concatenate(
        [first * cosine + second * sine, second * cosine - first * sine], axis=-1
    )


def allowed_mask(segment, padding, row_start, row_count):
    row_index = row_start + jnp.arange(row_count, dtype=jnp.int32)
    col_index = jnp.arange(segment.shape[0], dtype=jnp.int32)
    same_doc = segment[:, None] == segment[None, :]
    causal = col_index[None, :] <= row_index[:, None]
    usable = (padding[None, :] == 1) | (col_index[None, :] == row_index[:, None])
    return same_doc & causal & usable


def norm_forward(values, gain):
    scale = lax.rsqrt(jnp.mean(values * values, axis=-1, keepdims=True) + EPSILON)
    return (values * scale * gain, scale)


def norm_backward(values, scale, gain, grads):
    unit = values * scale
    gain_grad = jnp.sum(grads * unit, axis=0)
    scaled = grads * gain
    return (scale * (scaled - unit * jnp.mean(scaled * unit, axis=-1, keepdims=True)), gain_grad)


def gather_rows(values):
    return lax.all_gather(values, "tp", axis=0, tiled=True)


def scatter_rows(values):
    return lax.psum_scatter(
        values.astype(jnp.bfloat16), "tp", scatter_dimension=0, tiled=True
    ).astype(jnp.float32)


def tp_totals(first, second):
    return lax.psum((first, second), "tp")


def shards(
    tokens,
    seg_ids,
    pad_mask,
    expert_ids,
    w_qkv,
    w_out,
    w_router,
    norm_gains,
    w_gate,
    w_up,
    w_down,
    cotangent,
):
    tp_rank = lax.axis_index("tp")
    fsdp_count = lax.axis_size("fsdp")
    local_rows, width = tokens.shape
    seq_len = seg_ids.shape[1]
    exp_local = w_gate.shape[0]
    ff_local = w_gate.shape[2]
    n_experts = exp_local * fsdp_count
    top_count = expert_ids.shape[1]
    capacity = (seq_len * top_count * 33 + 32 * n_experts - 1) // (32 * n_experts)
    head_cols = w_qkv.shape[2]
    heads_local = head_cols // HD
    block_rows = min(512, seq_len)
    n_blocks = seq_len // block_rows
    score_scale = HD ** (-0.5)

    def send_experts(buffer):
        return lax.all_to_all(buffer, "fsdp", split_axis=0, concat_axis=1, tiled=True)

    def return_experts(buffer):
        back = lax.all_to_all(buffer, "fsdp", split_axis=1, concat_axis=0, tiled=True)
        return back.reshape(n_experts * capacity, back.shape[2])

    qkv_full, out_full = (
        lax.all_gather(w_qkv, "fsdp", axis=1, tiled=True),
        lax.all_gather(w_out, "fsdp", axis=1, tiled=True),
    )
    router_full, gains_full = (
        lax.all_gather(w_router, ("fsdp", "tp"), axis=0, tiled=True),
        lax.all_gather(norm_gains, ("fsdp", "tp"), axis=1, tiled=True),
    )
    gains_wide = gains_full.astype(jnp.float32)
    col_start = tp_rank * head_cols
    gain_query = lax.dynamic_slice_in_dim(gains_wide[2], col_start, head_cols)
    gain_key = lax.dynamic_slice_in_dim(gains_wide[3], col_start, head_cols)
    segment = seg_ids[0]
    padding = pad_mask[0]
    cosine, sine = rope_tables(seq_len, HD)
    x_own = tokens.astype(jnp.float32)
    normed1, scale1 = norm_forward(x_own, gains_wide[0])
    rows1 = gather_rows(normed1.astype(jnp.bfloat16))
    projected = jnp.einsum("sd,cdh->csh", rows1, qkv_full, preferred_element_type=jnp.float32)
    query_raw = projected[0]
    key_raw = projected[1]
    square_q, square_k = tp_totals(
        jnp.sum(query_raw * query_raw, axis=-1), jnp.sum(key_raw * key_raw, axis=-1)
    )
    scale_q = lax.rsqrt(square_q / width + EPSILON)[:, None]
    scale_k = lax.rsqrt(square_k / width + EPSILON)[:, None]
    unit_q = query_raw * scale_q
    unit_k = key_raw * scale_k
    queries = rotate((unit_q * gain_query).reshape(seq_len, heads_local, HD), cosine, sine).astype(
        jnp.bfloat16
    )
    keys = rotate((unit_k * gain_key).reshape(seq_len, heads_local, HD), cosine, sine).astype(
        jnp.bfloat16
    )
    values = projected[2].astype(jnp.bfloat16).reshape(seq_len, heads_local, HD)
    block_starts = jnp.arange(n_blocks, dtype=jnp.int32) * block_rows

    def block_scores(start):
        raw_scores = (
            jnp.einsum("qhd,khd->hqk", queries, keys, preferred_element_type=jnp.float32)
            * score_scale
        )
        allowed = allowed_mask(segment, padding, start, block_rows)
        return (queries, jnp.where(allowed[None], raw_scores, NEG_FILL), allowed)

    def attend(start):
        query_block, scores, allowed = block_scores(start)
        peak = jnp.max(scores, axis=-1, keepdims=True)
        powered = jnp.exp(scores - peak)
        total = jnp.sum(powered, axis=-1, keepdims=True)
        probs_low = (powered / total).astype(jnp.bfloat16)
        mixed_block = jnp.einsum(
            "hqk,khd->qhd", probs_low, values, preferred_element_type=jnp.float32
        )
        return (
            mixed_block.reshape(block_rows, head_cols).astype(jnp.bfloat16),
            (peak + jnp.log(total))[..., 0],
        )

    mixed_blocks, log_sums = lax.map(attend, block_starts)
    mixed = mixed_blocks.reshape(seq_len, head_cols)
    hidden = x_own + scatter_rows(jnp.dot(mixed, out_full, preferred_element_type=jnp.float32))
    normed2, scale2 = norm_forward(hidden, gains_wide[1])
    own_normed2 = normed2.astype(jnp.bfloat16)
    rows2 = gather_rows(own_normed2)
    logits = jnp.dot(rows2, router_full, preferred_element_type=jnp.float32)
    router_probs = jax.nn.softmax(logits, axis=-1)
    gates = jnp.take_along_axis(router_probs, expert_ids, axis=1)
    flat_index, source = route_slots(expert_ids, n_experts, capacity)
    padded_rows = jnp.concatenate([rows2, jnp.zeros((1, width), jnp.bfloat16)], axis=0)
    received = send_experts(padded_rows[source].reshape(n_experts, capacity, width))
    w_pair = jnp.concatenate([w_gate, w_up], axis=2)
    pair_pre = jnp.einsum("erd,edf->erf", received, w_pair, preferred_element_type=jnp.float32)
    gate_pre = pair_pre[..., :ff_local]
    up_pre = pair_pre[..., ff_local:]
    sigmoid_gate = jax.nn.sigmoid(gate_pre)
    silu_gate = gate_pre * sigmoid_gate
    active = (silu_gate * up_pre).astype(jnp.bfloat16)
    expert_part = jnp.einsum(
        "erf,efd->erd", active, w_down, preferred_element_type=jnp.float32
    ).astype(jnp.bfloat16)
    returned = return_experts(expert_part)
    combined = jnp.zeros((seq_len, returned.shape[1]), jnp.float32)
    for pick_rank in range(top_count):
        combined = combined + gates[:, pick_rank : pick_rank + 1] * returned[
            flat_index[:, pick_rank]
        ].astype(jnp.float32)
    layer_out = (hidden + scatter_rows(combined)).astype(jnp.bfloat16)
    grad_rows = gather_rows(cotangent)
    grad_cols = grad_rows.astype(jnp.float32)
    partial_dots = jnp.stack(
        [
            jnp.sum(returned[flat_index[:, pick_rank]].astype(jnp.float32) * grad_cols, axis=-1)
            for pick_rank in range(top_count)
        ],
        axis=1,
    )
    gate_dots = lax.psum(partial_dots, "tp")
    expert_range = jnp.arange(n_experts, dtype=jnp.int32)
    chosen = jnp.sum(
        gate_dots[:, :, None]
        * (expert_ids[:, :, None] == expert_range[None, None, :]).astype(jnp.float32),
        axis=1,
    )
    weighted = jnp.sum(gates * gate_dots, axis=-1, keepdims=True)
    logit_grad = (router_probs * (chosen - weighted)).astype(jnp.bfloat16)
    own_logit_grad = lax.dynamic_slice_in_dim(logit_grad, tp_rank * local_rows, local_rows, 0)
    slot_gates = (
        jnp.zeros((n_experts * capacity,), jnp.float32)
        .at[flat_index.reshape(-1)]
        .set(gates.reshape(-1))
    )
    padded_grads = jnp.concatenate([grad_rows, jnp.zeros((1, width), jnp.bfloat16)], axis=0)
    slot_grads = (padded_grads[source].astype(jnp.float32) * slot_gates[:, None]).astype(
        jnp.bfloat16
    )
    grad_received = send_experts(slot_grads.reshape(n_experts, capacity, width))
    active_grad = jnp.einsum(
        "erd,efd->erf", grad_received, w_down, preferred_element_type=jnp.float32
    )
    gate_grad = (
        active_grad * up_pre * sigmoid_gate * (1.0 + gate_pre * (1.0 - sigmoid_gate))
    ).astype(jnp.bfloat16)
    up_grad = (active_grad * silu_gate).astype(jnp.bfloat16)
    pair_grad = jnp.concatenate([gate_grad, up_grad], axis=2)
    grad_down = jnp.einsum(
        "erf,erd->efd", active, grad_received, preferred_element_type=jnp.float32
    )
    grad_pair = jnp.einsum("erd,erf->edf", received, pair_grad, preferred_element_type=jnp.float32)
    grad_gate = grad_pair[..., :ff_local]
    grad_up = grad_pair[..., ff_local:]
    input_part = jnp.einsum(
        "erf,edf->erd", pair_grad, w_pair, preferred_element_type=jnp.float32
    ).astype(jnp.bfloat16)
    sent_back = return_experts(input_part)
    token_grad = jnp.zeros((seq_len, sent_back.shape[1]), jnp.float32)
    for pick_rank in range(top_count):
        token_grad = token_grad + sent_back[flat_index[:, pick_rank]].astype(jnp.float32)
    normed2_grad = scatter_rows(token_grad) + jnp.dot(
        own_logit_grad, router_full.T, preferred_element_type=jnp.float32
    )
    hidden_norm_grad, gain2_grad = norm_backward(hidden, scale2, gains_wide[1], normed2_grad)
    hidden_grad = cotangent.astype(jnp.float32) + hidden_norm_grad
    router_grad = jnp.dot(own_normed2.T, own_logit_grad, preferred_element_type=jnp.float32)
    hidden_rows = gather_rows(hidden_grad.astype(jnp.bfloat16))
    grad_out_full = jnp.dot(mixed.T, hidden_rows, preferred_element_type=jnp.float32)
    mixed_grad = (
        jnp.dot(hidden_rows, out_full.T, preferred_element_type=jnp.float32)
        .astype(jnp.bfloat16)
        .reshape(seq_len, heads_local, HD)
    )

    def attend_back(carried, pieces):
        key_acc, value_acc = carried
        start, log_sum = pieces
        query_block, scores, allowed = block_scores(start)
        probs = jnp.where(allowed[None], jnp.exp(scores - log_sum[:, :, None]), 0.0)
        prob_grad = jnp.einsum(
            "qhd,khd->hqk", mixed_grad, values, preferred_element_type=jnp.float32
        )
        delta = jnp.sum(probs * prob_grad, axis=-1, keepdims=True)
        score_grad = (probs * (prob_grad - delta)).astype(jnp.bfloat16)
        query_block_grad = (
            jnp.einsum("hqk,khd->qhd", score_grad, keys, preferred_element_type=jnp.float32)
            * score_scale
        )
        key_acc = (
            key_acc
            + jnp.einsum(
                "hqk,qhd->khd", score_grad, query_block, preferred_element_type=jnp.float32
            )
            * score_scale
        )
        value_acc = value_acc + jnp.einsum(
            "hqk,qhd->khd",
            probs.astype(jnp.bfloat16),
            mixed_grad,
            preferred_element_type=jnp.float32,
        )
        return ((key_acc, value_acc), query_block_grad)

    zero_heads = jnp.zeros((seq_len, heads_local, HD), jnp.float32)
    (key_grad, value_grad), query_blocks = lax.scan(
        attend_back, (zero_heads, zero_heads), (block_starts, log_sums)
    )
    query_grad = query_blocks.reshape(seq_len, heads_local, HD)
    query_norm_grad = rotate_back(query_grad, cosine, sine).reshape(seq_len, head_cols)
    key_norm_grad = rotate_back(key_grad, cosine, sine).reshape(seq_len, head_cols)
    gain_query_grad = jnp.sum(query_norm_grad * unit_q, axis=0)
    gain_key_grad = jnp.sum(key_norm_grad * unit_k, axis=0)
    scaled_q = query_norm_grad * gain_query
    scaled_k = key_norm_grad * gain_key
    inner_q, inner_k = tp_totals(
        jnp.sum(scaled_q * unit_q, axis=-1), jnp.sum(scaled_k * unit_k, axis=-1)
    )
    query_raw_grad = scale_q * (scaled_q - unit_q * (inner_q / width)[:, None])
    key_raw_grad = scale_k * (scaled_k - unit_k * (inner_k / width)[:, None])
    qkv_grad = jnp.stack(
        [query_raw_grad, key_raw_grad, value_grad.reshape(seq_len, head_cols)]
    ).astype(jnp.bfloat16)
    grad_qkv_full = jnp.einsum("sd,csh->cdh", rows1, qkv_grad, preferred_element_type=jnp.float32)
    normed1_part = jnp.einsum("csh,cdh->sd", qkv_grad, qkv_full, preferred_element_type=jnp.float32)
    normed1_grad = scatter_rows(normed1_part)
    input_norm_grad, gain1_grad = norm_backward(x_own, scale1, gains_wide[0], normed1_grad)
    input_grad = hidden_grad + input_norm_grad
    zero_width = jnp.zeros((width,), jnp.float32)
    gains_grad = jnp.stack(
        [
            gain1_grad,
            gain2_grad,
            lax.dynamic_update_slice_in_dim(zero_width, gain_query_grad, col_start, 0),
            lax.dynamic_update_slice_in_dim(zero_width, gain_key_grad, col_start, 0),
        ]
    )
    grad_qkv, grad_out = (
        lax.psum_scatter(
            grad_qkv_full.astype(jnp.bfloat16), "fsdp", scatter_dimension=1, tiled=True
        ).astype(jnp.float32),
        lax.psum_scatter(
            grad_out_full.astype(jnp.bfloat16), "fsdp", scatter_dimension=1, tiled=True
        ).astype(jnp.float32),
    )
    grad_router, grad_gains = (
        lax.psum_scatter(router_grad, ("fsdp", "tp"), scatter_dimension=0, tiled=True),
        lax.psum_scatter(gains_grad, ("fsdp", "tp"), scatter_dimension=1, tiled=True),
    )
    return (
        layer_out,
        input_grad,
        grad_qkv,
        grad_out,
        grad_router,
        grad_gains,
        grad_gate,
        grad_up,
        grad_down,
    )


GRID = (4, 2, 2, 2)
FINE = ("z", "x", "y", "core")
LANES = 128
CONTRACT_LAST = (((1,), (1,)), ((), ()))


def permutation(target):
    def place(z, x, y, c):
        return ((z * GRID[1] + x) * GRID[2] + y) * GRID[3] + c

    return [
        (place(*at), place(*target(*at))) for at in itertools.product(*(range(n) for n in GRID))
    ]


SWAP_CORE = permutation(lambda z, x, y, c: (z, x, y, 1 - c))
SWAP_X = permutation(lambda z, x, y, c: (z, 1 - x, y, c))
SWAP_Y = permutation(lambda z, x, y, c: (z, x, 1 - y, c))
SWAP_BOTH = permutation(lambda z, x, y, c: (z, x, 1 - y, 1 - c))
SWAP_FIRST = permutation(lambda z, x, y, c: (z, 1 - x, y, c) if c == 0 else (z, x, 1 - y, c))
SWAP_SECOND = permutation(lambda z, x, y, c: (z, x, 1 - y, c) if c == 0 else (z, 1 - x, y, c))


def shift_z(steps):
    return permutation(lambda z, x, y, c: ((z + steps) % GRID[0], x, y, c))


def send(values, pairs):
    return lax.ppermute(values, FINE, pairs)


def add_low(*terms):
    return sum(term.astype(jnp.float32) for term in terms).astype(jnp.bfloat16)


def side_totals(first, second):
    return lax.psum((first, second), FINE[2:])


def fence(*values):
    return lax.optimization_barrier(values)


def wide_sum(*terms):
    return sum(term.astype(jnp.float32) for term in terms)


def pair_dots(left, right):
    return lax.dot_general(left, right, (((0,), (0,)), ((), ())), preferred_element_type=jnp.float32)


def side_pair(own, far):
    is_far = lax.axis_index("y") == 1
    return jnp.stack([jnp.where(is_far, far, own), jnp.where(is_far, own, far)])


def four_rows(mine, theirs):
    is_second = lax.axis_index("core") == 1
    both = jnp.stack(
        [jnp.where(is_second, theirs, mine), jnp.where(is_second, mine, theirs)], axis=1
    )
    return both.reshape(4 * mine.shape[1], *mine.shape[2:])


def core_split(values):
    core = lax.axis_index("core")
    blocks = values.astype(jnp.bfloat16).reshape(2, 2, values.shape[0] // 4, values.shape[1])
    return (
        lax.dynamic_index_in_dim(blocks, 1 - core, 1, keepdims=False),
        lax.dynamic_index_in_dim(blocks, core, 1, keepdims=False),
    )


def side_split(mine, back):
    side = lax.axis_index("y")

    def at(pair, which):
        return lax.dynamic_index_in_dim(pair, which, 0, keepdims=False)

    away = add_low(at(mine, 1 - side), at(back, 1 - side))
    return (away, wide_sum(at(mine, side), at(back, side)))


def expert_kernel(blocks_ref, near_ref, far_ref, *refs, n_experts):
    grad_block_refs, (router_ref, place_ref), own, other = refs[:4], refs[4:6], refs[6:9], refs[9:12]
    outputs, (gates_ref, dots_sum_ref, route_ref) = refs[-10:-3], refs[-3:]
    near_route_ref, far_route_ref, active_ref, hidden_ref, dots_ref, grads_ref, rows_ref = outputs
    _, width, units = own[0].shape
    exp_local = place_ref.shape[0]
    half = near_ref.shape[0]
    step = pl.program_id(0)

    @pl.when(step == 0)
    def _():
        rows_ref[:half] = near_ref[...]
        rows_ref[half:] = far_ref[...]
        quarter = half // 2
        for at, ref in enumerate(grad_block_refs):
            grads_ref[at * quarter : (at + 1) * quarter] = ref[:, :width]
        named = jnp.concatenate([ref[:, width:] for ref in grad_block_refs], axis=0)
        lane = lax.broadcasted_iota(jnp.int32, (1, LANES), 1)
        logits = jnp.dot(rows_ref[...], router_ref[...], preferred_element_type=jnp.float32)
        logits = jnp.where(lane < n_experts, logits, NEG_FILL)
        powered = jnp.exp(logits - jnp.max(logits, axis=-1, keepdims=True))
        total = jnp.sum(powered, axis=-1, keepdims=True)
        gates_ref[...] = powered / total * named.astype(jnp.float32)
        dots_sum_ref[...] = jnp.zeros_like(dots_sum_ref)
        route_ref[...] = jnp.zeros_like(route_ref)

    def expert(place, gate_ref, up_ref, down_ref):
        rows = rows_ref[...]
        gate = jnp.sum(gates_ref[...] * place, axis=-1, keepdims=True)
        gate_pre = jnp.dot(rows, gate_ref[0], preferred_element_type=jnp.float32)
        up_pre = jnp.dot(rows, up_ref[0], preferred_element_type=jnp.float32)
        y_down = lax.dot_general(
            grads_ref[...], down_ref[0], CONTRACT_LAST, preferred_element_type=jnp.float32
        )
        sigmoid = 1.0 / (1.0 + jnp.exp(-gate_pre))
        silu = gate_pre * sigmoid
        active = silu * up_pre
        dots_sum_ref[...] += jnp.sum(active * y_down, axis=-1, keepdims=True) * place
        active_ref[...] = (active * gate).astype(jnp.bfloat16)
        active_grad = y_down * gate
        gate_grad = (active_grad * up_pre * sigmoid * (1.0 + gate_pre * (1.0 - sigmoid))).astype(
            jnp.bfloat16
        )
        up_grad = (active_grad * silu).astype(jnp.bfloat16)
        hidden_ref[:, :units] = gate_grad
        hidden_ref[:, units:] = up_grad
        route_ref[...] += lax.dot_general(
            gate_grad, gate_ref[0], CONTRACT_LAST, preferred_element_type=jnp.float32
        ) + lax.dot_general(
            up_grad, up_ref[0], CONTRACT_LAST, preferred_element_type=jnp.float32
        )

    place = place_ref[pl.ds(step % exp_local, 1), :]

    @pl.when(step < exp_local)
    def _():
        expert(place, *own)

    @pl.when(step >= exp_local)
    def _():
        expert(place, *other)

    @pl.when(step == 2 * exp_local - 1)
    def _():
        near_route_ref[...] = route_ref[:half].astype(jnp.bfloat16)
        far_route_ref[...] = route_ref[half:].astype(jnp.bfloat16)
        dots_ref[...] = jnp.transpose(dots_sum_ref[...])[:n_experts]


def expert_rows(at, before, blocks, near, far, all_grads, router, place, own, other, n_experts):
    half, width = near.shape
    count = 2 * half
    exp_local, _, units = own[0].shape
    wide = all_grads.shape[1]

    def whole(array):
        return pl.BlockSpec(
            array.shape, lambda step, blocks: (0,) * array.ndim, pipeline_mode=pl.Buffered(1)
        )

    def picked(row):
        return pl.BlockSpec(
            (count // 4, wide), lambda step, blocks: (blocks[row], 0), pipeline_mode=pl.Buffered(1)
        )

    def own_expert(array):
        return pl.BlockSpec(
            (1, *array.shape[1:]), lambda step, blocks: (jnp.minimum(step, exp_local - 1), 0, 0)
        )

    def other_expert(array):
        return pl.BlockSpec(
            (1, *array.shape[1:]), lambda step, blocks: (jnp.maximum(step - exp_local, 0), 0, 0)
        )

    def first_block(shape):
        return pl.BlockSpec(shape, lambda step, blocks: (0, 0))

    def step_block(columns):
        return pl.BlockSpec((count, columns), lambda step, blocks: (at, step))

    def round_block(columns):
        return pl.BlockSpec((count, columns), lambda step, blocks: (at, 0))

    def rounds(columns):
        return jax.ShapeDtypeStruct((GRID[0] * count, columns), jnp.bfloat16)

    inputs = (blocks, near, far, *(all_grads for _ in range(4)), router, place, *own, *other, *before)
    order = (2, 3, 5, 6)
    route = jax.ShapeDtypeStruct((half, width), jnp.bfloat16)
    return pl.pallas_call(
        functools.partial(expert_kernel, n_experts=n_experts),
        out_shape=[
            route,
            route,
            rounds(2 * exp_local * units),
            rounds(4 * exp_local * units),
            jax.ShapeDtypeStruct((n_experts, count), jnp.float32),
            rounds(width),
            rounds(width),
        ],
        grid_spec=pltpu.PrefetchScalarGridSpec(
            num_scalar_prefetch=1,
            grid=(2 * exp_local,),
            in_specs=[
                whole(near),
                whole(far),
                *(picked(row) for row in range(4)),
                whole(router),
                whole(place),
                *(own_expert(array) for array in own),
                *(other_expert(array) for array in other),
                *(pl.BlockSpec(memory_space=pl.ANY) for _ in before),
            ],
            out_specs=[
                first_block((half, width)),
                first_block((half, width)),
                step_block(units),
                step_block(2 * units),
                first_block((n_experts, count)),
                round_block(width),
                round_block(width),
            ],
            scratch_shapes=[
                pltpu.VMEM((count, LANES), jnp.float32),
                pltpu.VMEM((count, LANES), jnp.float32),
                pltpu.VMEM((count, width), jnp.float32),
            ],
        ),
        input_output_aliases={
            len(inputs) - len(before) + index: order[index] for index in range(len(before))
        },
        cost_estimate=pl.CostEstimate(flops=1024, bytes_accessed=1024, transcendentals=0),
        compiler_params=pltpu.CompilerParams(
            dimension_semantics=("arbitrary",), vmem_limit_bytes=46 * 1024 * 1024
        ),
        name="expert_rows",
    )(*inputs)


def dense_shards(
    tokens,
    seg_ids,
    pad_mask,
    expert_ids,
    w_qkv,
    w_out,
    w_router,
    norm_gains,
    w_gate,
    w_up,
    w_down,
    cotangent,
):
    z, x, y, core = (lax.axis_index(name) for name in FINE)
    fsdp_rank = z * GRID[1] + x
    tp_rank = y * GRID[3] + core
    local_rows, width = tokens.shape
    seq_len = seg_ids.shape[1]
    exp_local, _, ff_local = w_gate.shape
    n_experts = w_router.shape[1]
    head_cols = w_qkv.shape[2]
    heads_local = head_cols // HD
    score_scale = HD ** (-0.5)
    own_start = tp_rank * local_rows
    small_cols = norm_gains.shape[1]
    fsdp = FINE[:2]

    def own_rows(values):
        return lax.dynamic_slice_in_dim(values, own_start, local_rows, 0)

    tp_swaps = (SWAP_CORE, SWAP_Y, SWAP_BOTH)
    z_shifts = [shift_z(steps) for steps in range(1, GRID[0])]
    small_own = jnp.pad(
        jnp.concatenate([w_router, norm_gains.T], axis=1), ((0, 0), (0, LANES - n_experts - 4))
    )
    small = lax.dynamic_update_slice_in_dim(
        jnp.zeros((w_qkv.shape[1], LANES), jnp.bfloat16), small_own, tp_rank * small_cols, 0
    )
    smalls, tokens_own = fence([send(small, swap) for swap in tp_swaps], tokens)
    small = small + smalls[0] + smalls[1] + smalls[2]
    weights_own = jnp.concatenate(
        [w_qkv.transpose(1, 0, 2).reshape(w_qkv.shape[1], -1), w_out.T, small], axis=1
    )
    weights_full = lax.all_gather(weights_own, fsdp, axis=0, tiled=True)
    names = jnp.arange(n_experts, dtype=jnp.int32)
    own_ids = own_rows(expert_ids)
    named = (own_ids[:, :, None] == names[None, None, :]).any(axis=1)
    named_wide = jnp.pad(named.astype(jnp.bfloat16), ((0, 0), (0, LANES - n_experts)))
    grads_own = jnp.concatenate([cotangent, named_wide], axis=1)
    far = send(tokens_own, SWAP_Y)
    mine = side_pair(tokens, far)
    theirs = send(mine, SWAP_CORE)
    rows_x = four_rows(mine, theirs).astype(jnp.float32)
    scale1 = lax.rsqrt(jnp.mean(rows_x * rows_x, axis=-1, keepdims=True) + EPSILON)
    own_weights = (w_gate, w_up, w_down)
    grads_own, weights_own, weights_full, scale1, rows_x = fence(
        grads_own, own_weights, weights_full, scale1, rows_x
    )
    all_grads_abs = lax.all_gather(grads_own, FINE[:3], axis=0, tiled=True)
    other_weights = tuple(send(weight, SWAP_CORE) for weight in weights_own)
    qkv_full = weights_full[:, : 3 * head_cols]
    out_full = weights_full[:, 3 * head_cols : 4 * head_cols]
    router_wide = weights_full[:, 4 * head_cols :]
    router_full = router_wide[:, :n_experts]
    gains_wide = router_wide[:, n_experts : n_experts + 4].T.astype(jnp.float32)

    cosine, sine = rope_tables(seq_len, HD)
    allowed = allowed_mask(seg_ids[0], pad_mask[0], 0, seq_len)
    x_own = tokens.astype(jnp.float32)
    col_start = tp_rank * head_cols
    gain_query = lax.dynamic_slice_in_dim(gains_wide[2], col_start, head_cols)
    gain_key = lax.dynamic_slice_in_dim(gains_wide[3], col_start, head_cols)
    rows1 = (rows_x * scale1 * gains_wide[0]).astype(jnp.bfloat16)
    projected = jnp.dot(rows1, qkv_full, preferred_element_type=jnp.float32)
    query_raw = projected[:, :head_cols]
    key_raw = projected[:, head_cols : 2 * head_cols]
    values = projected[:, 2 * head_cols :].astype(jnp.bfloat16).reshape(seq_len, heads_local, HD)
    squares = side_totals(
        jnp.sum(query_raw * query_raw, axis=-1), jnp.sum(key_raw * key_raw, axis=-1)
    )
    scale_q = lax.rsqrt(squares[0] / width + EPSILON)[:, None]
    scale_k = lax.rsqrt(squares[1] / width + EPSILON)[:, None]
    unit_q = query_raw * scale_q
    unit_k = key_raw * scale_k
    queries = rotate((unit_q * gain_query).reshape(seq_len, heads_local, HD), cosine, sine).astype(
        jnp.bfloat16
    )
    keys = rotate((unit_k * gain_key).reshape(seq_len, heads_local, HD), cosine, sine).astype(
        jnp.bfloat16
    )
    raw_scores = (
        jnp.einsum("qhd,khd->hqk", queries, keys, preferred_element_type=jnp.float32) * score_scale
    )
    scores = jnp.where(allowed[None], raw_scores, NEG_FILL)
    powered = jnp.exp(scores - jnp.max(scores, axis=-1, keepdims=True))
    probs = powered / jnp.sum(powered, axis=-1, keepdims=True)
    probs_low = probs.astype(jnp.bfloat16)
    mixed = (
        jnp.einsum("hqk,khd->qhd", probs_low, values, preferred_element_type=jnp.float32)
        .reshape(seq_len, head_cols)
        .astype(jnp.bfloat16)
    )
    away, mine = core_split(
        lax.dot_general(mixed, out_full, CONTRACT_LAST, preferred_element_type=jnp.float32)
    )
    away, kept = side_split(mine, send(away, SWAP_CORE))
    far, kept = fence(send(away, SWAP_Y), kept)
    hidden = x_own + kept + far
    normed2, scale2 = norm_forward(hidden, gains_wide[1])
    own_normed2 = normed2.astype(jnp.bfloat16)

    place = (
        jnp.arange(LANES)[None, :] == fsdp_rank * exp_local + jnp.arange(exp_local)[:, None]
    ).astype(jnp.float32)
    rows, rows_near, rows_far = [own_normed2], [], []
    results, seconds, firsts, homes = [], [], [], []

    def hop(column):
        return send(column, z_shifts[0])

    def experts(at):
        plane = (z - at) % GRID[0] * (GRID[1] * GRID[2])
        beside = jnp.where(core == 0, (1 - x) * GRID[2] + y, x * GRID[2] + 1 - y)
        across = jnp.where(core == 0, x * GRID[2] + 1 - y, (1 - x) * GRID[2] + y)
        opposite = (1 - x) * GRID[2] + 1 - y
        blocks = plane + jnp.stack([x * GRID[2] + y, beside, across, opposite])
        before = [results[at - 1][index] for index in (2, 3, 5, 6)] if at else []
        return expert_rows(
            at,
            before,
            blocks.astype(jnp.int32),
            rows_near[at],
            rows_far[at],
            all_grads_abs,
            router_wide,
            place,
            own_weights,
            other_weights,
            n_experts,
        )

    def near_of(at, arrived):
        return jnp.concatenate([rows[at], arrived], axis=0)

    def first_part(near, second):
        half = near.shape[0] // 2
        return add_low(near[half:], second[half:])

    def mine_part(near, second, first):
        half = near.shape[0] // 2
        return wide_sum(near[:half], second[:half], first)

    def route_first(at):
        return send(first_part(results[at][0], seconds[at]), SWAP_FIRST)

    def route_home(at):
        mine = mine_part(results[at][0], seconds[at], firsts[at])
        return send(mine.astype(jnp.bfloat16), z_shifts[GRID[0] - 1 - at])

    hopped, arrived = fence(hop(rows[0]), send(rows[0], SWAP_FIRST))
    rows.append(hopped)
    rows_near.append(near_of(0, arrived))
    hopped, arrived, second = fence(
        hop(rows[1]), send(rows[1], SWAP_FIRST), send(rows_near[0], SWAP_SECOND)
    )
    rows.append(hopped)
    rows_near.append(near_of(1, arrived))
    rows_far.append(second)
    hopped, arrived, second, result = fence(
        hop(rows[2]), send(rows[2], SWAP_FIRST), send(rows_near[1], SWAP_SECOND), experts(0)
    )
    rows.append(hopped)
    rows_near.append(near_of(2, arrived))
    rows_far.append(second)
    results.append(result)
    arrived, second, back, result = fence(
        send(rows[3], SWAP_FIRST),
        send(rows_near[2], SWAP_SECOND),
        send(results[0][1], SWAP_SECOND),
        experts(1),
    )
    rows_near.append(near_of(3, arrived))
    rows_far.append(second)
    seconds.append(back)
    results.append(result)
    second, back, first, result = fence(
        send(rows_near[3], SWAP_SECOND),
        send(results[1][1], SWAP_SECOND),
        route_first(0),
        experts(2),
    )
    rows_far.append(second)
    seconds.append(back)
    firsts.append(first)
    results.append(result)
    back, first, result = fence(
        send(results[2][1], SWAP_SECOND), route_first(1), experts(3)
    )
    seconds.append(back)
    firsts.append(first)
    results.append(result)
    homes.append(mine_part(results[0][0], seconds[0], firsts[0]))

    dots = jnp.stack([result[4] for result in results])
    part = dots.shape[-1] // 4
    all_active, all_hidden, all_grads, all_rows = (results[-1][index] for index in (2, 3, 5, 6))
    down_rows = jnp.concatenate(
        [weights[2].reshape(-1, width) for weights in (own_weights, other_weights)]
    )
    back, first, home, dots_back, dots, all_active, down_rows, all_hidden = fence(
        send(results[3][1], SWAP_SECOND),
        route_first(2),
        route_home(1),
        send(dots[..., 2 * part :], SWAP_SECOND),
        dots,
        all_active,
        down_rows,
        all_hidden,
    )
    seconds.append(back)
    firsts.append(first)
    homes.append(home)
    dots = dots[..., : 2 * part] + dots_back
    units = exp_local * ff_local
    pair_count = 2 * exp_local

    def piece(at):
        return all_hidden[:, at * ff_local : (at + 1) * ff_local]

    first, home, dots_back, dots, output, all_hidden = fence(
        route_first(3),
        route_home(2),
        send(dots[..., part:], SWAP_FIRST),
        dots,
        jnp.dot(all_active, down_rows, preferred_element_type=jnp.float32).astype(jnp.bfloat16),
        all_hidden,
    )
    half = output.shape[0] // (2 * GRID[0])
    outputs = [
        (output[2 * at * half : (2 * at + 1) * half], output[(2 * at + 1) * half : 2 * (at + 1) * half])
        for at in range(GRID[0])
    ]
    firsts.append(first)
    homes.append(home)
    dots = dots[..., :part] + dots_back
    home, dots_back, dots, outputs, all_hidden, others = fence(
        route_home(3),
        [send(dots[at], shift_z(-at)) for at in range(1, GRID[0])],
        dots[0],
        outputs,
        all_hidden,
        [pair_dots(all_rows, piece(pair_count))],
    )
    homes.append(home)
    token_grad = wide_sum(*homes)
    own_dots = (dots + dots_back[0] + dots_back[1] + dots_back[2]).T

    logits = jnp.dot(own_normed2, router_full, preferred_element_type=jnp.float32)
    router_probs = jax.nn.softmax(logits, axis=-1)
    own_gates = jnp.where(named, router_probs, 0.0)
    chosen = jnp.where(named, own_dots, 0.0)
    weighted = jnp.sum(own_gates * chosen, axis=-1, keepdims=True)
    own_logit_grad = (router_probs * (chosen - weighted)).astype(jnp.bfloat16)
    normed2_grad = token_grad + jnp.dot(
        own_logit_grad, router_full.T, preferred_element_type=jnp.float32
    )
    hidden_norm_grad, gain2_grad = norm_backward(hidden, scale2, gains_wide[1], normed2_grad)
    hidden_grad = cotangent.astype(jnp.float32) + hidden_norm_grad
    hidden_low = hidden_grad.astype(jnp.bfloat16)
    far, hidden_low, outputs, all_hidden, more = fence(
        send(hidden_low, SWAP_Y),
        hidden_low,
        outputs,
        all_hidden,
        [pair_dots(all_rows, piece(pair_count + 1))],
    )
    others = [*others, *more]
    mine = side_pair(hidden_low, far)
    theirs, mine, outputs, all_hidden = fence(send(mine, SWAP_CORE), mine, outputs, all_hidden)
    hidden_rows = four_rows(mine, theirs)
    mixed_grad = jnp.dot(hidden_rows, out_full, preferred_element_type=jnp.float32).astype(
        jnp.bfloat16
    )
    mixed_grad, grad_out_full = fence(
        mixed_grad, pair_dots(hidden_rows, mixed).astype(jnp.bfloat16)
    )
    grad_out = (
        lax.psum_scatter(grad_out_full, fsdp, scatter_dimension=0, tiled=True)
        .astype(jnp.float32)
        .T
    )
    mixed_grad = mixed_grad.reshape(seq_len, heads_local, HD)
    prob_grad = jnp.einsum("qhd,khd->hqk", mixed_grad, values, preferred_element_type=jnp.float32)
    delta = jnp.sum(probs * prob_grad, axis=-1, keepdims=True)
    score_grad = (probs * (prob_grad - delta)).astype(jnp.bfloat16)
    value_grad = jnp.einsum(
        "hqk,qhd->khd", probs_low, mixed_grad, preferred_element_type=jnp.float32
    )
    query_grad = (
        jnp.einsum("hqk,khd->qhd", score_grad, keys, preferred_element_type=jnp.float32)
        * score_scale
    )
    key_grad = (
        jnp.einsum("hqk,qhd->khd", score_grad, queries, preferred_element_type=jnp.float32)
        * score_scale
    )
    query_norm_grad = rotate_back(query_grad, cosine, sine).reshape(seq_len, head_cols)
    key_norm_grad = rotate_back(key_grad, cosine, sine).reshape(seq_len, head_cols)
    gain_query_grad = jnp.sum(query_norm_grad * unit_q, axis=0)
    gain_key_grad = jnp.sum(key_norm_grad * unit_k, axis=0)
    scaled_q = query_norm_grad * gain_query
    scaled_k = key_norm_grad * gain_key
    inners = side_totals(jnp.sum(scaled_q * unit_q, axis=-1), jnp.sum(scaled_k * unit_k, axis=-1))
    query_raw_grad = scale_q * (scaled_q - unit_q * (inners[0] / width)[:, None])
    key_raw_grad = scale_k * (scaled_k - unit_k * (inners[1] / width)[:, None])
    qkv_grad = jnp.concatenate(
        [query_raw_grad, key_raw_grad, value_grad.reshape(seq_len, head_cols)], axis=1
    ).astype(jnp.bfloat16)
    normed1_part = lax.dot_general(
        qkv_grad, qkv_full, CONTRACT_LAST, preferred_element_type=jnp.float32
    )
    gain1_grad = jnp.sum(normed1_part * (rows_x * scale1), axis=0)
    away, mine = core_split(normed1_part)
    zero_width = jnp.zeros((width,), jnp.float32)
    gains_grad = jnp.stack(
        [
            gain1_grad,
            gain2_grad,
            lax.dynamic_update_slice_in_dim(zero_width, gain_query_grad, col_start, 0),
            lax.dynamic_update_slice_in_dim(zero_width, gain_key_grad, col_start, 0),
        ]
    )
    small = jnp.concatenate([pair_dots(own_normed2, own_logit_grad), gains_grad.T], axis=1)
    small = jnp.pad(small, ((0, 0), (0, LANES - n_experts - 4)))
    grad_full = jnp.concatenate([pair_dots(rows1, qkv_grad), small], axis=1).astype(jnp.bfloat16)
    grad_own = lax.psum_scatter(grad_full, fsdp, scatter_dimension=0, tiled=True)
    grad_qkv = (
        grad_own[:, : 3 * head_cols].astype(jnp.float32).reshape(-1, 3, head_cols).transpose(1, 0, 2)
    )
    small = grad_own[:, 3 * head_cols :]
    away, mine, outputs, all_hidden, all_active, _ = fence(
        away, mine, outputs, all_hidden, all_active, grad_full
    )
    back, mine, output_seconds, others, more, other_down, all_hidden = fence(
        send(away, SWAP_CORE),
        mine,
        [send(pair[1], SWAP_SECOND) for pair in outputs],
        [send(other, SWAP_CORE) for other in others],
        [pair_dots(all_rows, piece(pair_count + at)) for at in range(2, pair_count)],
        pair_dots(all_active[:, units:], all_grads),
        all_hidden,
    )
    away, kept = side_split(mine, back)
    output_firsts = [
        send(first_part(pair[0], second), SWAP_FIRST)
        for pair, second in zip(outputs, output_seconds)
    ]
    far, kept, output_firsts, more, other_down, grad_pair, all_hidden = fence(
        send(away, SWAP_Y),
        kept,
        output_firsts,
        [send(other, SWAP_CORE) for other in more],
        send(other_down, SWAP_CORE),
        [pair_dots(all_rows, piece(at)) + other for at, other in enumerate(others)],
        all_hidden,
    )
    output_mine = [
        mine_part(pair[0], second, first)
        for pair, second, first in zip(outputs, output_seconds, output_firsts)
    ]
    output_homes = [
        send(output_mine[at].astype(jnp.bfloat16), shift_z(-at)) for at in range(1, GRID[0])
    ]
    normed1_grad = kept + far
    input_norm_grad, _ = norm_backward(x_own, own_rows(scale1), gains_wide[0], normed1_grad)
    input_grad = hidden_grad + input_norm_grad
    grad_pair = [
        *grad_pair,
        *(pair_dots(all_rows, piece(2 + at)) + other for at, other in enumerate(more)),
    ]
    grad_down = (pair_dots(all_active[:, :units], all_grads) + other_down).reshape(
        exp_local, ff_local, width
    )
    layer_out = (hidden + wide_sum(output_mine[0], *output_homes)).astype(jnp.bfloat16)
    grad_gate = jnp.stack(grad_pair[0::2])
    grad_up = jnp.stack(grad_pair[1::2])
    small = lax.dynamic_slice_in_dim(
        wide_sum(small, *(send(small, swap) for swap in tp_swaps)),
        tp_rank * small_cols,
        small_cols,
        0,
    )
    grad_router = small[:, :n_experts]
    grad_gains = small[:, n_experts : n_experts + 4].T
    return (
        layer_out,
        input_grad,
        grad_qkv,
        grad_out,
        grad_router,
        grad_gains,
        grad_gate,
        grad_up,
        grad_down,
    )


def solution(mesh):
    fast = tuple(mesh.shape.values()) == (GRID[0] * GRID[1], GRID[2] * GRID[3])
    fine = Mesh(mesh.devices.reshape(GRID), FINE) if fast else None

    def layer(*arguments):
        n_experts = arguments[8].shape[0]
        top_count = arguments[3].shape[1]
        if fast and n_experts <= 2 * top_count:
            return placed_shards(dense_shards, fine, FINE[:2], FINE[2:])(*arguments)
        return placed_shards(shards, mesh, ("fsdp",), ("tp",))(*arguments)

    return layer


def placed_shards(body, mesh, fsdp, tp):
    rows = P((*fsdp, *tp), None)
    experts = P(fsdp, None, tp)
    columns = P(None, (*fsdp, *tp))
    return jax.shard_map(
        body,
        mesh=mesh,
        in_specs=(
            rows,
            P(fsdp, None),
            P(fsdp, None),
            P(fsdp, None),
            P(None, fsdp, tp),
            P(tp, fsdp),
            rows,
            columns,
            experts,
            experts,
            P(fsdp, tp, None),
            rows,
        ),
        out_specs=(
            rows,
            rows,
            P(None, fsdp, tp),
            P(tp, fsdp),
            rows,
            columns,
            experts,
            experts,
            P(fsdp, tp, None),
        ),
        check_vma=False,
    )
```

```python
import functools
import itertools

import jax
import jax.numpy as jnp
from jax import lax
from jax.experimental import pallas as pl
from jax.experimental.pallas import tpu as pltpu
from jax.sharding import Mesh
from jax.sharding import PartitionSpec as P

HD = 128


EPSILON = 1e-05
NEG_FILL = -1e30


def route_slots(expert_ids, n_experts, capacity):
    seq_len, top_count = expert_ids.shape
    experts = jnp.arange(n_experts, dtype=jnp.int32)
    counts = jnp.sum((expert_ids[:, :, None] == experts[None, None, :]).astype(jnp.int32), axis=1)
    earlier = jnp.cumsum(counts, axis=0) - counts
    slot_rank = jnp.take_along_axis(earlier, expert_ids, axis=1)
    flat_index = expert_ids * capacity + slot_rank
    token_index = jnp.broadcast_to(
        jnp.arange(seq_len, dtype=jnp.int32)[:, None], (seq_len, top_count)
    )
    source = jnp.full((n_experts * capacity,), seq_len, jnp.int32)
    source = source.at[flat_index.reshape(-1)].set(token_index.reshape(-1))
    return (flat_index, source)


def rope_tables(seq_len, head_size):
    half_size = head_size // 2
    inverse = 10000.0 ** (-2.0 * jnp.arange(half_size, dtype=jnp.float32) / head_size)
    angles = jnp.arange(seq_len, dtype=jnp.float32)[:, None] * inverse[None, :]
    return (jnp.cos(angles)[:, None, :], jnp.sin(angles)[:, None, :])


def rotate(values, cosine, sine):
    half_size = values.shape[-1] // 2
    first = values[..., :half_size]
    second = values[..., half_size:]
    return jnp.concatenate(
        [first * cosine - second * sine, second * cosine + first * sine], axis=-1
    )


def rotate_back(grads, cosine, sine):
    half_size = grads.shape[-1] // 2
    first = grads[..., :half_size]
    second = grads[..., half_size:]
    return jnp.concatenate(
        [first * cosine + second * sine, second * cosine - first * sine], axis=-1
    )


def allowed_mask(segment, padding, row_start, row_count):
    row_index = row_start + jnp.arange(row_count, dtype=jnp.int32)
    col_index = jnp.arange(segment.shape[0], dtype=jnp.int32)
    same_doc = segment[:, None] == segment[None, :]
    causal = col_index[None, :] <= row_index[:, None]
    usable = (padding[None, :] == 1) | (col_index[None, :] == row_index[:, None])
    return same_doc & causal & usable


def norm_forward(values, gain):
    scale = lax.rsqrt(jnp.mean(values * values, axis=-1, keepdims=True) + EPSILON)
    return (values * scale * gain, scale)


def norm_backward(values, scale, gain, grads):
    unit = values * scale
    gain_grad = jnp.sum(grads * unit, axis=0)
    scaled = grads * gain
    return (scale * (scaled - unit * jnp.mean(scaled * unit, axis=-1, keepdims=True)), gain_grad)


def gather_rows(values):
    return lax.all_gather(values, "tp", axis=0, tiled=True)


def scatter_rows(values):
    return lax.psum_scatter(
        values.astype(jnp.bfloat16), "tp", scatter_dimension=0, tiled=True
    ).astype(jnp.float32)


def tp_totals(first, second):
    return lax.psum((first, second), "tp")


def shards(
    tokens,
    seg_ids,
    pad_mask,
    expert_ids,
    w_qkv,
    w_out,
    w_router,
    norm_gains,
    w_gate,
    w_up,
    w_down,
    cotangent,
):
    tp_rank = lax.axis_index("tp")
    fsdp_count = lax.axis_size("fsdp")
    local_rows, width = tokens.shape
    seq_len = seg_ids.shape[1]
    exp_local = w_gate.shape[0]
    ff_local = w_gate.shape[2]
    n_experts = exp_local * fsdp_count
    top_count = expert_ids.shape[1]
    capacity = (seq_len * top_count * 33 + 32 * n_experts - 1) // (32 * n_experts)
    head_cols = w_qkv.shape[2]
    heads_local = head_cols // HD
    block_rows = min(512, seq_len)
    n_blocks = seq_len // block_rows
    score_scale = HD ** (-0.5)

    def send_experts(buffer):
        return lax.all_to_all(buffer, "fsdp", split_axis=0, concat_axis=1, tiled=True)

    def return_experts(buffer):
        back = lax.all_to_all(buffer, "fsdp", split_axis=1, concat_axis=0, tiled=True)
        return back.reshape(n_experts * capacity, back.shape[2])

    qkv_full, out_full = (
        lax.all_gather(w_qkv, "fsdp", axis=1, tiled=True),
        lax.all_gather(w_out, "fsdp", axis=1, tiled=True),
    )
    router_full, gains_full = (
        lax.all_gather(w_router, ("fsdp", "tp"), axis=0, tiled=True),
        lax.all_gather(norm_gains, ("fsdp", "tp"), axis=1, tiled=True),
    )
    gains_wide = gains_full.astype(jnp.float32)
    col_start = tp_rank * head_cols
    gain_query = lax.dynamic_slice_in_dim(gains_wide[2], col_start, head_cols)
    gain_key = lax.dynamic_slice_in_dim(gains_wide[3], col_start, head_cols)
    segment = seg_ids[0]
    padding = pad_mask[0]
    cosine, sine = rope_tables(seq_len, HD)
    x_own = tokens.astype(jnp.float32)
    normed1, scale1 = norm_forward(x_own, gains_wide[0])
    rows1 = gather_rows(normed1.astype(jnp.bfloat16))
    projected = jnp.einsum("sd,cdh->csh", rows1, qkv_full, preferred_element_type=jnp.float32)
    query_raw = projected[0]
    key_raw = projected[1]
    square_q, square_k = tp_totals(
        jnp.sum(query_raw * query_raw, axis=-1), jnp.sum(key_raw * key_raw, axis=-1)
    )
    scale_q = lax.rsqrt(square_q / width + EPSILON)[:, None]
    scale_k = lax.rsqrt(square_k / width + EPSILON)[:, None]
    unit_q = query_raw * scale_q
    unit_k = key_raw * scale_k
    queries = rotate((unit_q * gain_query).reshape(seq_len, heads_local, HD), cosine, sine).astype(
        jnp.bfloat16
    )
    keys = rotate((unit_k * gain_key).reshape(seq_len, heads_local, HD), cosine, sine).astype(
        jnp.bfloat16
    )
    values = projected[2].astype(jnp.bfloat16).reshape(seq_len, heads_local, HD)
    block_starts = jnp.arange(n_blocks, dtype=jnp.int32) * block_rows

    def block_scores(start):
        raw_scores = (
            jnp.einsum("qhd,khd->hqk", queries, keys, preferred_element_type=jnp.float32)
            * score_scale
        )
        allowed = allowed_mask(segment, padding, start, block_rows)
        return (queries, jnp.where(allowed[None], raw_scores, NEG_FILL), allowed)

    def attend(start):
        query_block, scores, allowed = block_scores(start)
        peak = jnp.max(scores, axis=-1, keepdims=True)
        powered = jnp.exp(scores - peak)
        total = jnp.sum(powered, axis=-1, keepdims=True)
        probs_low = (powered / total).astype(jnp.bfloat16)
        mixed_block = jnp.einsum(
            "hqk,khd->qhd", probs_low, values, preferred_element_type=jnp.float32
        )
        return (
            mixed_block.reshape(block_rows, head_cols).astype(jnp.bfloat16),
            (peak + jnp.log(total))[..., 0],
        )

    mixed_blocks, log_sums = lax.map(attend, block_starts)
    mixed = mixed_blocks.reshape(seq_len, head_cols)
    hidden = x_own + scatter_rows(jnp.dot(mixed, out_full, preferred_element_type=jnp.float32))
    normed2, scale2 = norm_forward(hidden, gains_wide[1])
    own_normed2 = normed2.astype(jnp.bfloat16)
    rows2 = gather_rows(own_normed2)
    logits = jnp.dot(rows2, router_full, preferred_element_type=jnp.float32)
    router_probs = jax.nn.softmax(logits, axis=-1)
    gates = jnp.take_along_axis(router_probs, expert_ids, axis=1)
    flat_index, source = route_slots(expert_ids, n_experts, capacity)
    padded_rows = jnp.concatenate([rows2, jnp.zeros((1, width), jnp.bfloat16)], axis=0)
    received = send_experts(padded_rows[source].reshape(n_experts, capacity, width))
    w_pair = jnp.concatenate([w_gate, w_up], axis=2)
    pair_pre = jnp.einsum("erd,edf->erf", received, w_pair, preferred_element_type=jnp.float32)
    gate_pre = pair_pre[..., :ff_local]
    up_pre = pair_pre[..., ff_local:]
    sigmoid_gate = jax.nn.sigmoid(gate_pre)
    silu_gate = gate_pre * sigmoid_gate
    active = (silu_gate * up_pre).astype(jnp.bfloat16)
    expert_part = jnp.einsum(
        "erf,efd->erd", active, w_down, preferred_element_type=jnp.float32
    ).astype(jnp.bfloat16)
    returned = return_experts(expert_part)
    combined = jnp.zeros((seq_len, returned.shape[1]), jnp.float32)
    for pick_rank in range(top_count):
        combined = combined + gates[:, pick_rank : pick_rank + 1] * returned[
            flat_index[:, pick_rank]
        ].astype(jnp.float32)
    layer_out = (hidden + scatter_rows(combined)).astype(jnp.bfloat16)
    grad_rows = gather_rows(cotangent)
    grad_cols = grad_rows.astype(jnp.float32)
    partial_dots = jnp.stack(
        [
            jnp.sum(returned[flat_index[:, pick_rank]].astype(jnp.float32) * grad_cols, axis=-1)
            for pick_rank in range(top_count)
        ],
        axis=1,
    )
    gate_dots = lax.psum(partial_dots, "tp")
    expert_range = jnp.arange(n_experts, dtype=jnp.int32)
    chosen = jnp.sum(
        gate_dots[:, :, None]
        * (expert_ids[:, :, None] == expert_range[None, None, :]).astype(jnp.float32),
        axis=1,
    )
    weighted = jnp.sum(gates * gate_dots, axis=-1, keepdims=True)
    logit_grad = (router_probs * (chosen - weighted)).astype(jnp.bfloat16)
    own_logit_grad = lax.dynamic_slice_in_dim(logit_grad, tp_rank * local_rows, local_rows, 0)
    slot_gates = (
        jnp.zeros((n_experts * capacity,), jnp.float32)
        .at[flat_index.reshape(-1)]
        .set(gates.reshape(-1))
    )
    padded_grads = jnp.concatenate([grad_rows, jnp.zeros((1, width), jnp.bfloat16)], axis=0)
    slot_grads = (padded_grads[source].astype(jnp.float32) * slot_gates[:, None]).astype(
        jnp.bfloat16
    )
    grad_received = send_experts(slot_grads.reshape(n_experts, capacity, width))
    active_grad = jnp.einsum(
        "erd,efd->erf", grad_received, w_down, preferred_element_type=jnp.float32
    )
    gate_grad = (
        active_grad * up_pre * sigmoid_gate * (1.0 + gate_pre * (1.0 - sigmoid_gate))
    ).astype(jnp.bfloat16)
    up_grad = (active_grad * silu_gate).astype(jnp.bfloat16)
    pair_grad = jnp.concatenate([gate_grad, up_grad], axis=2)
    grad_down = jnp.einsum(
        "erf,erd->efd", active, grad_received, preferred_element_type=jnp.float32
    )
    grad_pair = jnp.einsum("erd,erf->edf", received, pair_grad, preferred_element_type=jnp.float32)
    grad_gate = grad_pair[..., :ff_local]
    grad_up = grad_pair[..., ff_local:]
    input_part = jnp.einsum(
        "erf,edf->erd", pair_grad, w_pair, preferred_element_type=jnp.float32
    ).astype(jnp.bfloat16)
    sent_back = return_experts(input_part)
    token_grad = jnp.zeros((seq_len, sent_back.shape[1]), jnp.float32)
    for pick_rank in range(top_count):
        token_grad = token_grad + sent_back[flat_index[:, pick_rank]].astype(jnp.float32)
    normed2_grad = scatter_rows(token_grad) + jnp.dot(
        own_logit_grad, router_full.T, preferred_element_type=jnp.float32
    )
    hidden_norm_grad, gain2_grad = norm_backward(hidden, scale2, gains_wide[1], normed2_grad)
    hidden_grad = cotangent.astype(jnp.float32) + hidden_norm_grad
    router_grad = jnp.dot(own_normed2.T, own_logit_grad, preferred_element_type=jnp.float32)
    hidden_rows = gather_rows(hidden_grad.astype(jnp.bfloat16))
    grad_out_full = jnp.dot(mixed.T, hidden_rows, preferred_element_type=jnp.float32)
    mixed_grad = (
        jnp.dot(hidden_rows, out_full.T, preferred_element_type=jnp.float32)
        .astype(jnp.bfloat16)
        .reshape(seq_len, heads_local, HD)
    )

    def attend_back(carried, pieces):
        key_acc, value_acc = carried
        start, log_sum = pieces
        query_block, scores, allowed = block_scores(start)
        probs = jnp.where(allowed[None], jnp.exp(scores - log_sum[:, :, None]), 0.0)
        prob_grad = jnp.einsum(
            "qhd,khd->hqk", mixed_grad, values, preferred_element_type=jnp.float32
        )
        delta = jnp.sum(probs * prob_grad, axis=-1, keepdims=True)
        score_grad = (probs * (prob_grad - delta)).astype(jnp.bfloat16)
        query_block_grad = (
            jnp.einsum("hqk,khd->qhd", score_grad, keys, preferred_element_type=jnp.float32)
            * score_scale
        )
        key_acc = (
            key_acc
            + jnp.einsum(
                "hqk,qhd->khd", score_grad, query_block, preferred_element_type=jnp.float32
            )
            * score_scale
        )
        value_acc = value_acc + jnp.einsum(
            "hqk,qhd->khd",
            probs.astype(jnp.bfloat16),
            mixed_grad,
            preferred_element_type=jnp.float32,
        )
        return ((key_acc, value_acc), query_block_grad)

    zero_heads = jnp.zeros((seq_len, heads_local, HD), jnp.float32)
    (key_grad, value_grad), query_blocks = lax.scan(
        attend_back, (zero_heads, zero_heads), (block_starts, log_sums)
    )
    query_grad = query_blocks.reshape(seq_len, heads_local, HD)
    query_norm_grad = rotate_back(query_grad, cosine, sine).reshape(seq_len, head_cols)
    key_norm_grad = rotate_back(key_grad, cosine, sine).reshape(seq_len, head_cols)
    gain_query_grad = jnp.sum(query_norm_grad * unit_q, axis=0)
    gain_key_grad = jnp.sum(key_norm_grad * unit_k, axis=0)
    scaled_q = query_norm_grad * gain_query
    scaled_k = key_norm_grad * gain_key
    inner_q, inner_k = tp_totals(
        jnp.sum(scaled_q * unit_q, axis=-1), jnp.sum(scaled_k * unit_k, axis=-1)
    )
    query_raw_grad = scale_q * (scaled_q - unit_q * (inner_q / width)[:, None])
    key_raw_grad = scale_k * (scaled_k - unit_k * (inner_k / width)[:, None])
    qkv_grad = jnp.stack(
        [query_raw_grad, key_raw_grad, value_grad.reshape(seq_len, head_cols)]
    ).astype(jnp.bfloat16)
    grad_qkv_full = jnp.einsum("sd,csh->cdh", rows1, qkv_grad, preferred_element_type=jnp.float32)
    normed1_part = jnp.einsum("csh,cdh->sd", qkv_grad, qkv_full, preferred_element_type=jnp.float32)
    normed1_grad = scatter_rows(normed1_part)
    input_norm_grad, gain1_grad = norm_backward(x_own, scale1, gains_wide[0], normed1_grad)
    input_grad = hidden_grad + input_norm_grad
    zero_width = jnp.zeros((width,), jnp.float32)
    gains_grad = jnp.stack(
        [
            gain1_grad,
            gain2_grad,
            lax.dynamic_update_slice_in_dim(zero_width, gain_query_grad, col_start, 0),
            lax.dynamic_update_slice_in_dim(zero_width, gain_key_grad, col_start, 0),
        ]
    )
    grad_qkv, grad_out = (
        lax.psum_scatter(
            grad_qkv_full.astype(jnp.bfloat16), "fsdp", scatter_dimension=1, tiled=True
        ).astype(jnp.float32),
        lax.psum_scatter(
            grad_out_full.astype(jnp.bfloat16), "fsdp", scatter_dimension=1, tiled=True
        ).astype(jnp.float32),
    )
    grad_router, grad_gains = (
        lax.psum_scatter(router_grad, ("fsdp", "tp"), scatter_dimension=0, tiled=True),
        lax.psum_scatter(gains_grad, ("fsdp", "tp"), scatter_dimension=1, tiled=True),
    )
    return (
        layer_out,
        input_grad,
        grad_qkv,
        grad_out,
        grad_router,
        grad_gains,
        grad_gate,
        grad_up,
        grad_down,
    )


GRID = (4, 2, 2, 2)
FINE = ("z", "x", "y", "core")
LANES = 128
CONTRACT_LAST = (((1,), (1,)), ((), ()))


def permutation(target):
    def place(z, x, y, c):
        return ((z * GRID[1] + x) * GRID[2] + y) * GRID[3] + c

    return [
        (place(*at), place(*target(*at))) for at in itertools.product(*(range(n) for n in GRID))
    ]


SWAP_CORE = permutation(lambda z, x, y, c: (z, x, y, 1 - c))
SWAP_X = permutation(lambda z, x, y, c: (z, 1 - x, y, c))
SWAP_Y = permutation(lambda z, x, y, c: (z, x, 1 - y, c))
SWAP_BOTH = permutation(lambda z, x, y, c: (z, x, 1 - y, 1 - c))
SWAP_FIRST = permutation(lambda z, x, y, c: (z, 1 - x, y, c) if c == 0 else (z, x, 1 - y, c))
SWAP_SECOND = permutation(lambda z, x, y, c: (z, x, 1 - y, c) if c == 0 else (z, 1 - x, y, c))


def shift_z(steps):
    return permutation(lambda z, x, y, c: ((z + steps) % GRID[0], x, y, c))


def send(values, pairs):
    return lax.ppermute(values, FINE, pairs)


def add_low(*terms):
    return sum(term.astype(jnp.float32) for term in terms).astype(jnp.bfloat16)


def side_totals(first, second):
    return lax.psum((first, second), FINE[2:])


def fence(*values):
    return lax.optimization_barrier(values)


def wide_sum(*terms):
    return sum(term.astype(jnp.float32) for term in terms)


def pair_dots(left, right):
    return lax.dot_general(left, right, (((0,), (0,)), ((), ())), preferred_element_type=jnp.float32)


def side_pair(own, far):
    is_far = lax.axis_index("y") == 1
    return jnp.stack([jnp.where(is_far, far, own), jnp.where(is_far, own, far)])


def four_rows(mine, theirs):
    is_second = lax.axis_index("core") == 1
    both = jnp.stack(
        [jnp.where(is_second, theirs, mine), jnp.where(is_second, mine, theirs)], axis=1
    )
    return both.reshape(4 * mine.shape[1], *mine.shape[2:])


def core_split(values):
    core = lax.axis_index("core")
    blocks = values.astype(jnp.bfloat16).reshape(2, 2, values.shape[0] // 4, values.shape[1])
    return (
        lax.dynamic_index_in_dim(blocks, 1 - core, 1, keepdims=False),
        lax.dynamic_index_in_dim(blocks, core, 1, keepdims=False),
    )


def side_split(mine, back):
    side = lax.axis_index("y")

    def at(pair, which):
        return lax.dynamic_index_in_dim(pair, which, 0, keepdims=False)

    away = add_low(at(mine, 1 - side), at(back, 1 - side))
    return (away, wide_sum(at(mine, side), at(back, side)))


def expert_kernel(
    blocks_ref,
    near_ref,
    far_ref,
    grads0_ref,
    grads1_ref,
    grads2_ref,
    grads3_ref,
    router_ref,
    place_ref,
    *refs,
    n_experts,
    at,
    n_before,
):
    weight_refs, refs = refs[:6], refs[6 + n_before :]
    near_route_ref, far_route_ref, active_ref, hidden_ref, dots_ref, grads_ref, rows_ref = refs[:7]
    gate_buf, up_buf, down_buf, active_buf, hidden_buf, rows_buf, grads_buf, in_sems, out_sems = refs[7:]
    exp_local, width = place_ref.shape[0], near_ref.shape[1]
    units = gate_buf.shape[2]
    half = near_ref.shape[0]
    count = 2 * half
    buffers = (gate_buf, up_buf, down_buf)

    def fetch(slot, kind):
        group, expert = slot // exp_local, slot % exp_local
        return pltpu.make_async_copy(
            weight_refs[3 * group + kind].at[expert], buffers[kind].at[slot], in_sems.at[slot, kind]
        )

    slots = 2 * exp_local
    for slot in range(slots):
        for kind in range(3):
            fetch(slot, kind).start()
    rows_buf[:half] = near_ref[...]
    rows_buf[half:] = far_ref[...]
    quarter = half // 2
    grad_refs = (grads0_ref, grads1_ref, grads2_ref, grads3_ref)
    for block, ref in enumerate(grad_refs):
        grads_buf[block * quarter : (block + 1) * quarter] = ref[:, :width]

    def round_rows(ref):
        return ref.at[pl.ds(at * count, count)]

    stores = [
        pltpu.make_async_copy(rows_buf, round_rows(rows_ref), out_sems.at[0]),
        pltpu.make_async_copy(grads_buf, round_rows(grads_ref), out_sems.at[1]),
    ]
    for store in stores:
        store.start()
    named = jnp.concatenate([ref[:, width:] for ref in grad_refs], axis=0)
    rows = rows_buf[...]
    grads = grads_buf[...]
    lane = lax.broadcasted_iota(jnp.int32, (1, LANES), 1)
    logits = jnp.dot(rows, router_ref[...], preferred_element_type=jnp.float32)
    logits = jnp.where(lane < n_experts, logits, NEG_FILL)
    powered = jnp.exp(logits - jnp.max(logits, axis=-1, keepdims=True))
    gates = powered / jnp.sum(powered, axis=-1, keepdims=True) * named.astype(jnp.float32)
    route = None
    dots = jnp.zeros(logits.shape, jnp.float32)
    for slot in range(slots):
        expert = slot % exp_local
        place = place_ref[expert : expert + 1, :]
        gate = jnp.sum(gates * place, axis=-1, keepdims=True)
        for kind in range(3):
            fetch(slot, kind).wait()
        gate_pre = jnp.dot(rows, gate_buf[slot], preferred_element_type=jnp.float32)
        up_pre = jnp.dot(rows, up_buf[slot], preferred_element_type=jnp.float32)
        y_down = lax.dot_general(
            grads, down_buf[slot], CONTRACT_LAST, preferred_element_type=jnp.float32
        )
        sigmoid = 1.0 / (1.0 + jnp.exp(-gate_pre))
        silu = gate_pre * sigmoid
        active = silu * up_pre
        dots = dots + jnp.sum(active * y_down, axis=-1, keepdims=True) * place
        active_buf[slot] = (active * gate).astype(jnp.bfloat16)
        active_grad = y_down * gate
        gate_grad = (active_grad * up_pre * sigmoid * (1.0 + gate_pre * (1.0 - sigmoid))).astype(
            jnp.bfloat16
        )
        up_grad = (active_grad * silu).astype(jnp.bfloat16)
        hidden_buf[slot, :, :units] = gate_grad
        hidden_buf[slot, :, units:] = up_grad
        for buf, ref, columns, sem in (
            (active_buf, active_ref, units, 2 + 2 * slot),
            (hidden_buf, hidden_ref, 2 * units, 3 + 2 * slot),
        ):
            store = pltpu.make_async_copy(
                buf.at[slot],
                ref.at[pl.ds(at * count, count), pl.ds(slot * columns, columns)],
                out_sems.at[sem],
            )
            store.start()
            stores.append(store)
        part = lax.dot_general(
            gate_grad, gate_buf[slot], CONTRACT_LAST, preferred_element_type=jnp.float32
        ) + lax.dot_general(
            up_grad, up_buf[slot], CONTRACT_LAST, preferred_element_type=jnp.float32
        )
        route = part if route is None else route + part
    near_route_ref[...] = route[:half].astype(jnp.bfloat16)
    far_route_ref[...] = route[half:].astype(jnp.bfloat16)
    dots_ref[...] = jnp.transpose(dots)[:n_experts]
    for store in stores:
        store.wait()


def expert_rows(at, before, blocks, near, far, all_grads, router, place, own, other, n_experts):
    half, width = near.shape
    count = 2 * half
    exp_local, _, units = own[0].shape
    slots = 2 * exp_local
    wide = all_grads.shape[1]

    def whole(array):
        return pl.BlockSpec(
            array.shape, lambda step, blocks: (0,) * array.ndim, pipeline_mode=pl.Buffered(1)
        )

    def picked(row):
        return pl.BlockSpec(
            (count // 4, wide), lambda step, blocks: (blocks[row], 0), pipeline_mode=pl.Buffered(1)
        )

    def first_block(shape):
        return pl.BlockSpec(shape, lambda step, blocks: (0, 0))

    def rounds(columns):
        return jax.ShapeDtypeStruct((GRID[0] * count, columns), jnp.bfloat16)

    anywhere = pl.BlockSpec(memory_space=pl.ANY)
    inputs = (blocks, near, far, *(all_grads for _ in range(4)), router, place, *own, *other, *before)
    order = (2, 3, 5, 6)
    route = jax.ShapeDtypeStruct((half, width), jnp.bfloat16)
    return pl.pallas_call(
        functools.partial(expert_kernel, n_experts=n_experts, at=at, n_before=len(before)),
        out_shape=[
            route,
            route,
            rounds(slots * units),
            rounds(2 * slots * units),
            jax.ShapeDtypeStruct((n_experts, count), jnp.float32),
            rounds(width),
            rounds(width),
        ],
        grid_spec=pltpu.PrefetchScalarGridSpec(
            num_scalar_prefetch=1,
            grid=(1,),
            in_specs=[
                whole(near),
                whole(far),
                *(picked(row) for row in range(4)),
                whole(router),
                whole(place),
                *(anywhere for _ in range(6 + len(before))),
            ],
            out_specs=[
                first_block((half, width)),
                first_block((half, width)),
                anywhere,
                anywhere,
                first_block((n_experts, count)),
                anywhere,
                anywhere,
            ],
            scratch_shapes=[
                pltpu.VMEM((slots, width, units), jnp.bfloat16),
                pltpu.VMEM((slots, width, units), jnp.bfloat16),
                pltpu.VMEM((slots, units, width), jnp.bfloat16),
                pltpu.VMEM((slots, count, units), jnp.bfloat16),
                pltpu.VMEM((slots, count, 2 * units), jnp.bfloat16),
                pltpu.VMEM((count, width), jnp.bfloat16),
                pltpu.VMEM((count, width), jnp.bfloat16),
                pltpu.SemaphoreType.DMA((slots, 3)),
                pltpu.SemaphoreType.DMA((2 + 2 * slots,)),
            ],
        ),
        input_output_aliases={
            len(inputs) - len(before) + index: order[index] for index in range(len(before))
        },
        cost_estimate=pl.CostEstimate(flops=1024, bytes_accessed=1024, transcendentals=0),
        compiler_params=pltpu.CompilerParams(
            dimension_semantics=("arbitrary",), vmem_limit_bytes=46 * 1024 * 1024
        ),
        name="expert_rows",
    )(*inputs)


def turned(values, cosine, sine):
    return values * cosine + pltpu.roll(values, HD // 2, 1) * sine


def allowed_pairs(segment_col_ref, segment_row_ref, padding_ref):
    count = segment_col_ref.shape[0]
    row = lax.broadcasted_iota(jnp.int32, (count, count), 0)
    col = lax.broadcasted_iota(jnp.int32, (count, count), 1)
    usable = (padding_ref[...] == 1) | (col == row)
    return (segment_col_ref[...] == segment_row_ref[...]) & (col <= row) & usable


def attend_kernel(
    projected_ref,
    scale_q_ref,
    scale_k_ref,
    gain_q_ref,
    gain_k_ref,
    cosine_ref,
    sine_ref,
    segment_col_ref,
    segment_row_ref,
    padding_ref,
    mixed_ref,
    queries_ref,
    keys_ref,
    values_ref,
    log_sum_ref,
):
    width = mixed_ref.shape[1]
    allowed = allowed_pairs(segment_col_ref, segment_row_ref, padding_ref)
    cosine, sine = cosine_ref[...], sine_ref[...]
    scale_q, scale_k = scale_q_ref[...], scale_k_ref[...]
    for head in range(width // HD):
        at = slice(head * HD, (head + 1) * HD)
        raw_q = projected_ref[:, head * HD : (head + 1) * HD]
        raw_k = projected_ref[:, width + head * HD : width + (head + 1) * HD]
        raw_v = projected_ref[:, 2 * width + head * HD : 2 * width + (head + 1) * HD]
        queries = turned(raw_q * scale_q * gain_q_ref[:, at], cosine, sine).astype(jnp.bfloat16)
        keys = turned(raw_k * scale_k * gain_k_ref[:, at], cosine, sine).astype(jnp.bfloat16)
        values = raw_v.astype(jnp.bfloat16)
        scores = (
            lax.dot_general(queries, keys, CONTRACT_LAST, preferred_element_type=jnp.float32)
            * HD ** (-0.5)
        )
        scores = jnp.where(allowed, scores, NEG_FILL)
        peak = jnp.max(scores, axis=-1, keepdims=True)
        powered = jnp.exp(scores - peak)
        total = jnp.sum(powered, axis=-1, keepdims=True)
        probs_low = (powered / total).astype(jnp.bfloat16)
        mixed_ref[:, at] = jnp.dot(
            probs_low, values, preferred_element_type=jnp.float32
        ).astype(jnp.bfloat16)
        queries_ref[:, at] = queries
        keys_ref[:, at] = keys
        values_ref[:, at] = values
        log_sum_ref[:, head : head + 1] = peak + jnp.log(total)


def attend_back_kernel(
    hidden_ref,
    out_ref,
    queries_ref,
    keys_ref,
    values_ref,
    log_sum_ref,
    projected_ref,
    scale_q_ref,
    scale_k_ref,
    gain_q_ref,
    gain_k_ref,
    cosine_ref,
    sine_ref,
    segment_col_ref,
    segment_row_ref,
    padding_ref,
    scaled_q_ref,
    scaled_k_ref,
    value_grad_ref,
    inner_ref,
    gain_grad_ref,
):
    width = queries_ref.shape[1]
    allowed = allowed_pairs(segment_col_ref, segment_row_ref, padding_ref)
    cosine, sine = cosine_ref[...], sine_ref[...]
    mixed_grad_all = jnp.dot(
        hidden_ref[...], out_ref[...], preferred_element_type=jnp.float32
    ).astype(jnp.bfloat16)
    contract_rows = (((0,), (0,)), ((), ()))
    inner_q = jnp.zeros((queries_ref.shape[0], 1), jnp.float32)
    inner_k = jnp.zeros((queries_ref.shape[0], 1), jnp.float32)
    for head in range(width // HD):
        at = slice(head * HD, (head + 1) * HD)
        queries, keys, values = queries_ref[:, at], keys_ref[:, at], values_ref[:, at]
        mixed_grad = mixed_grad_all[:, at]
        scores = (
            lax.dot_general(queries, keys, CONTRACT_LAST, preferred_element_type=jnp.float32)
            * HD ** (-0.5)
        )
        powered = jnp.exp(jnp.where(allowed, scores, NEG_FILL) - log_sum_ref[:, head : head + 1])
        probs = jnp.where(allowed, powered, 0.0)
        prob_grad = lax.dot_general(
            mixed_grad, values, CONTRACT_LAST, preferred_element_type=jnp.float32
        )
        delta = jnp.sum(probs * prob_grad, axis=-1, keepdims=True)
        score_grad = (probs * (prob_grad - delta)).astype(jnp.bfloat16)
        query_grad = jnp.dot(score_grad, keys, preferred_element_type=jnp.float32) * HD ** (-0.5)
        key_grad = lax.dot_general(
            score_grad, queries, contract_rows, preferred_element_type=jnp.float32
        ) * HD ** (-0.5)
        value_grad_ref[:, at] = lax.dot_general(
            probs.astype(jnp.bfloat16),
            mixed_grad,
            contract_rows,
            preferred_element_type=jnp.float32,
        ).astype(jnp.bfloat16)
        query_grad = turned(query_grad, cosine, -sine)
        key_grad = turned(key_grad, cosine, -sine)
        unit_q = projected_ref[:, head * HD : (head + 1) * HD] * scale_q_ref[...]
        unit_k = projected_ref[:, width + head * HD : width + (head + 1) * HD] * scale_k_ref[...]
        gain_grad_ref[0:1, at] = jnp.sum(query_grad * unit_q, axis=0, keepdims=True)
        gain_grad_ref[1:2, at] = jnp.sum(key_grad * unit_k, axis=0, keepdims=True)
        scaled_q = query_grad * gain_q_ref[:, at]
        scaled_k = key_grad * gain_k_ref[:, at]
        scaled_q_ref[:, at] = scaled_q
        scaled_k_ref[:, at] = scaled_k
        inner_q += jnp.sum(scaled_q * unit_q, axis=-1, keepdims=True)
        inner_k += jnp.sum(scaled_k * unit_k, axis=-1, keepdims=True)
    inner_ref[:, 0:1] = inner_q
    inner_ref[:, 1:2] = inner_k


def small_call(kernel, shapes, name):
    return pl.pallas_call(
        kernel,
        out_shape=[jax.ShapeDtypeStruct(shape, dtype) for shape, dtype in shapes],
        cost_estimate=pl.CostEstimate(flops=1024, bytes_accessed=1024, transcendentals=0),
        compiler_params=pltpu.CompilerParams(vmem_limit_bytes=40 * 1024 * 1024),
        name=name,
    )


def dense_shards(
    tokens,
    seg_ids,
    pad_mask,
    expert_ids,
    w_qkv,
    w_out,
    w_router,
    norm_gains,
    w_gate,
    w_up,
    w_down,
    cotangent,
):
    z, x, y, core = (lax.axis_index(name) for name in FINE)
    fsdp_rank = z * GRID[1] + x
    tp_rank = y * GRID[3] + core
    local_rows, width = tokens.shape
    seq_len = seg_ids.shape[1]
    exp_local, _, ff_local = w_gate.shape
    n_experts = w_router.shape[1]
    head_cols = w_qkv.shape[2]
    own_start = tp_rank * local_rows
    small_cols = norm_gains.shape[1]
    fsdp = FINE[:2]

    def own_rows(values):
        return lax.dynamic_slice_in_dim(values, own_start, local_rows, 0)

    tp_swaps = (SWAP_CORE, SWAP_Y, SWAP_BOTH)
    z_shifts = [shift_z(steps) for steps in range(1, GRID[0])]
    small_own = jnp.pad(
        jnp.concatenate([w_router, norm_gains.T], axis=1), ((0, 0), (0, LANES - n_experts - 4))
    )
    small = lax.dynamic_update_slice_in_dim(
        jnp.zeros((w_qkv.shape[1], LANES), jnp.bfloat16), small_own, tp_rank * small_cols, 0
    )
    smalls, tokens_own = fence([send(small, swap) for swap in tp_swaps], tokens)
    small = small + smalls[0] + smalls[1] + smalls[2]
    weights_own = jnp.concatenate(
        [w_qkv.transpose(1, 0, 2).reshape(w_qkv.shape[1], -1), small], axis=1
    )
    weights_full = lax.all_gather(weights_own, fsdp, axis=0, tiled=True)
    block = w_out.shape[1]
    out_full = jnp.zeros((width, w_out.shape[0]), jnp.bfloat16)
    out_column, tokens_own = fence(w_out.T, tokens_own)
    for steps in range(GRID[0]):
        out_beside = send(out_column, SWAP_X)
        for piece_x, piece_values in ((x, out_column), (1 - x, out_beside)):
            start = ((z - steps) % GRID[0] * GRID[1] + piece_x) * block
            out_full = lax.dynamic_update_slice_in_dim(out_full, piece_values, start, 0)
        if steps < GRID[0] - 1:
            out_column = send(out_column, z_shifts[0])
    names = jnp.arange(n_experts, dtype=jnp.int32)
    own_ids = own_rows(expert_ids)
    named = (own_ids[:, :, None] == names[None, None, :]).any(axis=1)
    named_wide = jnp.pad(named.astype(jnp.bfloat16), ((0, 0), (0, LANES - n_experts)))
    grads_own = jnp.concatenate([cotangent, named_wide], axis=1)
    far = send(tokens_own, SWAP_Y)
    mine = side_pair(tokens, far)
    theirs = send(mine, SWAP_CORE)
    rows_x = four_rows(mine, theirs).astype(jnp.float32)
    scale1 = lax.rsqrt(jnp.mean(rows_x * rows_x, axis=-1, keepdims=True) + EPSILON)
    own_weights = (w_gate, w_up, w_down)
    grads_own, weights_own, weights_full, scale1, rows_x, out_full = fence(
        grads_own, own_weights, weights_full, scale1, rows_x, out_full
    )
    all_grads_abs = lax.all_gather(grads_own, FINE[:3], axis=0, tiled=True)
    other_weights = tuple(send(weight, SWAP_CORE) for weight in weights_own)
    qkv_full = weights_full[:, : 3 * head_cols]
    router_wide = weights_full[:, 3 * head_cols :]
    router_full = router_wide[:, :n_experts]
    gains_wide = router_wide[:, n_experts : n_experts + 4].T.astype(jnp.float32)

    cosine, sine = (table[:, 0] for table in rope_tables(seq_len, HD))
    turns = (
        jnp.concatenate([cosine, cosine], axis=1),
        jnp.concatenate([-sine, sine], axis=1),
        seg_ids.T,
        seg_ids,
        pad_mask,
    )
    x_own = tokens.astype(jnp.float32)
    col_start = tp_rank * head_cols
    gain_query = lax.dynamic_slice_in_dim(gains_wide[2], col_start, head_cols)
    gain_key = lax.dynamic_slice_in_dim(gains_wide[3], col_start, head_cols)
    rows1 = (rows_x * scale1 * gains_wide[0]).astype(jnp.bfloat16)
    projected = jnp.dot(rows1, qkv_full, preferred_element_type=jnp.float32)
    query_raw = projected[:, :head_cols]
    key_raw = projected[:, head_cols : 2 * head_cols]
    squares = side_totals(
        jnp.sum(query_raw * query_raw, axis=-1), jnp.sum(key_raw * key_raw, axis=-1)
    )
    scale_q = lax.rsqrt(squares[0] / width + EPSILON)[:, None]
    scale_k = lax.rsqrt(squares[1] / width + EPSILON)[:, None]
    low_heads = ((seq_len, head_cols), jnp.bfloat16)
    wide_heads = ((seq_len, head_cols), jnp.float32)
    norms = (scale_q, scale_k, gain_query[None], gain_key[None])
    mixed, queries, keys, values, log_sums = small_call(
        attend_kernel, [low_heads] * 4 + [((seq_len, LANES), jnp.float32)], "attend"
    )(projected, *norms, *turns)
    away, mine = core_split(
        lax.dot_general(mixed, out_full, CONTRACT_LAST, preferred_element_type=jnp.float32)
    )
    away, kept = side_split(mine, send(away, SWAP_CORE))
    far, kept = fence(send(away, SWAP_Y), kept)
    hidden = x_own + kept + far
    normed2, scale2 = norm_forward(hidden, gains_wide[1])
    own_normed2 = normed2.astype(jnp.bfloat16)

    place = (
        jnp.arange(LANES)[None, :] == fsdp_rank * exp_local + jnp.arange(exp_local)[:, None]
    ).astype(jnp.float32)
    rows, rows_near, rows_far = [own_normed2], [], []
    results, seconds, firsts, homes = [], [], [], []

    def hop(column):
        return send(column, z_shifts[0])

    def experts(at):
        beside = jnp.where(core == 0, (1 - x) * GRID[2] + y, x * GRID[2] + 1 - y)
        across = jnp.where(core == 0, x * GRID[2] + 1 - y, (1 - x) * GRID[2] + y)
        opposite = (1 - x) * GRID[2] + 1 - y
        plane = (z - at) % GRID[0] * (GRID[1] * GRID[2])
        blocks = plane + jnp.stack([x * GRID[2] + y, beside, across, opposite])
        before = [results[at - 1][index] for index in (2, 3, 5, 6)] if at else []
        return expert_rows(
            at,
            before,
            blocks.astype(jnp.int32),
            rows_near[at],
            rows_far[at],
            all_grads_abs,
            router_wide,
            place,
            own_weights,
            other_weights,
            n_experts,
        )

    def near_of(at, arrived):
        return jnp.concatenate([rows[at], arrived], axis=0)

    def first_part(near, second):
        half = near.shape[0] // 2
        return add_low(near[half:], second[half:])

    def mine_part(near, second, first):
        half = near.shape[0] // 2
        return wide_sum(near[:half], second[:half], first)

    def route_first(at):
        return send(first_part(results[at][0], seconds[at]), SWAP_FIRST)

    def route_home(at):
        mine = mine_part(results[at][0], seconds[at], firsts[at])
        return send(mine.astype(jnp.bfloat16), z_shifts[GRID[0] - 1 - at])

    hopped, arrived = fence(hop(rows[0]), send(rows[0], SWAP_FIRST))
    rows.append(hopped)
    rows_near.append(near_of(0, arrived))
    hopped, arrived, second = fence(
        hop(rows[1]), send(rows[1], SWAP_FIRST), send(rows_near[0], SWAP_SECOND)
    )
    rows.append(hopped)
    rows_near.append(near_of(1, arrived))
    rows_far.append(second)
    hopped, arrived, second, result = fence(
        hop(rows[2]), send(rows[2], SWAP_FIRST), send(rows_near[1], SWAP_SECOND), experts(0)
    )
    rows.append(hopped)
    rows_near.append(near_of(2, arrived))
    rows_far.append(second)
    results.append(result)
    arrived, second, back, result = fence(
        send(rows[3], SWAP_FIRST),
        send(rows_near[2], SWAP_SECOND),
        send(results[0][1], SWAP_SECOND),
        experts(1),
    )
    rows_near.append(near_of(3, arrived))
    rows_far.append(second)
    seconds.append(back)
    results.append(result)
    second, back, first, result = fence(
        send(rows_near[3], SWAP_SECOND),
        send(results[1][1], SWAP_SECOND),
        route_first(0),
        experts(2),
    )
    rows_far.append(second)
    seconds.append(back)
    firsts.append(first)
    results.append(result)
    back, first, result = fence(
        send(results[2][1], SWAP_SECOND), route_first(1), experts(3)
    )
    seconds.append(back)
    firsts.append(first)
    results.append(result)
    homes.append(mine_part(results[0][0], seconds[0], firsts[0]))

    dots = jnp.stack([result[4] for result in results])
    part = dots.shape[-1] // 4
    all_active, all_hidden, all_grads, all_rows = (results[-1][index] for index in (2, 3, 5, 6))
    down_rows = jnp.concatenate(
        [weights[2].reshape(-1, width) for weights in (own_weights, other_weights)]
    )
    back, first, home, dots_back, dots, all_active, down_rows, all_hidden = fence(
        send(results[3][1], SWAP_SECOND),
        route_first(2),
        route_home(1),
        send(dots[..., 2 * part :], SWAP_SECOND),
        dots,
        all_active,
        down_rows,
        all_hidden,
    )
    seconds.append(back)
    firsts.append(first)
    homes.append(home)
    dots = dots[..., : 2 * part] + dots_back
    units = exp_local * ff_local
    pair_count = 2 * exp_local

    def piece(at):
        return all_hidden[:, at * ff_local : (at + 1) * ff_local]

    first, home, dots_back, dots, output, all_hidden = fence(
        route_first(3),
        route_home(2),
        send(dots[..., part:], SWAP_FIRST),
        dots,
        jnp.dot(all_active, down_rows, preferred_element_type=jnp.float32).astype(jnp.bfloat16),
        all_hidden,
    )
    half = output.shape[0] // (2 * GRID[0])
    outputs = [
        (output[2 * at * half : (2 * at + 1) * half], output[(2 * at + 1) * half : 2 * (at + 1) * half])
        for at in range(GRID[0])
    ]
    firsts.append(first)
    homes.append(home)
    dots = dots[..., :part] + dots_back
    home, dots_back, dots, outputs, all_hidden, others = fence(
        route_home(3),
        [send(dots[at], shift_z(-at)) for at in range(1, GRID[0])],
        dots[0],
        outputs,
        all_hidden,
        [pair_dots(all_rows, piece(pair_count))],
    )
    homes.append(home)
    token_grad = wide_sum(*homes)
    own_dots = (dots + dots_back[0] + dots_back[1] + dots_back[2]).T

    logits = jnp.dot(own_normed2, router_full, preferred_element_type=jnp.float32)
    router_probs = jax.nn.softmax(logits, axis=-1)
    own_gates = jnp.where(named, router_probs, 0.0)
    chosen = jnp.where(named, own_dots, 0.0)
    weighted = jnp.sum(own_gates * chosen, axis=-1, keepdims=True)
    own_logit_grad = (router_probs * (chosen - weighted)).astype(jnp.bfloat16)
    normed2_grad = token_grad + jnp.dot(
        own_logit_grad, router_full.T, preferred_element_type=jnp.float32
    )
    hidden_norm_grad, gain2_grad = norm_backward(hidden, scale2, gains_wide[1], normed2_grad)
    hidden_grad = cotangent.astype(jnp.float32) + hidden_norm_grad
    hidden_low = hidden_grad.astype(jnp.bfloat16)
    far, hidden_low, outputs, all_hidden, more = fence(
        send(hidden_low, SWAP_Y),
        hidden_low,
        outputs,
        all_hidden,
        [pair_dots(all_rows, piece(pair_count + 1))],
    )
    others = [*others, *more]
    mine = side_pair(hidden_low, far)
    theirs, mine, outputs, all_hidden = fence(send(mine, SWAP_CORE), mine, outputs, all_hidden)
    hidden_rows = four_rows(mine, theirs)
    grad_out_full, hidden_rows = fence(
        pair_dots(hidden_rows, mixed).astype(jnp.bfloat16), hidden_rows
    )
    grad_out = (
        lax.psum_scatter(grad_out_full, fsdp, scatter_dimension=0, tiled=True)
        .astype(jnp.float32)
        .T
    )
    output_seconds, (scaled_q, scaled_k, value_grad, inners, gain_grads), outputs = fence(
        [send(pair[1], SWAP_SECOND) for pair in outputs[:2]],
        small_call(
            attend_back_kernel,
            [
                wide_heads,
                wide_heads,
                low_heads,
                ((seq_len, 2), jnp.float32),
                ((2, head_cols), jnp.float32),
            ],
            "attend_back",
        )(hidden_rows, out_full, queries, keys, values, log_sums, projected, *norms, *turns),
        outputs,
    )
    gain_query_grad, gain_key_grad = gain_grads[0], gain_grads[1]
    inners = side_totals(inners[:, 0], inners[:, 1])
    unit_q = query_raw * scale_q
    unit_k = key_raw * scale_k
    query_raw_grad = scale_q * (scaled_q - unit_q * (inners[0] / width)[:, None])
    key_raw_grad = scale_k * (scaled_k - unit_k * (inners[1] / width)[:, None])
    qkv_grad = jnp.concatenate(
        [query_raw_grad.astype(jnp.bfloat16), key_raw_grad.astype(jnp.bfloat16), value_grad], axis=1
    )
    normed1_part = lax.dot_general(
        qkv_grad, qkv_full, CONTRACT_LAST, preferred_element_type=jnp.float32
    )
    gain1_grad = jnp.sum(normed1_part * (rows_x * scale1), axis=0)
    away, mine = core_split(normed1_part)
    zero_width = jnp.zeros((width,), jnp.float32)
    gains_grad = jnp.stack(
        [
            gain1_grad,
            gain2_grad,
            lax.dynamic_update_slice_in_dim(zero_width, gain_query_grad, col_start, 0),
            lax.dynamic_update_slice_in_dim(zero_width, gain_key_grad, col_start, 0),
        ]
    )
    small = jnp.concatenate([pair_dots(own_normed2, own_logit_grad), gains_grad.T], axis=1)
    small = jnp.pad(small, ((0, 0), (0, LANES - n_experts - 4)))
    grad_full = jnp.concatenate([pair_dots(rows1, qkv_grad), small], axis=1).astype(jnp.bfloat16)
    grad_own = lax.psum_scatter(grad_full, fsdp, scatter_dimension=0, tiled=True)
    grad_qkv = (
        grad_own[:, : 3 * head_cols].astype(jnp.float32).reshape(-1, 3, head_cols).transpose(1, 0, 2)
    )
    small = grad_own[:, 3 * head_cols :]
    away, mine, outputs, all_hidden, all_active, _ = fence(
        away, mine, outputs, all_hidden, all_active, grad_full
    )
    back, mine, output_rest, others, more, other_down, all_hidden = fence(
        send(away, SWAP_CORE),
        mine,
        [send(pair[1], SWAP_SECOND) for pair in outputs[2:]],
        [send(other, SWAP_CORE) for other in others],
        [pair_dots(all_rows, piece(pair_count + at)) for at in range(2, pair_count)],
        pair_dots(all_active[:, units:], all_grads),
        all_hidden,
    )
    output_seconds = [*output_seconds, *output_rest]
    away, kept = side_split(mine, back)
    output_firsts = [
        send(first_part(pair[0], second), SWAP_FIRST)
        for pair, second in zip(outputs, output_seconds)
    ]
    far, kept, output_firsts, more, other_down, grad_pair, all_hidden = fence(
        send(away, SWAP_Y),
        kept,
        output_firsts,
        [send(other, SWAP_CORE) for other in more],
        send(other_down, SWAP_CORE),
        [pair_dots(all_rows, piece(at)) + other for at, other in enumerate(others)],
        all_hidden,
    )
    output_mine = [
        mine_part(pair[0], second, first)
        for pair, second, first in zip(outputs, output_seconds, output_firsts)
    ]
    output_homes = [
        send(output_mine[at].astype(jnp.bfloat16), shift_z(-at)) for at in range(1, GRID[0])
    ]
    normed1_grad = kept + far
    input_norm_grad, _ = norm_backward(x_own, own_rows(scale1), gains_wide[0], normed1_grad)
    input_grad = hidden_grad + input_norm_grad
    grad_pair = [
        *grad_pair,
        *(pair_dots(all_rows, piece(2 + at)) + other for at, other in enumerate(more)),
    ]
    grad_down = (pair_dots(all_active[:, :units], all_grads) + other_down).reshape(
        exp_local, ff_local, width
    )
    layer_out = (hidden + wide_sum(output_mine[0], *output_homes)).astype(jnp.bfloat16)
    grad_gate = jnp.stack(grad_pair[0::2])
    grad_up = jnp.stack(grad_pair[1::2])
    small = lax.dynamic_slice_in_dim(
        wide_sum(small, *(send(small, swap) for swap in tp_swaps)),
        tp_rank * small_cols,
        small_cols,
        0,
    )
    grad_router = small[:, :n_experts]
    grad_gains = small[:, n_experts : n_experts + 4].T
    return (
        layer_out,
        input_grad,
        grad_qkv,
        grad_out,
        grad_router,
        grad_gains,
        grad_gate,
        grad_up,
        grad_down,
    )


def solution(mesh):
    fast = tuple(mesh.shape.values()) == (GRID[0] * GRID[1], GRID[2] * GRID[3])
    fine = Mesh(mesh.devices.reshape(GRID), FINE) if fast else None

    def layer(*arguments):
        n_experts = arguments[8].shape[0]
        top_count = arguments[3].shape[1]
        if fast and n_experts <= 2 * top_count:
            return placed_shards(dense_shards, fine, FINE[:2], FINE[2:])(*arguments)
        return placed_shards(shards, mesh, ("fsdp",), ("tp",))(*arguments)

    return layer


def placed_shards(body, mesh, fsdp, tp):
    rows = P((*fsdp, *tp), None)
    experts = P(fsdp, None, tp)
    columns = P(None, (*fsdp, *tp))
    return jax.shard_map(
        body,
        mesh=mesh,
        in_specs=(
            rows,
            P(fsdp, None),
            P(fsdp, None),
            P(fsdp, None),
            P(None, fsdp, tp),
            P(tp, fsdp),
            rows,
            columns,
            experts,
            experts,
            P(fsdp, tp, None),
            rows,
        ),
        out_specs=(
            rows,
            rows,
            P(None, fsdp, tp),
            P(tp, fsdp),
            rows,
            columns,
            experts,
            experts,
            P(fsdp, tp, None),
        ),
        check_vma=False,
    )
```

```python
import functools
import itertools

import jax
import jax.numpy as jnp
from jax import lax
from jax.experimental import pallas as pl
from jax.experimental.pallas import tpu as pltpu
from jax.sharding import Mesh
from jax.sharding import PartitionSpec as P

HD = 128


EPSILON = 1e-05
NEG_FILL = -1e30


def route_slots(expert_ids, n_experts, capacity):
    seq_len, top_count = expert_ids.shape
    experts = jnp.arange(n_experts, dtype=jnp.int32)
    counts = jnp.sum((expert_ids[:, :, None] == experts[None, None, :]).astype(jnp.int32), axis=1)
    earlier = jnp.cumsum(counts, axis=0) - counts
    slot_rank = jnp.take_along_axis(earlier, expert_ids, axis=1)
    flat_index = expert_ids * capacity + slot_rank
    token_index = jnp.broadcast_to(
        jnp.arange(seq_len, dtype=jnp.int32)[:, None], (seq_len, top_count)
    )
    source = jnp.full((n_experts * capacity,), seq_len, jnp.int32)
    source = source.at[flat_index.reshape(-1)].set(token_index.reshape(-1))
    return (flat_index, source)


def rope_tables(seq_len, head_size):
    half_size = head_size // 2
    inverse = 10000.0 ** (-2.0 * jnp.arange(half_size, dtype=jnp.float32) / head_size)
    angles = jnp.arange(seq_len, dtype=jnp.float32)[:, None] * inverse[None, :]
    return (jnp.cos(angles)[:, None, :], jnp.sin(angles)[:, None, :])


def rotate(values, cosine, sine):
    half_size = values.shape[-1] // 2
    first = values[..., :half_size]
    second = values[..., half_size:]
    return jnp.concatenate(
        [first * cosine - second * sine, second * cosine + first * sine], axis=-1
    )


def rotate_back(grads, cosine, sine):
    half_size = grads.shape[-1] // 2
    first = grads[..., :half_size]
    second = grads[..., half_size:]
    return jnp.concatenate(
        [first * cosine + second * sine, second * cosine - first * sine], axis=-1
    )


def allowed_mask(segment, padding, row_start, row_count):
    row_index = row_start + jnp.arange(row_count, dtype=jnp.int32)
    col_index = jnp.arange(segment.shape[0], dtype=jnp.int32)
    same_doc = segment[:, None] == segment[None, :]
    causal = col_index[None, :] <= row_index[:, None]
    usable = (padding[None, :] == 1) | (col_index[None, :] == row_index[:, None])
    return same_doc & causal & usable


def norm_forward(values, gain):
    scale = lax.rsqrt(jnp.mean(values * values, axis=-1, keepdims=True) + EPSILON)
    return (values * scale * gain, scale)


def norm_backward(values, scale, gain, grads):
    unit = values * scale
    gain_grad = jnp.sum(grads * unit, axis=0)
    scaled = grads * gain
    return (scale * (scaled - unit * jnp.mean(scaled * unit, axis=-1, keepdims=True)), gain_grad)


def gather_rows(values):
    return lax.all_gather(values, "tp", axis=0, tiled=True)


def scatter_rows(values):
    return lax.psum_scatter(
        values.astype(jnp.bfloat16), "tp", scatter_dimension=0, tiled=True
    ).astype(jnp.float32)


def tp_totals(first, second):
    return lax.psum((first, second), "tp")


def shards(
    tokens,
    seg_ids,
    pad_mask,
    expert_ids,
    w_qkv,
    w_out,
    w_router,
    norm_gains,
    w_gate,
    w_up,
    w_down,
    cotangent,
):
    tp_rank = lax.axis_index("tp")
    fsdp_count = lax.axis_size("fsdp")
    local_rows, width = tokens.shape
    seq_len = seg_ids.shape[1]
    exp_local = w_gate.shape[0]
    ff_local = w_gate.shape[2]
    n_experts = exp_local * fsdp_count
    top_count = expert_ids.shape[1]
    capacity = (seq_len * top_count * 33 + 32 * n_experts - 1) // (32 * n_experts)
    head_cols = w_qkv.shape[2]
    heads_local = head_cols // HD
    block_rows = min(512, seq_len)
    n_blocks = seq_len // block_rows
    score_scale = HD ** (-0.5)

    def send_experts(buffer):
        return lax.all_to_all(buffer, "fsdp", split_axis=0, concat_axis=1, tiled=True)

    def return_experts(buffer):
        back = lax.all_to_all(buffer, "fsdp", split_axis=1, concat_axis=0, tiled=True)
        return back.reshape(n_experts * capacity, back.shape[2])

    qkv_full, out_full = (
        lax.all_gather(w_qkv, "fsdp", axis=1, tiled=True),
        lax.all_gather(w_out, "fsdp", axis=1, tiled=True),
    )
    router_full, gains_full = (
        lax.all_gather(w_router, ("fsdp", "tp"), axis=0, tiled=True),
        lax.all_gather(norm_gains, ("fsdp", "tp"), axis=1, tiled=True),
    )
    gains_wide = gains_full.astype(jnp.float32)
    col_start = tp_rank * head_cols
    gain_query = lax.dynamic_slice_in_dim(gains_wide[2], col_start, head_cols)
    gain_key = lax.dynamic_slice_in_dim(gains_wide[3], col_start, head_cols)
    segment = seg_ids[0]
    padding = pad_mask[0]
    cosine, sine = rope_tables(seq_len, HD)
    x_own = tokens.astype(jnp.float32)
    normed1, scale1 = norm_forward(x_own, gains_wide[0])
    rows1 = gather_rows(normed1.astype(jnp.bfloat16))
    projected = jnp.einsum("sd,cdh->csh", rows1, qkv_full, preferred_element_type=jnp.float32)
    query_raw = projected[0]
    key_raw = projected[1]
    square_q, square_k = tp_totals(
        jnp.sum(query_raw * query_raw, axis=-1), jnp.sum(key_raw * key_raw, axis=-1)
    )
    scale_q = lax.rsqrt(square_q / width + EPSILON)[:, None]
    scale_k = lax.rsqrt(square_k / width + EPSILON)[:, None]
    unit_q = query_raw * scale_q
    unit_k = key_raw * scale_k
    queries = rotate((unit_q * gain_query).reshape(seq_len, heads_local, HD), cosine, sine).astype(
        jnp.bfloat16
    )
    keys = rotate((unit_k * gain_key).reshape(seq_len, heads_local, HD), cosine, sine).astype(
        jnp.bfloat16
    )
    values = projected[2].astype(jnp.bfloat16).reshape(seq_len, heads_local, HD)
    block_starts = jnp.arange(n_blocks, dtype=jnp.int32) * block_rows

    def block_scores(start):
        raw_scores = (
            jnp.einsum("qhd,khd->hqk", queries, keys, preferred_element_type=jnp.float32)
            * score_scale
        )
        allowed = allowed_mask(segment, padding, start, block_rows)
        return (queries, jnp.where(allowed[None], raw_scores, NEG_FILL), allowed)

    def attend(start):
        query_block, scores, allowed = block_scores(start)
        peak = jnp.max(scores, axis=-1, keepdims=True)
        powered = jnp.exp(scores - peak)
        total = jnp.sum(powered, axis=-1, keepdims=True)
        probs_low = (powered / total).astype(jnp.bfloat16)
        mixed_block = jnp.einsum(
            "hqk,khd->qhd", probs_low, values, preferred_element_type=jnp.float32
        )
        return (
            mixed_block.reshape(block_rows, head_cols).astype(jnp.bfloat16),
            (peak + jnp.log(total))[..., 0],
        )

    mixed_blocks, log_sums = lax.map(attend, block_starts)
    mixed = mixed_blocks.reshape(seq_len, head_cols)
    hidden = x_own + scatter_rows(jnp.dot(mixed, out_full, preferred_element_type=jnp.float32))
    normed2, scale2 = norm_forward(hidden, gains_wide[1])
    own_normed2 = normed2.astype(jnp.bfloat16)
    rows2 = gather_rows(own_normed2)
    logits = jnp.dot(rows2, router_full, preferred_element_type=jnp.float32)
    router_probs = jax.nn.softmax(logits, axis=-1)
    gates = jnp.take_along_axis(router_probs, expert_ids, axis=1)
    flat_index, source = route_slots(expert_ids, n_experts, capacity)
    padded_rows = jnp.concatenate([rows2, jnp.zeros((1, width), jnp.bfloat16)], axis=0)
    received = send_experts(padded_rows[source].reshape(n_experts, capacity, width))
    w_pair = jnp.concatenate([w_gate, w_up], axis=2)
    pair_pre = jnp.einsum("erd,edf->erf", received, w_pair, preferred_element_type=jnp.float32)
    gate_pre = pair_pre[..., :ff_local]
    up_pre = pair_pre[..., ff_local:]
    sigmoid_gate = jax.nn.sigmoid(gate_pre)
    silu_gate = gate_pre * sigmoid_gate
    active = (silu_gate * up_pre).astype(jnp.bfloat16)
    expert_part = jnp.einsum(
        "erf,efd->erd", active, w_down, preferred_element_type=jnp.float32
    ).astype(jnp.bfloat16)
    returned = return_experts(expert_part)
    combined = jnp.zeros((seq_len, returned.shape[1]), jnp.float32)
    for pick_rank in range(top_count):
        combined = combined + gates[:, pick_rank : pick_rank + 1] * returned[
            flat_index[:, pick_rank]
        ].astype(jnp.float32)
    layer_out = (hidden + scatter_rows(combined)).astype(jnp.bfloat16)
    grad_rows = gather_rows(cotangent)
    grad_cols = grad_rows.astype(jnp.float32)
    partial_dots = jnp.stack(
        [
            jnp.sum(returned[flat_index[:, pick_rank]].astype(jnp.float32) * grad_cols, axis=-1)
            for pick_rank in range(top_count)
        ],
        axis=1,
    )
    gate_dots = lax.psum(partial_dots, "tp")
    expert_range = jnp.arange(n_experts, dtype=jnp.int32)
    chosen = jnp.sum(
        gate_dots[:, :, None]
        * (expert_ids[:, :, None] == expert_range[None, None, :]).astype(jnp.float32),
        axis=1,
    )
    weighted = jnp.sum(gates * gate_dots, axis=-1, keepdims=True)
    logit_grad = (router_probs * (chosen - weighted)).astype(jnp.bfloat16)
    own_logit_grad = lax.dynamic_slice_in_dim(logit_grad, tp_rank * local_rows, local_rows, 0)
    slot_gates = (
        jnp.zeros((n_experts * capacity,), jnp.float32)
        .at[flat_index.reshape(-1)]
        .set(gates.reshape(-1))
    )
    padded_grads = jnp.concatenate([grad_rows, jnp.zeros((1, width), jnp.bfloat16)], axis=0)
    slot_grads = (padded_grads[source].astype(jnp.float32) * slot_gates[:, None]).astype(
        jnp.bfloat16
    )
    grad_received = send_experts(slot_grads.reshape(n_experts, capacity, width))
    active_grad = jnp.einsum(
        "erd,efd->erf", grad_received, w_down, preferred_element_type=jnp.float32
    )
    gate_grad = (
        active_grad * up_pre * sigmoid_gate * (1.0 + gate_pre * (1.0 - sigmoid_gate))
    ).astype(jnp.bfloat16)
    up_grad = (active_grad * silu_gate).astype(jnp.bfloat16)
    pair_grad = jnp.concatenate([gate_grad, up_grad], axis=2)
    grad_down = jnp.einsum(
        "erf,erd->efd", active, grad_received, preferred_element_type=jnp.float32
    )
    grad_pair = jnp.einsum("erd,erf->edf", received, pair_grad, preferred_element_type=jnp.float32)
    grad_gate = grad_pair[..., :ff_local]
    grad_up = grad_pair[..., ff_local:]
    input_part = jnp.einsum(
        "erf,edf->erd", pair_grad, w_pair, preferred_element_type=jnp.float32
    ).astype(jnp.bfloat16)
    sent_back = return_experts(input_part)
    token_grad = jnp.zeros((seq_len, sent_back.shape[1]), jnp.float32)
    for pick_rank in range(top_count):
        token_grad = token_grad + sent_back[flat_index[:, pick_rank]].astype(jnp.float32)
    normed2_grad = scatter_rows(token_grad) + jnp.dot(
        own_logit_grad, router_full.T, preferred_element_type=jnp.float32
    )
    hidden_norm_grad, gain2_grad = norm_backward(hidden, scale2, gains_wide[1], normed2_grad)
    hidden_grad = cotangent.astype(jnp.float32) + hidden_norm_grad
    router_grad = jnp.dot(own_normed2.T, own_logit_grad, preferred_element_type=jnp.float32)
    hidden_rows = gather_rows(hidden_grad.astype(jnp.bfloat16))
    grad_out_full = jnp.dot(mixed.T, hidden_rows, preferred_element_type=jnp.float32)
    mixed_grad = (
        jnp.dot(hidden_rows, out_full.T, preferred_element_type=jnp.float32)
        .astype(jnp.bfloat16)
        .reshape(seq_len, heads_local, HD)
    )

    def attend_back(carried, pieces):
        key_acc, value_acc = carried
        start, log_sum = pieces
        query_block, scores, allowed = block_scores(start)
        probs = jnp.where(allowed[None], jnp.exp(scores - log_sum[:, :, None]), 0.0)
        prob_grad = jnp.einsum(
            "qhd,khd->hqk", mixed_grad, values, preferred_element_type=jnp.float32
        )
        delta = jnp.sum(probs * prob_grad, axis=-1, keepdims=True)
        score_grad = (probs * (prob_grad - delta)).astype(jnp.bfloat16)
        query_block_grad = (
            jnp.einsum("hqk,khd->qhd", score_grad, keys, preferred_element_type=jnp.float32)
            * score_scale
        )
        key_acc = (
            key_acc
            + jnp.einsum(
                "hqk,qhd->khd", score_grad, query_block, preferred_element_type=jnp.float32
            )
            * score_scale
        )
        value_acc = value_acc + jnp.einsum(
            "hqk,qhd->khd",
            probs.astype(jnp.bfloat16),
            mixed_grad,
            preferred_element_type=jnp.float32,
        )
        return ((key_acc, value_acc), query_block_grad)

    zero_heads = jnp.zeros((seq_len, heads_local, HD), jnp.float32)
    (key_grad, value_grad), query_blocks = lax.scan(
        attend_back, (zero_heads, zero_heads), (block_starts, log_sums)
    )
    query_grad = query_blocks.reshape(seq_len, heads_local, HD)
    query_norm_grad = rotate_back(query_grad, cosine, sine).reshape(seq_len, head_cols)
    key_norm_grad = rotate_back(key_grad, cosine, sine).reshape(seq_len, head_cols)
    gain_query_grad = jnp.sum(query_norm_grad * unit_q, axis=0)
    gain_key_grad = jnp.sum(key_norm_grad * unit_k, axis=0)
    scaled_q = query_norm_grad * gain_query
    scaled_k = key_norm_grad * gain_key
    inner_q, inner_k = tp_totals(
        jnp.sum(scaled_q * unit_q, axis=-1), jnp.sum(scaled_k * unit_k, axis=-1)
    )
    query_raw_grad = scale_q * (scaled_q - unit_q * (inner_q / width)[:, None])
    key_raw_grad = scale_k * (scaled_k - unit_k * (inner_k / width)[:, None])
    qkv_grad = jnp.stack(
        [query_raw_grad, key_raw_grad, value_grad.reshape(seq_len, head_cols)]
    ).astype(jnp.bfloat16)
    grad_qkv_full = jnp.einsum("sd,csh->cdh", rows1, qkv_grad, preferred_element_type=jnp.float32)
    normed1_part = jnp.einsum("csh,cdh->sd", qkv_grad, qkv_full, preferred_element_type=jnp.float32)
    normed1_grad = scatter_rows(normed1_part)
    input_norm_grad, gain1_grad = norm_backward(x_own, scale1, gains_wide[0], normed1_grad)
    input_grad = hidden_grad + input_norm_grad
    zero_width = jnp.zeros((width,), jnp.float32)
    gains_grad = jnp.stack(
        [
            gain1_grad,
            gain2_grad,
            lax.dynamic_update_slice_in_dim(zero_width, gain_query_grad, col_start, 0),
            lax.dynamic_update_slice_in_dim(zero_width, gain_key_grad, col_start, 0),
        ]
    )
    grad_qkv, grad_out = (
        lax.psum_scatter(
            grad_qkv_full.astype(jnp.bfloat16), "fsdp", scatter_dimension=1, tiled=True
        ).astype(jnp.float32),
        lax.psum_scatter(
            grad_out_full.astype(jnp.bfloat16), "fsdp", scatter_dimension=1, tiled=True
        ).astype(jnp.float32),
    )
    grad_router, grad_gains = (
        lax.psum_scatter(router_grad, ("fsdp", "tp"), scatter_dimension=0, tiled=True),
        lax.psum_scatter(gains_grad, ("fsdp", "tp"), scatter_dimension=1, tiled=True),
    )
    return (
        layer_out,
        input_grad,
        grad_qkv,
        grad_out,
        grad_router,
        grad_gains,
        grad_gate,
        grad_up,
        grad_down,
    )


GRID = (4, 2, 2, 2)
FINE = ("z", "x", "y", "core")
LANES = 128
CONTRACT_LAST = (((1,), (1,)), ((), ()))


def permutation(target):
    def place(z, x, y, c):
        return ((z * GRID[1] + x) * GRID[2] + y) * GRID[3] + c

    return [
        (place(*at), place(*target(*at))) for at in itertools.product(*(range(n) for n in GRID))
    ]


SWAP_CORE = permutation(lambda z, x, y, c: (z, x, y, 1 - c))
SWAP_X = permutation(lambda z, x, y, c: (z, 1 - x, y, c))
SWAP_Y = permutation(lambda z, x, y, c: (z, x, 1 - y, c))
SWAP_BOTH = permutation(lambda z, x, y, c: (z, x, 1 - y, 1 - c))
SWAP_FIRST = permutation(lambda z, x, y, c: (z, 1 - x, y, c) if c == 0 else (z, x, 1 - y, c))
SWAP_SECOND = permutation(lambda z, x, y, c: (z, x, 1 - y, c) if c == 0 else (z, 1 - x, y, c))


def shift_z(steps):
    return permutation(lambda z, x, y, c: ((z + steps) % GRID[0], x, y, c))


def send(values, pairs):
    return lax.ppermute(values, FINE, pairs)


def add_low(*terms):
    return sum(term.astype(jnp.float32) for term in terms).astype(jnp.bfloat16)


def side_totals(first, second):
    return lax.psum((first, second), FINE[2:])


def fence(*values):
    return lax.optimization_barrier(values)


def wide_sum(*terms):
    return sum(term.astype(jnp.float32) for term in terms)


def pair_dots(left, right):
    return lax.dot_general(left, right, (((0,), (0,)), ((), ())), preferred_element_type=jnp.float32)


def side_pair(own, far):
    is_far = lax.axis_index("y") == 1
    return jnp.stack([jnp.where(is_far, far, own), jnp.where(is_far, own, far)])


def four_rows(mine, theirs):
    is_second = lax.axis_index("core") == 1
    both = jnp.stack(
        [jnp.where(is_second, theirs, mine), jnp.where(is_second, mine, theirs)], axis=1
    )
    return both.reshape(4 * mine.shape[1], *mine.shape[2:])


def core_split(values):
    core = lax.axis_index("core")
    blocks = values.astype(jnp.bfloat16).reshape(2, 2, values.shape[0] // 4, values.shape[1])
    return (
        lax.dynamic_index_in_dim(blocks, 1 - core, 1, keepdims=False),
        lax.dynamic_index_in_dim(blocks, core, 1, keepdims=False),
    )


def side_split(mine, back):
    side = lax.axis_index("y")

    def at(pair, which):
        return lax.dynamic_index_in_dim(pair, which, 0, keepdims=False)

    away = add_low(at(mine, 1 - side), at(back, 1 - side))
    return (away, wide_sum(at(mine, side), at(back, side)))


def expert_kernel(
    blocks_ref,
    near_ref,
    far_ref,
    grads0_ref,
    grads1_ref,
    grads2_ref,
    grads3_ref,
    router_ref,
    place_ref,
    *refs,
    n_experts,
    at,
    n_before,
):
    weight_refs, refs = refs[:6], refs[6 + n_before :]
    near_route_ref, far_route_ref, active_ref, hidden_ref, dots_ref, grads_ref, rows_ref = refs[:7]
    gate_buf, up_buf, down_buf, active_buf, hidden_buf, rows_buf, grads_buf, in_sems, out_sems = refs[7:]
    exp_local, width = place_ref.shape[0], near_ref.shape[1]
    units = gate_buf.shape[2]
    half = near_ref.shape[0]
    count = 2 * half
    buffers = (gate_buf, up_buf, down_buf)

    def fetch(slot, kind):
        group, expert = slot // exp_local, slot % exp_local
        return pltpu.make_async_copy(
            weight_refs[3 * group + kind].at[expert], buffers[kind].at[slot], in_sems.at[slot, kind]
        )

    slots = 2 * exp_local
    for slot in range(slots):
        for kind in range(3):
            fetch(slot, kind).start()
    rows_buf[:half] = near_ref[...]
    rows_buf[half:] = far_ref[...]
    quarter = half // 2
    grad_refs = (grads0_ref, grads1_ref, grads2_ref, grads3_ref)
    for block, ref in enumerate(grad_refs):
        grads_buf[block * quarter : (block + 1) * quarter] = ref[:, :width]

    def round_rows(ref):
        return ref.at[pl.ds(at * count, count)]

    stores = [
        pltpu.make_async_copy(rows_buf, round_rows(rows_ref), out_sems.at[0]),
        pltpu.make_async_copy(grads_buf, round_rows(grads_ref), out_sems.at[1]),
    ]
    for store in stores:
        store.start()
    named = jnp.concatenate([ref[:, width:] for ref in grad_refs], axis=0)
    rows = rows_buf[...]
    grads = grads_buf[...]
    lane = lax.broadcasted_iota(jnp.int32, (1, LANES), 1)
    logits = jnp.dot(rows, router_ref[...], preferred_element_type=jnp.float32)
    logits = jnp.where(lane < n_experts, logits, NEG_FILL)
    powered = jnp.exp(logits - jnp.max(logits, axis=-1, keepdims=True))
    gates = powered / jnp.sum(powered, axis=-1, keepdims=True) * named.astype(jnp.float32)
    route = None
    dots = jnp.zeros(logits.shape, jnp.float32)
    for slot in range(slots):
        expert = slot % exp_local
        place = place_ref[expert : expert + 1, :]
        gate = jnp.sum(gates * place, axis=-1, keepdims=True)
        for kind in range(3):
            fetch(slot, kind).wait()
        gate_pre = jnp.dot(rows, gate_buf[slot], preferred_element_type=jnp.float32)
        up_pre = jnp.dot(rows, up_buf[slot], preferred_element_type=jnp.float32)
        y_down = lax.dot_general(
            grads, down_buf[slot], CONTRACT_LAST, preferred_element_type=jnp.float32
        )
        sigmoid = 1.0 / (1.0 + jnp.exp(-gate_pre))
        silu = gate_pre * sigmoid
        active = silu * up_pre
        dots = dots + jnp.sum(active * y_down, axis=-1, keepdims=True) * place
        active_buf[slot] = (active * gate).astype(jnp.bfloat16)
        active_grad = y_down * gate
        gate_grad = (active_grad * up_pre * sigmoid * (1.0 + gate_pre * (1.0 - sigmoid))).astype(
            jnp.bfloat16
        )
        up_grad = (active_grad * silu).astype(jnp.bfloat16)
        hidden_buf[slot, :, :units] = gate_grad
        hidden_buf[slot, :, units:] = up_grad
        for buf, ref, columns, sem in (
            (active_buf, active_ref, units, 2 + 2 * slot),
            (hidden_buf, hidden_ref, 2 * units, 3 + 2 * slot),
        ):
            store = pltpu.make_async_copy(
                buf.at[slot],
                ref.at[pl.ds(at * count, count), pl.ds(slot * columns, columns)],
                out_sems.at[sem],
            )
            store.start()
            stores.append(store)
        part = lax.dot_general(
            gate_grad, gate_buf[slot], CONTRACT_LAST, preferred_element_type=jnp.float32
        ) + lax.dot_general(
            up_grad, up_buf[slot], CONTRACT_LAST, preferred_element_type=jnp.float32
        )
        route = part if route is None else route + part
    near_route_ref[...] = route[:half].astype(jnp.bfloat16)
    far_route_ref[...] = route[half:].astype(jnp.bfloat16)
    dots_ref[...] = jnp.transpose(dots)[:n_experts]
    for store in stores:
        store.wait()


def expert_rows(at, before, blocks, near, far, all_grads, router, place, own, other, n_experts):
    half, width = near.shape
    count = 2 * half
    exp_local, _, units = own[0].shape
    slots = 2 * exp_local
    wide = all_grads.shape[1]

    def whole(array):
        return pl.BlockSpec(
            array.shape, lambda step, blocks: (0,) * array.ndim, pipeline_mode=pl.Buffered(1)
        )

    def picked(row):
        return pl.BlockSpec(
            (count // 4, wide), lambda step, blocks: (blocks[row], 0), pipeline_mode=pl.Buffered(1)
        )

    def first_block(shape):
        return pl.BlockSpec(shape, lambda step, blocks: (0, 0))

    def rounds(columns):
        return jax.ShapeDtypeStruct((GRID[0] * count, columns), jnp.bfloat16)

    anywhere = pl.BlockSpec(memory_space=pl.ANY)
    inputs = (blocks, near, far, *(all_grads for _ in range(4)), router, place, *own, *other, *before)
    order = (2, 3, 5, 6)
    route = jax.ShapeDtypeStruct((half, width), jnp.bfloat16)
    return pl.pallas_call(
        functools.partial(expert_kernel, n_experts=n_experts, at=at, n_before=len(before)),
        out_shape=[
            route,
            route,
            rounds(slots * units),
            rounds(2 * slots * units),
            jax.ShapeDtypeStruct((n_experts, count), jnp.float32),
            rounds(width),
            rounds(width),
        ],
        grid_spec=pltpu.PrefetchScalarGridSpec(
            num_scalar_prefetch=1,
            grid=(1,),
            in_specs=[
                whole(near),
                whole(far),
                *(picked(row) for row in range(4)),
                whole(router),
                whole(place),
                *(anywhere for _ in range(6 + len(before))),
            ],
            out_specs=[
                first_block((half, width)),
                first_block((half, width)),
                anywhere,
                anywhere,
                first_block((n_experts, count)),
                anywhere,
                anywhere,
            ],
            scratch_shapes=[
                pltpu.VMEM((slots, width, units), jnp.bfloat16),
                pltpu.VMEM((slots, width, units), jnp.bfloat16),
                pltpu.VMEM((slots, units, width), jnp.bfloat16),
                pltpu.VMEM((slots, count, units), jnp.bfloat16),
                pltpu.VMEM((slots, count, 2 * units), jnp.bfloat16),
                pltpu.VMEM((count, width), jnp.bfloat16),
                pltpu.VMEM((count, width), jnp.bfloat16),
                pltpu.SemaphoreType.DMA((slots, 3)),
                pltpu.SemaphoreType.DMA((2 + 2 * slots,)),
            ],
        ),
        input_output_aliases={
            len(inputs) - len(before) + index: order[index] for index in range(len(before))
        },
        cost_estimate=pl.CostEstimate(flops=1024, bytes_accessed=1024, transcendentals=0),
        compiler_params=pltpu.CompilerParams(
            dimension_semantics=("arbitrary",), vmem_limit_bytes=46 * 1024 * 1024
        ),
        name="expert_rows",
    )(*inputs)


def turned(values, cosine, sine):
    return values * cosine + pltpu.roll(values, HD // 2, 1) * sine


def allowed_pairs(segment_col_ref, segment_row_ref, padding_ref):
    count = segment_col_ref.shape[0]
    row = lax.broadcasted_iota(jnp.int32, (count, count), 0)
    col = lax.broadcasted_iota(jnp.int32, (count, count), 1)
    usable = (padding_ref[...] == 1) | (col == row)
    return (segment_col_ref[...] == segment_row_ref[...]) & (col <= row) & usable


def attend_kernel(
    projected_ref,
    scale_q_ref,
    scale_k_ref,
    gain_q_ref,
    gain_k_ref,
    cosine_ref,
    sine_ref,
    segment_col_ref,
    segment_row_ref,
    padding_ref,
    mixed_ref,
    queries_ref,
    keys_ref,
    values_ref,
    log_sum_ref,
):
    width = mixed_ref.shape[1]
    allowed = allowed_pairs(segment_col_ref, segment_row_ref, padding_ref)
    cosine, sine = cosine_ref[...], sine_ref[...]
    scale_q, scale_k = scale_q_ref[...], scale_k_ref[...]
    for head in range(width // HD):
        at = slice(head * HD, (head + 1) * HD)
        raw_q = projected_ref[:, head * HD : (head + 1) * HD]
        raw_k = projected_ref[:, width + head * HD : width + (head + 1) * HD]
        raw_v = projected_ref[:, 2 * width + head * HD : 2 * width + (head + 1) * HD]
        queries = turned(raw_q * scale_q * gain_q_ref[:, at], cosine, sine).astype(jnp.bfloat16)
        keys = turned(raw_k * scale_k * gain_k_ref[:, at], cosine, sine).astype(jnp.bfloat16)
        values = raw_v.astype(jnp.bfloat16)
        scores = (
            lax.dot_general(queries, keys, CONTRACT_LAST, preferred_element_type=jnp.float32)
            * HD ** (-0.5)
        )
        scores = jnp.where(allowed, scores, NEG_FILL)
        peak = jnp.max(scores, axis=-1, keepdims=True)
        powered = jnp.exp(scores - peak)
        total = jnp.sum(powered, axis=-1, keepdims=True)
        probs_low = (powered / total).astype(jnp.bfloat16)
        mixed_ref[:, at] = jnp.dot(
            probs_low, values, preferred_element_type=jnp.float32
        ).astype(jnp.bfloat16)
        queries_ref[:, at] = queries
        keys_ref[:, at] = keys
        values_ref[:, at] = values
        log_sum_ref[:, head : head + 1] = peak + jnp.log(total)


def attend_back_kernel(
    hidden_ref,
    out_ref,
    queries_ref,
    keys_ref,
    values_ref,
    log_sum_ref,
    projected_ref,
    scale_q_ref,
    scale_k_ref,
    gain_q_ref,
    gain_k_ref,
    cosine_ref,
    sine_ref,
    segment_col_ref,
    segment_row_ref,
    padding_ref,
    scaled_q_ref,
    scaled_k_ref,
    value_grad_ref,
    inner_ref,
    gain_grad_ref,
):
    width = queries_ref.shape[1]
    allowed = allowed_pairs(segment_col_ref, segment_row_ref, padding_ref)
    cosine, sine = cosine_ref[...], sine_ref[...]
    mixed_grad_all = jnp.dot(
        hidden_ref[...], out_ref[...], preferred_element_type=jnp.float32
    ).astype(jnp.bfloat16)
    contract_rows = (((0,), (0,)), ((), ()))
    inner_q = jnp.zeros((queries_ref.shape[0], 1), jnp.float32)
    inner_k = jnp.zeros((queries_ref.shape[0], 1), jnp.float32)
    for head in range(width // HD):
        at = slice(head * HD, (head + 1) * HD)
        queries, keys, values = queries_ref[:, at], keys_ref[:, at], values_ref[:, at]
        mixed_grad = mixed_grad_all[:, at]
        scores = (
            lax.dot_general(queries, keys, CONTRACT_LAST, preferred_element_type=jnp.float32)
            * HD ** (-0.5)
        )
        powered = jnp.exp(jnp.where(allowed, scores, NEG_FILL) - log_sum_ref[:, head : head + 1])
        probs = jnp.where(allowed, powered, 0.0)
        prob_grad = lax.dot_general(
            mixed_grad, values, CONTRACT_LAST, preferred_element_type=jnp.float32
        )
        delta = jnp.sum(probs * prob_grad, axis=-1, keepdims=True)
        score_grad = (probs * (prob_grad - delta)).astype(jnp.bfloat16)
        query_grad = jnp.dot(score_grad, keys, preferred_element_type=jnp.float32) * HD ** (-0.5)
        key_grad = lax.dot_general(
            score_grad, queries, contract_rows, preferred_element_type=jnp.float32
        ) * HD ** (-0.5)
        value_grad_ref[:, at] = lax.dot_general(
            probs.astype(jnp.bfloat16),
            mixed_grad,
            contract_rows,
            preferred_element_type=jnp.float32,
        ).astype(jnp.bfloat16)
        query_grad = turned(query_grad, cosine, -sine)
        key_grad = turned(key_grad, cosine, -sine)
        unit_q = projected_ref[:, head * HD : (head + 1) * HD] * scale_q_ref[...]
        unit_k = projected_ref[:, width + head * HD : width + (head + 1) * HD] * scale_k_ref[...]
        gain_grad_ref[0:1, at] = jnp.sum(query_grad * unit_q, axis=0, keepdims=True)
        gain_grad_ref[1:2, at] = jnp.sum(key_grad * unit_k, axis=0, keepdims=True)
        scaled_q = query_grad * gain_q_ref[:, at]
        scaled_k = key_grad * gain_k_ref[:, at]
        scaled_q_ref[:, at] = scaled_q
        scaled_k_ref[:, at] = scaled_k
        inner_q += jnp.sum(scaled_q * unit_q, axis=-1, keepdims=True)
        inner_k += jnp.sum(scaled_k * unit_k, axis=-1, keepdims=True)
    inner_ref[:, 0:1] = inner_q
    inner_ref[:, 1:2] = inner_k


def small_call(kernel, shapes, name):
    return pl.pallas_call(
        kernel,
        out_shape=[jax.ShapeDtypeStruct(shape, dtype) for shape, dtype in shapes],
        cost_estimate=pl.CostEstimate(flops=1024, bytes_accessed=1024, transcendentals=0),
        compiler_params=pltpu.CompilerParams(vmem_limit_bytes=40 * 1024 * 1024),
        name=name,
    )


def dense_shards(
    tokens,
    seg_ids,
    pad_mask,
    expert_ids,
    w_qkv,
    w_out,
    w_router,
    norm_gains,
    w_gate,
    w_up,
    w_down,
    cotangent,
):
    z, x, y, core = (lax.axis_index(name) for name in FINE)
    fsdp_rank = z * GRID[1] + x
    tp_rank = y * GRID[3] + core
    local_rows, width = tokens.shape
    seq_len = seg_ids.shape[1]
    exp_local, _, ff_local = w_gate.shape
    n_experts = w_router.shape[1]
    head_cols = w_qkv.shape[2]
    own_start = tp_rank * local_rows
    small_cols = norm_gains.shape[1]
    fsdp = FINE[:2]

    def own_rows(values):
        return lax.dynamic_slice_in_dim(values, own_start, local_rows, 0)

    tp_swaps = (SWAP_CORE, SWAP_Y, SWAP_BOTH)
    z_shifts = [shift_z(steps) for steps in range(1, GRID[0])]
    small_own = jnp.pad(
        jnp.concatenate([w_router, norm_gains.T], axis=1), ((0, 0), (0, LANES - n_experts - 4))
    )
    small = lax.dynamic_update_slice_in_dim(
        jnp.zeros((w_qkv.shape[1], LANES), jnp.bfloat16), small_own, tp_rank * small_cols, 0
    )
    smalls, tokens_own = fence([send(small, swap) for swap in tp_swaps], tokens)
    small = small + smalls[0] + smalls[1] + smalls[2]
    weights_own = jnp.concatenate(
        [w_qkv.transpose(1, 0, 2).reshape(w_qkv.shape[1], -1), small], axis=1
    )
    weights_full = lax.all_gather(weights_own, fsdp, axis=0, tiled=True)
    block = w_out.shape[1]
    out_full = jnp.zeros((width, w_out.shape[0]), jnp.bfloat16)
    out_column, tokens_own = fence(w_out.T, tokens_own)
    for steps in range(GRID[0]):
        out_beside = send(out_column, SWAP_X)
        for piece_x, piece_values in ((x, out_column), (1 - x, out_beside)):
            start = ((z - steps) % GRID[0] * GRID[1] + piece_x) * block
            out_full = lax.dynamic_update_slice_in_dim(out_full, piece_values, start, 0)
        if steps < GRID[0] - 1:
            out_column = send(out_column, z_shifts[0])
    names = jnp.arange(n_experts, dtype=jnp.int32)
    own_ids = own_rows(expert_ids)
    named = (own_ids[:, :, None] == names[None, None, :]).any(axis=1)
    named_wide = jnp.pad(named.astype(jnp.bfloat16), ((0, 0), (0, LANES - n_experts)))
    grads_own = jnp.concatenate([cotangent, named_wide], axis=1)
    far = send(tokens_own, SWAP_Y)
    mine = side_pair(tokens, far)
    theirs = send(mine, SWAP_CORE)
    rows_x = four_rows(mine, theirs).astype(jnp.float32)
    scale1 = lax.rsqrt(jnp.mean(rows_x * rows_x, axis=-1, keepdims=True) + EPSILON)
    own_weights = (w_gate, w_up, w_down)
    grads_own, weights_own, weights_full, scale1, rows_x, out_full = fence(
        grads_own, own_weights, weights_full, scale1, rows_x, out_full
    )
    all_grads_abs = lax.all_gather(grads_own, FINE[:3], axis=0, tiled=True)
    other_weights = tuple(send(weight, SWAP_CORE) for weight in weights_own)
    qkv_full = weights_full[:, : 3 * head_cols]
    router_wide = weights_full[:, 3 * head_cols :]
    router_full = router_wide[:, :n_experts]
    gains_wide = router_wide[:, n_experts : n_experts + 4].T.astype(jnp.float32)

    cosine, sine = (table[:, 0] for table in rope_tables(seq_len, HD))
    turns = (
        jnp.concatenate([cosine, cosine], axis=1),
        jnp.concatenate([-sine, sine], axis=1),
        seg_ids.T,
        seg_ids,
        pad_mask,
    )
    x_own = tokens.astype(jnp.float32)
    col_start = tp_rank * head_cols
    gain_query = lax.dynamic_slice_in_dim(gains_wide[2], col_start, head_cols)
    gain_key = lax.dynamic_slice_in_dim(gains_wide[3], col_start, head_cols)
    rows1 = (rows_x * scale1 * gains_wide[0]).astype(jnp.bfloat16)
    projected = jnp.dot(rows1, qkv_full, preferred_element_type=jnp.float32)
    query_raw = projected[:, :head_cols]
    key_raw = projected[:, head_cols : 2 * head_cols]
    squares = side_totals(
        jnp.sum(query_raw * query_raw, axis=-1), jnp.sum(key_raw * key_raw, axis=-1)
    )
    scale_q = lax.rsqrt(squares[0] / width + EPSILON)[:, None]
    scale_k = lax.rsqrt(squares[1] / width + EPSILON)[:, None]
    low_heads = ((seq_len, head_cols), jnp.bfloat16)
    wide_heads = ((seq_len, head_cols), jnp.float32)
    norms = (scale_q, scale_k, gain_query[None], gain_key[None])
    mixed, queries, keys, values, log_sums = small_call(
        attend_kernel, [low_heads] * 4 + [((seq_len, LANES), jnp.float32)], "attend"
    )(projected, *norms, *turns)
    away, mine = core_split(
        lax.dot_general(mixed, out_full, CONTRACT_LAST, preferred_element_type=jnp.float32)
    )
    away, kept = side_split(mine, send(away, SWAP_CORE))
    far, kept = fence(send(away, SWAP_Y), kept)
    hidden = x_own + kept + far
    normed2, scale2 = norm_forward(hidden, gains_wide[1])
    own_normed2 = normed2.astype(jnp.bfloat16)

    place = (
        jnp.arange(LANES)[None, :] == fsdp_rank * exp_local + jnp.arange(exp_local)[:, None]
    ).astype(jnp.float32)
    rows, rows_near, rows_far = [own_normed2], [], []
    results, seconds, firsts, homes = [], [], [], []

    def hop(column):
        return send(column, z_shifts[0])

    def experts(at):
        beside = jnp.where(core == 0, (1 - x) * GRID[2] + y, x * GRID[2] + 1 - y)
        across = jnp.where(core == 0, x * GRID[2] + 1 - y, (1 - x) * GRID[2] + y)
        opposite = (1 - x) * GRID[2] + 1 - y
        plane = (z - at) % GRID[0] * (GRID[1] * GRID[2])
        blocks = plane + jnp.stack([x * GRID[2] + y, beside, across, opposite])
        before = [results[at - 1][index] for index in (2, 3, 5, 6)] if at else []
        return expert_rows(
            at,
            before,
            blocks.astype(jnp.int32),
            rows_near[at],
            rows_far[at],
            all_grads_abs,
            router_wide,
            place,
            own_weights,
            other_weights,
            n_experts,
        )

    def near_of(at, arrived):
        return jnp.concatenate([rows[at], arrived], axis=0)

    def first_part(near, second):
        half = near.shape[0] // 2
        return add_low(near[half:], second[half:])

    def mine_part(near, second, first):
        half = near.shape[0] // 2
        return wide_sum(near[:half], second[:half], first)

    def route_first(at):
        return send(first_part(results[at][0], seconds[at]), SWAP_FIRST)

    def route_home(at):
        mine = mine_part(results[at][0], seconds[at], firsts[at])
        return send(mine.astype(jnp.bfloat16), z_shifts[GRID[0] - 1 - at])

    hopped, arrived = fence(hop(rows[0]), send(rows[0], SWAP_FIRST))
    rows.append(hopped)
    rows_near.append(near_of(0, arrived))
    hopped, arrived, second = fence(
        hop(rows[1]), send(rows[1], SWAP_FIRST), send(rows_near[0], SWAP_SECOND)
    )
    rows.append(hopped)
    rows_near.append(near_of(1, arrived))
    rows_far.append(second)
    hopped, arrived, second, result = fence(
        hop(rows[2]), send(rows[2], SWAP_FIRST), send(rows_near[1], SWAP_SECOND), experts(0)
    )
    rows.append(hopped)
    rows_near.append(near_of(2, arrived))
    rows_far.append(second)
    results.append(result)
    arrived, second, back, result = fence(
        send(rows[3], SWAP_FIRST),
        send(rows_near[2], SWAP_SECOND),
        send(results[0][1], SWAP_SECOND),
        experts(1),
    )
    rows_near.append(near_of(3, arrived))
    rows_far.append(second)
    seconds.append(back)
    results.append(result)
    second, back, first, result = fence(
        send(rows_near[3], SWAP_SECOND),
        send(results[1][1], SWAP_SECOND),
        route_first(0),
        experts(2),
    )
    rows_far.append(second)
    seconds.append(back)
    firsts.append(first)
    results.append(result)
    back, first, result = fence(
        send(results[2][1], SWAP_SECOND), route_first(1), experts(3)
    )
    seconds.append(back)
    firsts.append(first)
    results.append(result)
    homes.append(mine_part(results[0][0], seconds[0], firsts[0]))

    dots = jnp.stack([result[4] for result in results])
    part = dots.shape[-1] // 4
    all_active, all_hidden, all_grads, all_rows = (results[-1][index] for index in (2, 3, 5, 6))
    down_rows = jnp.concatenate(
        [weights[2].reshape(-1, width) for weights in (own_weights, other_weights)]
    )
    back, first, home, dots_back, dots, all_active, down_rows, all_hidden = fence(
        send(results[3][1], SWAP_SECOND),
        route_first(2),
        route_home(1),
        send(dots[..., 2 * part :], SWAP_SECOND),
        dots,
        all_active,
        down_rows,
        all_hidden,
    )
    seconds.append(back)
    firsts.append(first)
    homes.append(home)
    dots = dots[..., : 2 * part] + dots_back
    units = exp_local * ff_local
    pair_count = 2 * exp_local

    def piece(at):
        return all_hidden[:, at * ff_local : (at + 1) * ff_local]

    first, home, dots_back, dots, output, all_hidden = fence(
        route_first(3),
        route_home(2),
        send(dots[..., part:], SWAP_FIRST),
        dots,
        jnp.dot(all_active, down_rows, preferred_element_type=jnp.float32).astype(jnp.bfloat16),
        all_hidden,
    )
    half = output.shape[0] // (2 * GRID[0])
    outputs = [
        (output[2 * at * half : (2 * at + 1) * half], output[(2 * at + 1) * half : 2 * (at + 1) * half])
        for at in range(GRID[0])
    ]
    firsts.append(first)
    homes.append(home)
    dots = dots[..., :part] + dots_back
    home, output_early, dots_back, dots, outputs, all_hidden, others = fence(
        route_home(3),
        send(outputs[0][1], SWAP_SECOND),
        [send(dots[at], shift_z(-at)) for at in range(1, GRID[0])],
        dots[0],
        outputs,
        all_hidden,
        [pair_dots(all_rows, piece(pair_count))],
    )
    homes.append(home)
    token_grad = wide_sum(*homes)
    own_dots = (dots + dots_back[0] + dots_back[1] + dots_back[2]).T

    logits = jnp.dot(own_normed2, router_full, preferred_element_type=jnp.float32)
    router_probs = jax.nn.softmax(logits, axis=-1)
    own_gates = jnp.where(named, router_probs, 0.0)
    chosen = jnp.where(named, own_dots, 0.0)
    weighted = jnp.sum(own_gates * chosen, axis=-1, keepdims=True)
    own_logit_grad = (router_probs * (chosen - weighted)).astype(jnp.bfloat16)
    normed2_grad = token_grad + jnp.dot(
        own_logit_grad, router_full.T, preferred_element_type=jnp.float32
    )
    hidden_norm_grad, gain2_grad = norm_backward(hidden, scale2, gains_wide[1], normed2_grad)
    hidden_grad = cotangent.astype(jnp.float32) + hidden_norm_grad
    hidden_low = hidden_grad.astype(jnp.bfloat16)
    far, hidden_low, outputs, all_hidden, more = fence(
        send(hidden_low, SWAP_Y),
        hidden_low,
        outputs,
        all_hidden,
        [pair_dots(all_rows, piece(pair_count + 1))],
    )
    others = [*others, *more]
    mine = side_pair(hidden_low, far)
    theirs, mine, outputs, all_hidden = fence(send(mine, SWAP_CORE), mine, outputs, all_hidden)
    hidden_rows = four_rows(mine, theirs)
    grad_out_full, hidden_rows = fence(
        pair_dots(hidden_rows, mixed).astype(jnp.bfloat16), hidden_rows
    )
    grad_out = (
        lax.psum_scatter(grad_out_full, fsdp, scatter_dimension=0, tiled=True)
        .astype(jnp.float32)
        .T
    )
    output_seconds, (scaled_q, scaled_k, value_grad, inners, gain_grads), outputs = fence(
        [send(pair[1], SWAP_SECOND) for pair in outputs[1:3]],
        small_call(
            attend_back_kernel,
            [
                wide_heads,
                wide_heads,
                low_heads,
                ((seq_len, 2), jnp.float32),
                ((2, head_cols), jnp.float32),
            ],
            "attend_back",
        )(hidden_rows, out_full, queries, keys, values, log_sums, projected, *norms, *turns),
        outputs,
    )
    gain_query_grad, gain_key_grad = gain_grads[0], gain_grads[1]
    inners = side_totals(inners[:, 0], inners[:, 1])
    unit_q = query_raw * scale_q
    unit_k = key_raw * scale_k
    query_raw_grad = scale_q * (scaled_q - unit_q * (inners[0] / width)[:, None])
    key_raw_grad = scale_k * (scaled_k - unit_k * (inners[1] / width)[:, None])
    qkv_grad = jnp.concatenate(
        [query_raw_grad.astype(jnp.bfloat16), key_raw_grad.astype(jnp.bfloat16), value_grad], axis=1
    )
    normed1_part = lax.dot_general(
        qkv_grad, qkv_full, CONTRACT_LAST, preferred_element_type=jnp.float32
    )
    gain1_grad = jnp.sum(normed1_part * (rows_x * scale1), axis=0)
    away, mine = core_split(normed1_part)
    zero_width = jnp.zeros((width,), jnp.float32)
    gains_grad = jnp.stack(
        [
            gain1_grad,
            gain2_grad,
            lax.dynamic_update_slice_in_dim(zero_width, gain_query_grad, col_start, 0),
            lax.dynamic_update_slice_in_dim(zero_width, gain_key_grad, col_start, 0),
        ]
    )
    small = jnp.concatenate([pair_dots(own_normed2, own_logit_grad), gains_grad.T], axis=1)
    small = jnp.pad(small, ((0, 0), (0, LANES - n_experts - 4)))
    grad_full = jnp.concatenate([pair_dots(rows1, qkv_grad), small], axis=1).astype(jnp.bfloat16)
    grad_own = lax.psum_scatter(grad_full, fsdp, scatter_dimension=0, tiled=True)
    grad_qkv = (
        grad_own[:, : 3 * head_cols].astype(jnp.float32).reshape(-1, 3, head_cols).transpose(1, 0, 2)
    )
    small = grad_own[:, 3 * head_cols :]
    away, mine, outputs, all_hidden, all_active, _ = fence(
        away, mine, outputs, all_hidden, all_active, grad_full
    )
    back, mine, output_rest, others, more, other_down, all_hidden = fence(
        send(away, SWAP_CORE),
        mine,
        [send(pair[1], SWAP_SECOND) for pair in outputs[3:]],
        [send(other, SWAP_CORE) for other in others],
        [pair_dots(all_rows, piece(pair_count + at)) for at in range(2, pair_count)],
        pair_dots(all_active[:, units:], all_grads),
        all_hidden,
    )
    output_seconds = [output_early, *output_seconds, *output_rest]
    away, kept = side_split(mine, back)
    output_firsts = [
        send(first_part(pair[0], second), SWAP_FIRST)
        for pair, second in zip(outputs, output_seconds)
    ]
    far, kept, output_firsts, more, other_down, grad_pair, all_hidden = fence(
        send(away, SWAP_Y),
        kept,
        output_firsts,
        [send(other, SWAP_CORE) for other in more],
        send(other_down, SWAP_CORE),
        [pair_dots(all_rows, piece(at)) + other for at, other in enumerate(others)],
        all_hidden,
    )
    output_mine = [
        mine_part(pair[0], second, first)
        for pair, second, first in zip(outputs, output_seconds, output_firsts)
    ]
    output_homes = [
        send(output_mine[at].astype(jnp.bfloat16), shift_z(-at)) for at in range(1, GRID[0])
    ]
    normed1_grad = kept + far
    input_norm_grad, _ = norm_backward(x_own, own_rows(scale1), gains_wide[0], normed1_grad)
    input_grad = hidden_grad + input_norm_grad
    grad_pair = [
        *grad_pair,
        *(pair_dots(all_rows, piece(2 + at)) + other for at, other in enumerate(more)),
    ]
    grad_down = (pair_dots(all_active[:, :units], all_grads) + other_down).reshape(
        exp_local, ff_local, width
    )
    layer_out = (hidden + wide_sum(output_mine[0], *output_homes)).astype(jnp.bfloat16)
    grad_gate = jnp.stack(grad_pair[0::2])
    grad_up = jnp.stack(grad_pair[1::2])
    small = lax.dynamic_slice_in_dim(
        wide_sum(small, *(send(small, swap) for swap in tp_swaps)),
        tp_rank * small_cols,
        small_cols,
        0,
    )
    grad_router = small[:, :n_experts]
    grad_gains = small[:, n_experts : n_experts + 4].T
    return (
        layer_out,
        input_grad,
        grad_qkv,
        grad_out,
        grad_router,
        grad_gains,
        grad_gate,
        grad_up,
        grad_down,
    )


def solution(mesh):
    fast = tuple(mesh.shape.values()) == (GRID[0] * GRID[1], GRID[2] * GRID[3])
    fine = Mesh(mesh.devices.reshape(GRID), FINE) if fast else None

    def layer(*arguments):
        n_experts = arguments[8].shape[0]
        top_count = arguments[3].shape[1]
        if fast and n_experts <= 2 * top_count:
            return placed_shards(dense_shards, fine, FINE[:2], FINE[2:])(*arguments)
        return placed_shards(shards, mesh, ("fsdp",), ("tp",))(*arguments)

    return layer


def placed_shards(body, mesh, fsdp, tp):
    rows = P((*fsdp, *tp), None)
    experts = P(fsdp, None, tp)
    columns = P(None, (*fsdp, *tp))
    return jax.shard_map(
        body,
        mesh=mesh,
        in_specs=(
            rows,
            P(fsdp, None),
            P(fsdp, None),
            P(fsdp, None),
            P(None, fsdp, tp),
            P(tp, fsdp),
            rows,
            columns,
            experts,
            experts,
            P(fsdp, tp, None),
            rows,
        ),
        out_specs=(
            rows,
            rows,
            P(None, fsdp, tp),
            P(tp, fsdp),
            rows,
            columns,
            experts,
            experts,
            P(fsdp, tp, None),
        ),
        check_vma=False,
    )
```

```python
import functools
import itertools

import jax
import jax.numpy as jnp
from jax import lax
from jax.experimental import pallas as pl
from jax.experimental.pallas import tpu as pltpu
from jax.sharding import Mesh
from jax.sharding import PartitionSpec as P

HD = 128


EPSILON = 1e-05
NEG_FILL = -1e30


def route_slots(expert_ids, n_experts, capacity):
    seq_len, top_count = expert_ids.shape
    experts = jnp.arange(n_experts, dtype=jnp.int32)
    counts = jnp.sum((expert_ids[:, :, None] == experts[None, None, :]).astype(jnp.int32), axis=1)
    earlier = jnp.cumsum(counts, axis=0) - counts
    slot_rank = jnp.take_along_axis(earlier, expert_ids, axis=1)
    flat_index = expert_ids * capacity + slot_rank
    token_index = jnp.broadcast_to(
        jnp.arange(seq_len, dtype=jnp.int32)[:, None], (seq_len, top_count)
    )
    source = jnp.full((n_experts * capacity,), seq_len, jnp.int32)
    source = source.at[flat_index.reshape(-1)].set(token_index.reshape(-1))
    return (flat_index, source)


def rope_tables(seq_len, head_size):
    half_size = head_size // 2
    inverse = 10000.0 ** (-2.0 * jnp.arange(half_size, dtype=jnp.float32) / head_size)
    angles = jnp.arange(seq_len, dtype=jnp.float32)[:, None] * inverse[None, :]
    return (jnp.cos(angles)[:, None, :], jnp.sin(angles)[:, None, :])


def rotate(values, cosine, sine):
    half_size = values.shape[-1] // 2
    first = values[..., :half_size]
    second = values[..., half_size:]
    return jnp.concatenate(
        [first * cosine - second * sine, second * cosine + first * sine], axis=-1
    )


def rotate_back(grads, cosine, sine):
    half_size = grads.shape[-1] // 2
    first = grads[..., :half_size]
    second = grads[..., half_size:]
    return jnp.concatenate(
        [first * cosine + second * sine, second * cosine - first * sine], axis=-1
    )


def allowed_mask(segment, padding, row_start, row_count):
    row_index = row_start + jnp.arange(row_count, dtype=jnp.int32)
    col_index = jnp.arange(segment.shape[0], dtype=jnp.int32)
    same_doc = segment[:, None] == segment[None, :]
    causal = col_index[None, :] <= row_index[:, None]
    usable = (padding[None, :] == 1) | (col_index[None, :] == row_index[:, None])
    return same_doc & causal & usable


def norm_forward(values, gain):
    scale = lax.rsqrt(jnp.mean(values * values, axis=-1, keepdims=True) + EPSILON)
    return (values * scale * gain, scale)


def norm_backward(values, scale, gain, grads):
    unit = values * scale
    gain_grad = jnp.sum(grads * unit, axis=0)
    scaled = grads * gain
    return (scale * (scaled - unit * jnp.mean(scaled * unit, axis=-1, keepdims=True)), gain_grad)


def gather_rows(values):
    return lax.all_gather(values, "tp", axis=0, tiled=True)


def scatter_rows(values):
    return lax.psum_scatter(
        values.astype(jnp.bfloat16), "tp", scatter_dimension=0, tiled=True
    ).astype(jnp.float32)


def tp_totals(first, second):
    return lax.psum((first, second), "tp")


def shards(
    tokens,
    seg_ids,
    pad_mask,
    expert_ids,
    w_qkv,
    w_out,
    w_router,
    norm_gains,
    w_gate,
    w_up,
    w_down,
    cotangent,
):
    tp_rank = lax.axis_index("tp")
    fsdp_count = lax.axis_size("fsdp")
    local_rows, width = tokens.shape
    seq_len = seg_ids.shape[1]
    exp_local = w_gate.shape[0]
    ff_local = w_gate.shape[2]
    n_experts = exp_local * fsdp_count
    top_count = expert_ids.shape[1]
    capacity = (seq_len * top_count * 33 + 32 * n_experts - 1) // (32 * n_experts)
    head_cols = w_qkv.shape[2]
    heads_local = head_cols // HD
    block_rows = min(512, seq_len)
    n_blocks = seq_len // block_rows
    score_scale = HD ** (-0.5)

    def send_experts(buffer):
        return lax.all_to_all(buffer, "fsdp", split_axis=0, concat_axis=1, tiled=True)

    def return_experts(buffer):
        back = lax.all_to_all(buffer, "fsdp", split_axis=1, concat_axis=0, tiled=True)
        return back.reshape(n_experts * capacity, back.shape[2])

    qkv_full, out_full = (
        lax.all_gather(w_qkv, "fsdp", axis=1, tiled=True),
        lax.all_gather(w_out, "fsdp", axis=1, tiled=True),
    )
    router_full, gains_full = (
        lax.all_gather(w_router, ("fsdp", "tp"), axis=0, tiled=True),
        lax.all_gather(norm_gains, ("fsdp", "tp"), axis=1, tiled=True),
    )
    gains_wide = gains_full.astype(jnp.float32)
    col_start = tp_rank * head_cols
    gain_query = lax.dynamic_slice_in_dim(gains_wide[2], col_start, head_cols)
    gain_key = lax.dynamic_slice_in_dim(gains_wide[3], col_start, head_cols)
    segment = seg_ids[0]
    padding = pad_mask[0]
    cosine, sine = rope_tables(seq_len, HD)
    x_own = tokens.astype(jnp.float32)
    normed1, scale1 = norm_forward(x_own, gains_wide[0])
    rows1 = gather_rows(normed1.astype(jnp.bfloat16))
    projected = jnp.einsum("sd,cdh->csh", rows1, qkv_full, preferred_element_type=jnp.float32)
    query_raw = projected[0]
    key_raw = projected[1]
    square_q, square_k = tp_totals(
        jnp.sum(query_raw * query_raw, axis=-1), jnp.sum(key_raw * key_raw, axis=-1)
    )
    scale_q = lax.rsqrt(square_q / width + EPSILON)[:, None]
    scale_k = lax.rsqrt(square_k / width + EPSILON)[:, None]
    unit_q = query_raw * scale_q
    unit_k = key_raw * scale_k
    queries = rotate((unit_q * gain_query).reshape(seq_len, heads_local, HD), cosine, sine).astype(
        jnp.bfloat16
    )
    keys = rotate((unit_k * gain_key).reshape(seq_len, heads_local, HD), cosine, sine).astype(
        jnp.bfloat16
    )
    values = projected[2].astype(jnp.bfloat16).reshape(seq_len, heads_local, HD)
    block_starts = jnp.arange(n_blocks, dtype=jnp.int32) * block_rows

    def block_scores(start):
        raw_scores = (
            jnp.einsum("qhd,khd->hqk", queries, keys, preferred_element_type=jnp.float32)
            * score_scale
        )
        allowed = allowed_mask(segment, padding, start, block_rows)
        return (queries, jnp.where(allowed[None], raw_scores, NEG_FILL), allowed)

    def attend(start):
        query_block, scores, allowed = block_scores(start)
        peak = jnp.max(scores, axis=-1, keepdims=True)
        powered = jnp.exp(scores - peak)
        total = jnp.sum(powered, axis=-1, keepdims=True)
        probs_low = (powered / total).astype(jnp.bfloat16)
        mixed_block = jnp.einsum(
            "hqk,khd->qhd", probs_low, values, preferred_element_type=jnp.float32
        )
        return (
            mixed_block.reshape(block_rows, head_cols).astype(jnp.bfloat16),
            (peak + jnp.log(total))[..., 0],
        )

    mixed_blocks, log_sums = lax.map(attend, block_starts)
    mixed = mixed_blocks.reshape(seq_len, head_cols)
    hidden = x_own + scatter_rows(jnp.dot(mixed, out_full, preferred_element_type=jnp.float32))
    normed2, scale2 = norm_forward(hidden, gains_wide[1])
    own_normed2 = normed2.astype(jnp.bfloat16)
    rows2 = gather_rows(own_normed2)
    logits = jnp.dot(rows2, router_full, preferred_element_type=jnp.float32)
    router_probs = jax.nn.softmax(logits, axis=-1)
    gates = jnp.take_along_axis(router_probs, expert_ids, axis=1)
    flat_index, source = route_slots(expert_ids, n_experts, capacity)
    padded_rows = jnp.concatenate([rows2, jnp.zeros((1, width), jnp.bfloat16)], axis=0)
    received = send_experts(padded_rows[source].reshape(n_experts, capacity, width))
    w_pair = jnp.concatenate([w_gate, w_up], axis=2)
    pair_pre = jnp.einsum("erd,edf->erf", received, w_pair, preferred_element_type=jnp.float32)
    gate_pre = pair_pre[..., :ff_local]
    up_pre = pair_pre[..., ff_local:]
    sigmoid_gate = jax.nn.sigmoid(gate_pre)
    silu_gate = gate_pre * sigmoid_gate
    active = (silu_gate * up_pre).astype(jnp.bfloat16)
    expert_part = jnp.einsum(
        "erf,efd->erd", active, w_down, preferred_element_type=jnp.float32
    ).astype(jnp.bfloat16)
    returned = return_experts(expert_part)
    combined = jnp.zeros((seq_len, returned.shape[1]), jnp.float32)
    for pick_rank in range(top_count):
        combined = combined + gates[:, pick_rank : pick_rank + 1] * returned[
            flat_index[:, pick_rank]
        ].astype(jnp.float32)
    layer_out = (hidden + scatter_rows(combined)).astype(jnp.bfloat16)
    grad_rows = gather_rows(cotangent)
    grad_cols = grad_rows.astype(jnp.float32)
    partial_dots = jnp.stack(
        [
            jnp.sum(returned[flat_index[:, pick_rank]].astype(jnp.float32) * grad_cols, axis=-1)
            for pick_rank in range(top_count)
        ],
        axis=1,
    )
    gate_dots = lax.psum(partial_dots, "tp")
    expert_range = jnp.arange(n_experts, dtype=jnp.int32)
    chosen = jnp.sum(
        gate_dots[:, :, None]
        * (expert_ids[:, :, None] == expert_range[None, None, :]).astype(jnp.float32),
        axis=1,
    )
    weighted = jnp.sum(gates * gate_dots, axis=-1, keepdims=True)
    logit_grad = (router_probs * (chosen - weighted)).astype(jnp.bfloat16)
    own_logit_grad = lax.dynamic_slice_in_dim(logit_grad, tp_rank * local_rows, local_rows, 0)
    slot_gates = (
        jnp.zeros((n_experts * capacity,), jnp.float32)
        .at[flat_index.reshape(-1)]
        .set(gates.reshape(-1))
    )
    padded_grads = jnp.concatenate([grad_rows, jnp.zeros((1, width), jnp.bfloat16)], axis=0)
    slot_grads = (padded_grads[source].astype(jnp.float32) * slot_gates[:, None]).astype(
        jnp.bfloat16
    )
    grad_received = send_experts(slot_grads.reshape(n_experts, capacity, width))
    active_grad = jnp.einsum(
        "erd,efd->erf", grad_received, w_down, preferred_element_type=jnp.float32
    )
    gate_grad = (
        active_grad * up_pre * sigmoid_gate * (1.0 + gate_pre * (1.0 - sigmoid_gate))
    ).astype(jnp.bfloat16)
    up_grad = (active_grad * silu_gate).astype(jnp.bfloat16)
    pair_grad = jnp.concatenate([gate_grad, up_grad], axis=2)
    grad_down = jnp.einsum(
        "erf,erd->efd", active, grad_received, preferred_element_type=jnp.float32
    )
    grad_pair = jnp.einsum("erd,erf->edf", received, pair_grad, preferred_element_type=jnp.float32)
    grad_gate = grad_pair[..., :ff_local]
    grad_up = grad_pair[..., ff_local:]
    input_part = jnp.einsum(
        "erf,edf->erd", pair_grad, w_pair, preferred_element_type=jnp.float32
    ).astype(jnp.bfloat16)
    sent_back = return_experts(input_part)
    token_grad = jnp.zeros((seq_len, sent_back.shape[1]), jnp.float32)
    for pick_rank in range(top_count):
        token_grad = token_grad + sent_back[flat_index[:, pick_rank]].astype(jnp.float32)
    normed2_grad = scatter_rows(token_grad) + jnp.dot(
        own_logit_grad, router_full.T, preferred_element_type=jnp.float32
    )
    hidden_norm_grad, gain2_grad = norm_backward(hidden, scale2, gains_wide[1], normed2_grad)
    hidden_grad = cotangent.astype(jnp.float32) + hidden_norm_grad
    router_grad = jnp.dot(own_normed2.T, own_logit_grad, preferred_element_type=jnp.float32)
    hidden_rows = gather_rows(hidden_grad.astype(jnp.bfloat16))
    grad_out_full = jnp.dot(mixed.T, hidden_rows, preferred_element_type=jnp.float32)
    mixed_grad = (
        jnp.dot(hidden_rows, out_full.T, preferred_element_type=jnp.float32)
        .astype(jnp.bfloat16)
        .reshape(seq_len, heads_local, HD)
    )

    def attend_back(carried, pieces):
        key_acc, value_acc = carried
        start, log_sum = pieces
        query_block, scores, allowed = block_scores(start)
        probs = jnp.where(allowed[None], jnp.exp(scores - log_sum[:, :, None]), 0.0)
        prob_grad = jnp.einsum(
            "qhd,khd->hqk", mixed_grad, values, preferred_element_type=jnp.float32
        )
        delta = jnp.sum(probs * prob_grad, axis=-1, keepdims=True)
        score_grad = (probs * (prob_grad - delta)).astype(jnp.bfloat16)
        query_block_grad = (
            jnp.einsum("hqk,khd->qhd", score_grad, keys, preferred_element_type=jnp.float32)
            * score_scale
        )
        key_acc = (
            key_acc
            + jnp.einsum(
                "hqk,qhd->khd", score_grad, query_block, preferred_element_type=jnp.float32
            )
            * score_scale
        )
        value_acc = value_acc + jnp.einsum(
            "hqk,qhd->khd",
            probs.astype(jnp.bfloat16),
            mixed_grad,
            preferred_element_type=jnp.float32,
        )
        return ((key_acc, value_acc), query_block_grad)

    zero_heads = jnp.zeros((seq_len, heads_local, HD), jnp.float32)
    (key_grad, value_grad), query_blocks = lax.scan(
        attend_back, (zero_heads, zero_heads), (block_starts, log_sums)
    )
    query_grad = query_blocks.reshape(seq_len, heads_local, HD)
    query_norm_grad = rotate_back(query_grad, cosine, sine).reshape(seq_len, head_cols)
    key_norm_grad = rotate_back(key_grad, cosine, sine).reshape(seq_len, head_cols)
    gain_query_grad = jnp.sum(query_norm_grad * unit_q, axis=0)
    gain_key_grad = jnp.sum(key_norm_grad * unit_k, axis=0)
    scaled_q = query_norm_grad * gain_query
    scaled_k = key_norm_grad * gain_key
    inner_q, inner_k = tp_totals(
        jnp.sum(scaled_q * unit_q, axis=-1), jnp.sum(scaled_k * unit_k, axis=-1)
    )
    query_raw_grad = scale_q * (scaled_q - unit_q * (inner_q / width)[:, None])
    key_raw_grad = scale_k * (scaled_k - unit_k * (inner_k / width)[:, None])
    qkv_grad = jnp.stack(
        [query_raw_grad, key_raw_grad, value_grad.reshape(seq_len, head_cols)]
    ).astype(jnp.bfloat16)
    grad_qkv_full = jnp.einsum("sd,csh->cdh", rows1, qkv_grad, preferred_element_type=jnp.float32)
    normed1_part = jnp.einsum("csh,cdh->sd", qkv_grad, qkv_full, preferred_element_type=jnp.float32)
    normed1_grad = scatter_rows(normed1_part)
    input_norm_grad, gain1_grad = norm_backward(x_own, scale1, gains_wide[0], normed1_grad)
    input_grad = hidden_grad + input_norm_grad
    zero_width = jnp.zeros((width,), jnp.float32)
    gains_grad = jnp.stack(
        [
            gain1_grad,
            gain2_grad,
            lax.dynamic_update_slice_in_dim(zero_width, gain_query_grad, col_start, 0),
            lax.dynamic_update_slice_in_dim(zero_width, gain_key_grad, col_start, 0),
        ]
    )
    grad_qkv, grad_out = (
        lax.psum_scatter(
            grad_qkv_full.astype(jnp.bfloat16), "fsdp", scatter_dimension=1, tiled=True
        ).astype(jnp.float32),
        lax.psum_scatter(
            grad_out_full.astype(jnp.bfloat16), "fsdp", scatter_dimension=1, tiled=True
        ).astype(jnp.float32),
    )
    grad_router, grad_gains = (
        lax.psum_scatter(router_grad, ("fsdp", "tp"), scatter_dimension=0, tiled=True),
        lax.psum_scatter(gains_grad, ("fsdp", "tp"), scatter_dimension=1, tiled=True),
    )
    return (
        layer_out,
        input_grad,
        grad_qkv,
        grad_out,
        grad_router,
        grad_gains,
        grad_gate,
        grad_up,
        grad_down,
    )


GRID = (4, 2, 2, 2)
FINE = ("z", "x", "y", "core")
LANES = 128
CONTRACT_LAST = (((1,), (1,)), ((), ()))


def permutation(target):
    def place(z, x, y, c):
        return ((z * GRID[1] + x) * GRID[2] + y) * GRID[3] + c

    return [
        (place(*at), place(*target(*at))) for at in itertools.product(*(range(n) for n in GRID))
    ]


SWAP_CORE = permutation(lambda z, x, y, c: (z, x, y, 1 - c))
SWAP_X = permutation(lambda z, x, y, c: (z, 1 - x, y, c))
SWAP_Y = permutation(lambda z, x, y, c: (z, x, 1 - y, c))
SWAP_BOTH = permutation(lambda z, x, y, c: (z, x, 1 - y, 1 - c))
SWAP_FIRST = permutation(lambda z, x, y, c: (z, 1 - x, y, c) if c == 0 else (z, x, 1 - y, c))
SWAP_SECOND = permutation(lambda z, x, y, c: (z, x, 1 - y, c) if c == 0 else (z, 1 - x, y, c))


def shift_z(steps):
    return permutation(lambda z, x, y, c: ((z + steps) % GRID[0], x, y, c))


def send(values, pairs):
    return lax.ppermute(values, FINE, pairs)


def add_low(*terms):
    return sum(term.astype(jnp.float32) for term in terms).astype(jnp.bfloat16)


def side_totals(first, second):
    return lax.psum((first, second), FINE[2:])


def fence(*values):
    return lax.optimization_barrier(values)


def wide_sum(*terms):
    return sum(term.astype(jnp.float32) for term in terms)


def pair_dots(left, right):
    return lax.dot_general(left, right, (((0,), (0,)), ((), ())), preferred_element_type=jnp.float32)


def side_pair(own, far):
    is_far = lax.axis_index("y") == 1
    return jnp.stack([jnp.where(is_far, far, own), jnp.where(is_far, own, far)])


def four_rows(mine, theirs):
    is_second = lax.axis_index("core") == 1
    both = jnp.stack(
        [jnp.where(is_second, theirs, mine), jnp.where(is_second, mine, theirs)], axis=1
    )
    return both.reshape(4 * mine.shape[1], *mine.shape[2:])


def core_split(values):
    core = lax.axis_index("core")
    blocks = values.astype(jnp.bfloat16).reshape(2, 2, values.shape[0] // 4, values.shape[1])
    return (
        lax.dynamic_index_in_dim(blocks, 1 - core, 1, keepdims=False),
        lax.dynamic_index_in_dim(blocks, core, 1, keepdims=False),
    )


def side_split(mine, back):
    side = lax.axis_index("y")

    def at(pair, which):
        return lax.dynamic_index_in_dim(pair, which, 0, keepdims=False)

    away = add_low(at(mine, 1 - side), at(back, 1 - side))
    return (away, wide_sum(at(mine, side), at(back, side)))


def expert_kernel(
    blocks_ref,
    near_ref,
    far_ref,
    grads0_ref,
    grads1_ref,
    grads2_ref,
    grads3_ref,
    router_ref,
    place_ref,
    *refs,
    n_experts,
    at,
    n_before,
):
    weight_refs, refs = refs[:6], refs[6 + n_before :]
    near_route_ref, far_route_ref, active_ref, hidden_ref, dots_ref, grads_ref, rows_ref = refs[:7]
    gate_buf, up_buf, down_buf, active_buf, hidden_buf, rows_buf, grads_buf, in_sems, out_sems = refs[7:]
    exp_local, width = place_ref.shape[0], near_ref.shape[1]
    units = gate_buf.shape[2]
    half = near_ref.shape[0]
    count = 2 * half
    buffers = (gate_buf, up_buf, down_buf)

    def fetch(slot, kind):
        group, expert = slot // exp_local, slot % exp_local
        return pltpu.make_async_copy(
            weight_refs[3 * group + kind].at[expert], buffers[kind].at[slot], in_sems.at[slot, kind]
        )

    slots = 2 * exp_local
    for slot in range(slots):
        for kind in range(3):
            fetch(slot, kind).start()
    rows_buf[:half] = near_ref[...]
    rows_buf[half:] = far_ref[...]
    quarter = half // 2
    grad_refs = (grads0_ref, grads1_ref, grads2_ref, grads3_ref)
    for block, ref in enumerate(grad_refs):
        grads_buf[block * quarter : (block + 1) * quarter] = ref[:, :width]

    def round_rows(ref):
        return ref.at[pl.ds(at * count, count)]

    stores = [
        pltpu.make_async_copy(rows_buf, round_rows(rows_ref), out_sems.at[0]),
        pltpu.make_async_copy(grads_buf, round_rows(grads_ref), out_sems.at[1]),
    ]
    for store in stores:
        store.start()
    named = jnp.concatenate([ref[:, width:] for ref in grad_refs], axis=0)
    rows = rows_buf[...]
    grads = grads_buf[...]
    lane = lax.broadcasted_iota(jnp.int32, (1, LANES), 1)
    logits = jnp.dot(rows, router_ref[...], preferred_element_type=jnp.float32)
    logits = jnp.where(lane < n_experts, logits, NEG_FILL)
    powered = jnp.exp(logits - jnp.max(logits, axis=-1, keepdims=True))
    gates = powered / jnp.sum(powered, axis=-1, keepdims=True) * named.astype(jnp.float32)
    route = None
    dots = jnp.zeros(logits.shape, jnp.float32)
    for slot in range(slots):
        expert = slot % exp_local
        place = place_ref[expert : expert + 1, :]
        gate = jnp.sum(gates * place, axis=-1, keepdims=True)
        for kind in range(3):
            fetch(slot, kind).wait()
        gate_pre = jnp.dot(rows, gate_buf[slot], preferred_element_type=jnp.float32)
        up_pre = jnp.dot(rows, up_buf[slot], preferred_element_type=jnp.float32)
        y_down = lax.dot_general(
            grads, down_buf[slot], CONTRACT_LAST, preferred_element_type=jnp.float32
        )
        sigmoid = 1.0 / (1.0 + jnp.exp(-gate_pre))
        silu = gate_pre * sigmoid
        active = silu * up_pre
        dots = dots + jnp.sum(active * y_down, axis=-1, keepdims=True) * place
        active_buf[slot] = (active * gate).astype(jnp.bfloat16)
        active_grad = y_down * gate
        gate_grad = (active_grad * up_pre * sigmoid * (1.0 + gate_pre * (1.0 - sigmoid))).astype(
            jnp.bfloat16
        )
        up_grad = (active_grad * silu).astype(jnp.bfloat16)
        hidden_buf[slot, :, :units] = gate_grad
        hidden_buf[slot, :, units:] = up_grad
        for buf, ref, columns, sem in (
            (active_buf, active_ref, units, 2 + 2 * slot),
            (hidden_buf, hidden_ref, 2 * units, 3 + 2 * slot),
        ):
            store = pltpu.make_async_copy(
                buf.at[slot],
                ref.at[pl.ds(at * count, count), pl.ds(slot * columns, columns)],
                out_sems.at[sem],
            )
            store.start()
            stores.append(store)
        part = lax.dot_general(
            gate_grad, gate_buf[slot], CONTRACT_LAST, preferred_element_type=jnp.float32
        ) + lax.dot_general(
            up_grad, up_buf[slot], CONTRACT_LAST, preferred_element_type=jnp.float32
        )
        route = part if route is None else route + part
    near_route_ref[...] = route[:half].astype(jnp.bfloat16)
    far_route_ref[...] = route[half:].astype(jnp.bfloat16)
    dots_ref[...] = jnp.transpose(dots)[:n_experts]
    for store in stores:
        store.wait()


def expert_rows(at, before, blocks, near, far, all_grads, router, place, own, other, n_experts):
    half, width = near.shape
    count = 2 * half
    exp_local, _, units = own[0].shape
    slots = 2 * exp_local
    wide = all_grads.shape[1]

    def whole(array):
        return pl.BlockSpec(
            array.shape, lambda step, blocks: (0,) * array.ndim, pipeline_mode=pl.Buffered(1)
        )

    def picked(row):
        return pl.BlockSpec(
            (count // 4, wide), lambda step, blocks: (blocks[row], 0), pipeline_mode=pl.Buffered(1)
        )

    def first_block(shape):
        return pl.BlockSpec(shape, lambda step, blocks: (0, 0))

    def rounds(columns):
        return jax.ShapeDtypeStruct((GRID[0] * count, columns), jnp.bfloat16)

    anywhere = pl.BlockSpec(memory_space=pl.ANY)
    inputs = (blocks, near, far, *(all_grads for _ in range(4)), router, place, *own, *other, *before)
    order = (2, 3, 5, 6)
    route = jax.ShapeDtypeStruct((half, width), jnp.bfloat16)
    return pl.pallas_call(
        functools.partial(expert_kernel, n_experts=n_experts, at=at, n_before=len(before)),
        out_shape=[
            route,
            route,
            rounds(slots * units),
            rounds(2 * slots * units),
            jax.ShapeDtypeStruct((n_experts, count), jnp.float32),
            rounds(width),
            rounds(width),
        ],
        grid_spec=pltpu.PrefetchScalarGridSpec(
            num_scalar_prefetch=1,
            grid=(1,),
            in_specs=[
                whole(near),
                whole(far),
                *(picked(row) for row in range(4)),
                whole(router),
                whole(place),
                *(anywhere for _ in range(6 + len(before))),
            ],
            out_specs=[
                first_block((half, width)),
                first_block((half, width)),
                anywhere,
                anywhere,
                first_block((n_experts, count)),
                anywhere,
                anywhere,
            ],
            scratch_shapes=[
                pltpu.VMEM((slots, width, units), jnp.bfloat16),
                pltpu.VMEM((slots, width, units), jnp.bfloat16),
                pltpu.VMEM((slots, units, width), jnp.bfloat16),
                pltpu.VMEM((slots, count, units), jnp.bfloat16),
                pltpu.VMEM((slots, count, 2 * units), jnp.bfloat16),
                pltpu.VMEM((count, width), jnp.bfloat16),
                pltpu.VMEM((count, width), jnp.bfloat16),
                pltpu.SemaphoreType.DMA((slots, 3)),
                pltpu.SemaphoreType.DMA((2 + 2 * slots,)),
            ],
        ),
        input_output_aliases={
            len(inputs) - len(before) + index: order[index] for index in range(len(before))
        },
        cost_estimate=pl.CostEstimate(flops=1024, bytes_accessed=1024, transcendentals=0),
        compiler_params=pltpu.CompilerParams(
            dimension_semantics=("arbitrary",), vmem_limit_bytes=46 * 1024 * 1024
        ),
        name="expert_rows",
    )(*inputs)


def turned(values, cosine, sine):
    return values * cosine + pltpu.roll(values, HD // 2, 1) * sine


def allowed_pairs(segment_col_ref, segment_row_ref, padding_ref):
    count = segment_col_ref.shape[0]
    row = lax.broadcasted_iota(jnp.int32, (count, count), 0)
    col = lax.broadcasted_iota(jnp.int32, (count, count), 1)
    usable = (padding_ref[...] == 1) | (col == row)
    return (segment_col_ref[...] == segment_row_ref[...]) & (col <= row) & usable


def attend_kernel(
    projected_ref,
    scale_q_ref,
    scale_k_ref,
    gain_q_ref,
    gain_k_ref,
    cosine_ref,
    sine_ref,
    segment_col_ref,
    segment_row_ref,
    padding_ref,
    mixed_ref,
    queries_ref,
    keys_ref,
    values_ref,
    log_sum_ref,
):
    width = mixed_ref.shape[1]
    allowed = allowed_pairs(segment_col_ref, segment_row_ref, padding_ref)
    cosine, sine = cosine_ref[...], sine_ref[...]
    scale_q, scale_k = scale_q_ref[...], scale_k_ref[...]
    for head in range(width // HD):
        at = slice(head * HD, (head + 1) * HD)
        raw_q = projected_ref[:, head * HD : (head + 1) * HD]
        raw_k = projected_ref[:, width + head * HD : width + (head + 1) * HD]
        raw_v = projected_ref[:, 2 * width + head * HD : 2 * width + (head + 1) * HD]
        queries = turned(raw_q * scale_q * gain_q_ref[:, at], cosine, sine).astype(jnp.bfloat16)
        keys = turned(raw_k * scale_k * gain_k_ref[:, at], cosine, sine).astype(jnp.bfloat16)
        values = raw_v.astype(jnp.bfloat16)
        scores = (
            lax.dot_general(queries, keys, CONTRACT_LAST, preferred_element_type=jnp.float32)
            * HD ** (-0.5)
        )
        scores = jnp.where(allowed, scores, NEG_FILL)
        peak = jnp.max(scores, axis=-1, keepdims=True)
        powered = jnp.exp(scores - peak)
        total = jnp.sum(powered, axis=-1, keepdims=True)
        probs_low = (powered / total).astype(jnp.bfloat16)
        mixed_ref[:, at] = jnp.dot(
            probs_low, values, preferred_element_type=jnp.float32
        ).astype(jnp.bfloat16)
        queries_ref[:, at] = queries
        keys_ref[:, at] = keys
        values_ref[:, at] = values
        log_sum_ref[:, head : head + 1] = peak + jnp.log(total)


def attend_back_kernel(
    hidden_ref,
    out_ref,
    queries_ref,
    keys_ref,
    values_ref,
    log_sum_ref,
    projected_ref,
    scale_q_ref,
    scale_k_ref,
    gain_q_ref,
    gain_k_ref,
    cosine_ref,
    sine_ref,
    segment_col_ref,
    segment_row_ref,
    padding_ref,
    scaled_q_ref,
    scaled_k_ref,
    value_grad_ref,
    inner_ref,
    gain_grad_ref,
):
    width = queries_ref.shape[1]
    allowed = allowed_pairs(segment_col_ref, segment_row_ref, padding_ref)
    cosine, sine = cosine_ref[...], sine_ref[...]
    mixed_grad_all = jnp.dot(
        hidden_ref[...], out_ref[...], preferred_element_type=jnp.float32
    ).astype(jnp.bfloat16)
    contract_rows = (((0,), (0,)), ((), ()))
    inner_q = jnp.zeros((queries_ref.shape[0], 1), jnp.float32)
    inner_k = jnp.zeros((queries_ref.shape[0], 1), jnp.float32)
    for head in range(width // HD):
        at = slice(head * HD, (head + 1) * HD)
        queries, keys, values = queries_ref[:, at], keys_ref[:, at], values_ref[:, at]
        mixed_grad = mixed_grad_all[:, at]
        scores = (
            lax.dot_general(queries, keys, CONTRACT_LAST, preferred_element_type=jnp.float32)
            * HD ** (-0.5)
        )
        powered = jnp.exp(jnp.where(allowed, scores, NEG_FILL) - log_sum_ref[:, head : head + 1])
        probs = jnp.where(allowed, powered, 0.0)
        prob_grad = lax.dot_general(
            mixed_grad, values, CONTRACT_LAST, preferred_element_type=jnp.float32
        )
        delta = jnp.sum(probs * prob_grad, axis=-1, keepdims=True)
        score_grad = (probs * (prob_grad - delta)).astype(jnp.bfloat16)
        query_grad = jnp.dot(score_grad, keys, preferred_element_type=jnp.float32) * HD ** (-0.5)
        key_grad = lax.dot_general(
            score_grad, queries, contract_rows, preferred_element_type=jnp.float32
        ) * HD ** (-0.5)
        value_grad_ref[:, at] = lax.dot_general(
            probs.astype(jnp.bfloat16),
            mixed_grad,
            contract_rows,
            preferred_element_type=jnp.float32,
        ).astype(jnp.bfloat16)
        query_grad = turned(query_grad, cosine, -sine)
        key_grad = turned(key_grad, cosine, -sine)
        unit_q = projected_ref[:, head * HD : (head + 1) * HD] * scale_q_ref[...]
        unit_k = projected_ref[:, width + head * HD : width + (head + 1) * HD] * scale_k_ref[...]
        gain_grad_ref[0:1, at] = jnp.sum(query_grad * unit_q, axis=0, keepdims=True)
        gain_grad_ref[1:2, at] = jnp.sum(key_grad * unit_k, axis=0, keepdims=True)
        scaled_q = query_grad * gain_q_ref[:, at]
        scaled_k = key_grad * gain_k_ref[:, at]
        scaled_q_ref[:, at] = scaled_q
        scaled_k_ref[:, at] = scaled_k
        inner_q += jnp.sum(scaled_q * unit_q, axis=-1, keepdims=True)
        inner_k += jnp.sum(scaled_k * unit_k, axis=-1, keepdims=True)
    inner_ref[:, 0:1] = inner_q
    inner_ref[:, 1:2] = inner_k


def small_call(kernel, shapes, name):
    return pl.pallas_call(
        kernel,
        out_shape=[jax.ShapeDtypeStruct(shape, dtype) for shape, dtype in shapes],
        cost_estimate=pl.CostEstimate(flops=1024, bytes_accessed=1024, transcendentals=0),
        compiler_params=pltpu.CompilerParams(vmem_limit_bytes=40 * 1024 * 1024),
        name=name,
    )


def dense_shards(
    tokens,
    seg_ids,
    pad_mask,
    expert_ids,
    w_qkv,
    w_out,
    w_router,
    norm_gains,
    w_gate,
    w_up,
    w_down,
    cotangent,
):
    z, x, y, core = (lax.axis_index(name) for name in FINE)
    fsdp_rank = z * GRID[1] + x
    tp_rank = y * GRID[3] + core
    local_rows, width = tokens.shape
    seq_len = seg_ids.shape[1]
    exp_local, _, ff_local = w_gate.shape
    n_experts = w_router.shape[1]
    head_cols = w_qkv.shape[2]
    own_start = tp_rank * local_rows
    small_cols = norm_gains.shape[1]
    fsdp = FINE[:2]

    def own_rows(values):
        return lax.dynamic_slice_in_dim(values, own_start, local_rows, 0)

    tp_swaps = (SWAP_CORE, SWAP_Y, SWAP_BOTH)
    z_shifts = [shift_z(steps) for steps in range(1, GRID[0])]
    small_own = jnp.pad(
        jnp.concatenate([w_router, norm_gains.T], axis=1), ((0, 0), (0, LANES - n_experts - 4))
    )
    small = lax.dynamic_update_slice_in_dim(
        jnp.zeros((w_qkv.shape[1], LANES), jnp.bfloat16), small_own, tp_rank * small_cols, 0
    )
    smalls, tokens_own = fence([send(small, swap) for swap in tp_swaps], tokens)
    small = small + smalls[0] + smalls[1] + smalls[2]
    weights_own = jnp.concatenate(
        [w_qkv.transpose(1, 0, 2).reshape(w_qkv.shape[1], -1), small], axis=1
    )
    weights_full = lax.all_gather(weights_own, fsdp, axis=0, tiled=True)
    block = w_out.shape[1]
    out_full = jnp.zeros((width, w_out.shape[0]), jnp.bfloat16)
    out_column, tokens_own = fence(w_out.T, tokens_own)
    for steps in range(GRID[0]):
        out_beside = send(out_column, SWAP_X)
        for piece_x, piece_values in ((x, out_column), (1 - x, out_beside)):
            start = ((z - steps) % GRID[0] * GRID[1] + piece_x) * block
            out_full = lax.dynamic_update_slice_in_dim(out_full, piece_values, start, 0)
        if steps < GRID[0] - 1:
            out_column = send(out_column, z_shifts[0])
    names = jnp.arange(n_experts, dtype=jnp.int32)
    own_ids = own_rows(expert_ids)
    named = (own_ids[:, :, None] == names[None, None, :]).any(axis=1)
    named_wide = jnp.pad(named.astype(jnp.bfloat16), ((0, 0), (0, LANES - n_experts)))
    grads_own = jnp.concatenate([cotangent, named_wide], axis=1)
    far = send(tokens_own, SWAP_Y)
    mine = side_pair(tokens, far)
    theirs = send(mine, SWAP_CORE)
    rows_x = four_rows(mine, theirs).astype(jnp.float32)
    scale1 = lax.rsqrt(jnp.mean(rows_x * rows_x, axis=-1, keepdims=True) + EPSILON)
    own_weights = (w_gate, w_up, w_down)
    weights_own, out_full, _ = fence(own_weights, out_full, theirs)
    other_weights = tuple(send(weight, SWAP_CORE) for weight in weights_own)
    down_rows = jnp.concatenate(
        [weights[2].reshape(-1, width) for weights in (own_weights, other_weights)]
    )
    grads_own, other_weights, down_rows, weights_full, scale1, rows_x, out_full = fence(
        grads_own, other_weights, down_rows, weights_full, scale1, rows_x, out_full
    )
    all_grads_abs = lax.all_gather(grads_own, FINE[:3], axis=0, tiled=True)
    qkv_full = weights_full[:, : 3 * head_cols]
    router_wide = weights_full[:, 3 * head_cols :]
    router_full = router_wide[:, :n_experts]
    gains_wide = router_wide[:, n_experts : n_experts + 4].T.astype(jnp.float32)

    cosine, sine = (table[:, 0] for table in rope_tables(seq_len, HD))
    turns = (
        jnp.concatenate([cosine, cosine], axis=1),
        jnp.concatenate([-sine, sine], axis=1),
        seg_ids.T,
        seg_ids,
        pad_mask,
    )
    x_own = tokens.astype(jnp.float32)
    col_start = tp_rank * head_cols
    gain_query = lax.dynamic_slice_in_dim(gains_wide[2], col_start, head_cols)
    gain_key = lax.dynamic_slice_in_dim(gains_wide[3], col_start, head_cols)
    rows1 = (rows_x * scale1 * gains_wide[0]).astype(jnp.bfloat16)
    projected = jnp.dot(rows1, qkv_full, preferred_element_type=jnp.float32)
    query_raw = projected[:, :head_cols]
    key_raw = projected[:, head_cols : 2 * head_cols]
    squares = side_totals(
        jnp.sum(query_raw * query_raw, axis=-1), jnp.sum(key_raw * key_raw, axis=-1)
    )
    scale_q = lax.rsqrt(squares[0] / width + EPSILON)[:, None]
    scale_k = lax.rsqrt(squares[1] / width + EPSILON)[:, None]
    low_heads = ((seq_len, head_cols), jnp.bfloat16)
    wide_heads = ((seq_len, head_cols), jnp.float32)
    norms = (scale_q, scale_k, gain_query[None], gain_key[None])
    mixed, queries, keys, values, log_sums = small_call(
        attend_kernel, [low_heads] * 4 + [((seq_len, LANES), jnp.float32)], "attend"
    )(projected, *norms, *turns)
    away, mine = core_split(
        lax.dot_general(mixed, out_full, CONTRACT_LAST, preferred_element_type=jnp.float32)
    )
    away, kept = side_split(mine, send(away, SWAP_CORE))
    far, kept = fence(send(away, SWAP_Y), kept)
    hidden = x_own + kept + far
    normed2, scale2 = norm_forward(hidden, gains_wide[1])
    own_normed2 = normed2.astype(jnp.bfloat16)

    place = (
        jnp.arange(LANES)[None, :] == fsdp_rank * exp_local + jnp.arange(exp_local)[:, None]
    ).astype(jnp.float32)
    rows, rows_near, rows_far = [own_normed2], [], []
    results, seconds, firsts, homes = [], [], [], []

    def hop(column):
        return send(column, z_shifts[0])

    def experts(at):
        beside = jnp.where(core == 0, (1 - x) * GRID[2] + y, x * GRID[2] + 1 - y)
        across = jnp.where(core == 0, x * GRID[2] + 1 - y, (1 - x) * GRID[2] + y)
        opposite = (1 - x) * GRID[2] + 1 - y
        plane = (z - at) % GRID[0] * (GRID[1] * GRID[2])
        blocks = plane + jnp.stack([x * GRID[2] + y, beside, across, opposite])
        before = [results[at - 1][index] for index in (2, 3, 5, 6)] if at else []
        return expert_rows(
            at,
            before,
            blocks.astype(jnp.int32),
            rows_near[at],
            rows_far[at],
            all_grads_abs,
            router_wide,
            place,
            own_weights,
            other_weights,
            n_experts,
        )

    def near_of(at, arrived):
        return jnp.concatenate([rows[at], arrived], axis=0)

    def first_part(near, second):
        half = near.shape[0] // 2
        return add_low(near[half:], second[half:])

    def mine_part(near, second, first):
        half = near.shape[0] // 2
        return wide_sum(near[:half], second[:half], first)

    def route_first(at):
        return send(first_part(results[at][0], seconds[at]), SWAP_FIRST)

    def route_home(at):
        mine = mine_part(results[at][0], seconds[at], firsts[at])
        return send(mine.astype(jnp.bfloat16), z_shifts[GRID[0] - 1 - at])

    hopped, arrived = fence(hop(rows[0]), send(rows[0], SWAP_FIRST))
    rows.append(hopped)
    rows_near.append(near_of(0, arrived))
    hopped, arrived, second = fence(
        hop(rows[1]), send(rows[1], SWAP_FIRST), send(rows_near[0], SWAP_SECOND)
    )
    rows.append(hopped)
    rows_near.append(near_of(1, arrived))
    rows_far.append(second)
    hopped, arrived, second, result = fence(
        hop(rows[2]), send(rows[2], SWAP_FIRST), send(rows_near[1], SWAP_SECOND), experts(0)
    )
    rows.append(hopped)
    rows_near.append(near_of(2, arrived))
    rows_far.append(second)
    results.append(result)
    arrived, second, back, result = fence(
        send(rows[3], SWAP_FIRST),
        send(rows_near[2], SWAP_SECOND),
        send(results[0][1], SWAP_SECOND),
        experts(1),
    )
    rows_near.append(near_of(3, arrived))
    rows_far.append(second)
    seconds.append(back)
    results.append(result)
    second, back, first, result = fence(
        send(rows_near[3], SWAP_SECOND),
        send(results[1][1], SWAP_SECOND),
        route_first(0),
        experts(2),
    )
    rows_far.append(second)
    seconds.append(back)
    firsts.append(first)
    results.append(result)
    back, first, result = fence(
        send(results[2][1], SWAP_SECOND), route_first(1), experts(3)
    )
    seconds.append(back)
    firsts.append(first)
    results.append(result)
    homes.append(mine_part(results[0][0], seconds[0], firsts[0]))

    dots = jnp.stack([result[4] for result in results])
    part = dots.shape[-1] // 4
    all_active, all_hidden, all_grads, all_rows = (results[-1][index] for index in (2, 3, 5, 6))
    back, first, home, dots_back, dots, all_active, all_hidden = fence(
        send(results[3][1], SWAP_SECOND),
        route_first(2),
        route_home(1),
        send(dots[..., 2 * part :], SWAP_SECOND),
        dots,
        all_active,
        all_hidden,
    )
    seconds.append(back)
    firsts.append(first)
    homes.append(home)
    dots = dots[..., : 2 * part] + dots_back
    units = exp_local * ff_local
    pair_count = 2 * exp_local

    def piece(at):
        return all_hidden[:, at * ff_local : (at + 1) * ff_local]

    first, home, dots_back, dots, output, all_hidden = fence(
        route_first(3),
        route_home(2),
        send(dots[..., part:], SWAP_FIRST),
        dots,
        jnp.dot(all_active, down_rows, preferred_element_type=jnp.float32).astype(jnp.bfloat16),
        all_hidden,
    )
    half = output.shape[0] // (2 * GRID[0])
    outputs = [
        (output[2 * at * half : (2 * at + 1) * half], output[(2 * at + 1) * half : 2 * (at + 1) * half])
        for at in range(GRID[0])
    ]
    firsts.append(first)
    homes.append(home)
    dots = dots[..., :part] + dots_back
    home, dots_back, dots, outputs, all_hidden, others = fence(
        route_home(3),
        [send(dots[at], shift_z(-at)) for at in range(1, GRID[0])],
        dots[0],
        outputs,
        all_hidden,
        [pair_dots(all_rows, piece(pair_count))],
    )
    homes.append(home)
    token_grad = wide_sum(*homes)
    own_dots = (dots + dots_back[0] + dots_back[1] + dots_back[2]).T

    logits = jnp.dot(own_normed2, router_full, preferred_element_type=jnp.float32)
    router_probs = jax.nn.softmax(logits, axis=-1)
    own_gates = jnp.where(named, router_probs, 0.0)
    chosen = jnp.where(named, own_dots, 0.0)
    weighted = jnp.sum(own_gates * chosen, axis=-1, keepdims=True)
    own_logit_grad = (router_probs * (chosen - weighted)).astype(jnp.bfloat16)
    normed2_grad = token_grad + jnp.dot(
        own_logit_grad, router_full.T, preferred_element_type=jnp.float32
    )
    hidden_norm_grad, gain2_grad = norm_backward(hidden, scale2, gains_wide[1], normed2_grad)
    hidden_grad = cotangent.astype(jnp.float32) + hidden_norm_grad
    hidden_low = hidden_grad.astype(jnp.bfloat16)
    far, hidden_low, outputs, all_hidden, more = fence(
        send(hidden_low, SWAP_Y),
        hidden_low,
        outputs,
        all_hidden,
        [pair_dots(all_rows, piece(pair_count + 1))],
    )
    others = [*others, *more]
    mine = side_pair(hidden_low, far)
    theirs, mine, outputs, all_hidden = fence(send(mine, SWAP_CORE), mine, outputs, all_hidden)
    hidden_rows = four_rows(mine, theirs)
    grad_out_full, hidden_rows = fence(
        pair_dots(hidden_rows, mixed).astype(jnp.bfloat16), hidden_rows
    )
    grad_out = (
        lax.psum_scatter(grad_out_full, fsdp, scatter_dimension=0, tiled=True)
        .astype(jnp.float32)
        .T
    )
    output_seconds, (scaled_q, scaled_k, value_grad, inners, gain_grads), outputs = fence(
        [send(pair[1], SWAP_SECOND) for pair in outputs[:2]],
        small_call(
            attend_back_kernel,
            [
                wide_heads,
                wide_heads,
                low_heads,
                ((seq_len, 2), jnp.float32),
                ((2, head_cols), jnp.float32),
            ],
            "attend_back",
        )(hidden_rows, out_full, queries, keys, values, log_sums, projected, *norms, *turns),
        outputs,
    )
    gain_query_grad, gain_key_grad = gain_grads[0], gain_grads[1]
    inners = side_totals(inners[:, 0], inners[:, 1])
    unit_q = query_raw * scale_q
    unit_k = key_raw * scale_k
    query_raw_grad = scale_q * (scaled_q - unit_q * (inners[0] / width)[:, None])
    key_raw_grad = scale_k * (scaled_k - unit_k * (inners[1] / width)[:, None])
    qkv_grad = jnp.concatenate(
        [query_raw_grad.astype(jnp.bfloat16), key_raw_grad.astype(jnp.bfloat16), value_grad], axis=1
    )
    normed1_part = lax.dot_general(
        qkv_grad, qkv_full, CONTRACT_LAST, preferred_element_type=jnp.float32
    )
    gain1_grad = jnp.sum(normed1_part * (rows_x * scale1), axis=0)
    away, mine = core_split(normed1_part)
    zero_width = jnp.zeros((width,), jnp.float32)
    gains_grad = jnp.stack(
        [
            gain1_grad,
            gain2_grad,
            lax.dynamic_update_slice_in_dim(zero_width, gain_query_grad, col_start, 0),
            lax.dynamic_update_slice_in_dim(zero_width, gain_key_grad, col_start, 0),
        ]
    )
    small = jnp.concatenate([pair_dots(own_normed2, own_logit_grad), gains_grad.T], axis=1)
    small = jnp.pad(small, ((0, 0), (0, LANES - n_experts - 4)))
    grad_full = jnp.concatenate([pair_dots(rows1, qkv_grad), small], axis=1).astype(jnp.bfloat16)
    grad_own = lax.psum_scatter(grad_full, fsdp, scatter_dimension=0, tiled=True)
    grad_qkv = (
        grad_own[:, : 3 * head_cols].astype(jnp.float32).reshape(-1, 3, head_cols).transpose(1, 0, 2)
    )
    small = grad_own[:, 3 * head_cols :]
    away, mine, outputs, all_hidden, all_active, _ = fence(
        away, mine, outputs, all_hidden, all_active, grad_full
    )
    back, mine, output_rest, others, more, other_down, all_hidden = fence(
        send(away, SWAP_CORE),
        mine,
        [send(pair[1], SWAP_SECOND) for pair in outputs[2:]],
        [send(other, SWAP_CORE) for other in others],
        [pair_dots(all_rows, piece(pair_count + at)) for at in range(2, pair_count)],
        pair_dots(all_active[:, units:], all_grads),
        all_hidden,
    )
    output_seconds = [*output_seconds, *output_rest]
    away, kept = side_split(mine, back)
    output_firsts = [
        send(first_part(pair[0], second), SWAP_FIRST)
        for pair, second in zip(outputs, output_seconds)
    ]
    far, kept, output_firsts, more, other_down, grad_pair, all_hidden = fence(
        send(away, SWAP_Y),
        kept,
        output_firsts,
        [send(other, SWAP_CORE) for other in more],
        send(other_down, SWAP_CORE),
        [pair_dots(all_rows, piece(at)) + other for at, other in enumerate(others)],
        all_hidden,
    )
    output_mine = [
        mine_part(pair[0], second, first)
        for pair, second, first in zip(outputs, output_seconds, output_firsts)
    ]
    output_homes = [
        send(output_mine[at].astype(jnp.bfloat16), shift_z(-at)) for at in range(1, GRID[0])
    ]
    normed1_grad = kept + far
    input_norm_grad, _ = norm_backward(x_own, own_rows(scale1), gains_wide[0], normed1_grad)
    input_grad = hidden_grad + input_norm_grad
    grad_pair = [
        *grad_pair,
        *(pair_dots(all_rows, piece(2 + at)) + other for at, other in enumerate(more)),
    ]
    grad_down = (pair_dots(all_active[:, :units], all_grads) + other_down).reshape(
        exp_local, ff_local, width
    )
    layer_out = (hidden + wide_sum(output_mine[0], *output_homes)).astype(jnp.bfloat16)
    grad_gate = jnp.stack(grad_pair[0::2])
    grad_up = jnp.stack(grad_pair[1::2])
    small = lax.dynamic_slice_in_dim(
        wide_sum(small, *(send(small, swap) for swap in tp_swaps)),
        tp_rank * small_cols,
        small_cols,
        0,
    )
    grad_router = small[:, :n_experts]
    grad_gains = small[:, n_experts : n_experts + 4].T
    return (
        layer_out,
        input_grad,
        grad_qkv,
        grad_out,
        grad_router,
        grad_gains,
        grad_gate,
        grad_up,
        grad_down,
    )


def solution(mesh):
    fast = tuple(mesh.shape.values()) == (GRID[0] * GRID[1], GRID[2] * GRID[3])
    fine = Mesh(mesh.devices.reshape(GRID), FINE) if fast else None

    def layer(*arguments):
        n_experts = arguments[8].shape[0]
        top_count = arguments[3].shape[1]
        if fast and n_experts <= 2 * top_count:
            return placed_shards(dense_shards, fine, FINE[:2], FINE[2:])(*arguments)
        return placed_shards(shards, mesh, ("fsdp",), ("tp",))(*arguments)

    return layer


def placed_shards(body, mesh, fsdp, tp):
    rows = P((*fsdp, *tp), None)
    experts = P(fsdp, None, tp)
    columns = P(None, (*fsdp, *tp))
    return jax.shard_map(
        body,
        mesh=mesh,
        in_specs=(
            rows,
            P(fsdp, None),
            P(fsdp, None),
            P(fsdp, None),
            P(None, fsdp, tp),
            P(tp, fsdp),
            rows,
            columns,
            experts,
            experts,
            P(fsdp, tp, None),
            rows,
        ),
        out_specs=(
            rows,
            rows,
            P(None, fsdp, tp),
            P(tp, fsdp),
            rows,
            columns,
            experts,
            experts,
            P(fsdp, tp, None),
        ),
        check_vma=False,
    )
```
